128 devices in a mesh: wide: 32 (over z, y_lo, x), narrow: 4 (over y_hi, core).
Axes of the slice: x: 4, y: 4 (y_hi: 2, y_lo: 2; y = y_hi * 2 + y_lo), z: 4, core: 2. Of those that a mesh axis runs over, the one named last changes fastest.
Arguments:
- hidden: bfloat16 [512, 4, 8192], P('narrow', None, 'wide'), may hold values from -0.1796875 to 0.1796875
- grad_out: bfloat16 [512, 8192], P('narrow', 'wide'), may hold values from -6 to 6
- weight_base: bfloat16 [32768, 8192], P('narrow', 'wide'), may hold values from -0.0625 to 0.0625
- block_scale: bfloat16 [2048, 512], P('narrow', 'wide'), may hold values from 0.25 to 4
Outputs:
- grad_hidden: bfloat16 [512, 4, 8192], P('narrow', None, 'wide')
- grad_weight: bfloat16 [8192, 4, 8192], P('narrow', None, 'wide')
The draws below stay inside these ranges and needn't reach their ends.
All inputs are finite; a program needn't handle non-finite values.
Results may differ from the reference program's by a relative error of at most 0.0049.
Values may be sent and summed in bfloat16 or wider, within the bound.
No kernel may reach another device: no remote copies, remote signals or barrier semaphores. Data moves between devices by JAX's collectives and lax.ppermute only.
A program may use at most 192 MiB of HBM per device.

```python
import math
import jax
import jax.numpy as jnp

D = 8192
FF = 32768
BLOCK = 16
TOKENS = 512
GROUPS = 4
FGROUP = 8192


def shard_levels(rng, extent, pieces, least, largest):
    def one(dim, shards_of):
        heights = jax.random.uniform(jax.random.fold_in(jax.random.fold_in(rng, 6), dim), (shards_of,), jnp.float32, least / len(pieces), largest / len(pieces))
        return jnp.repeat(jnp.exp(heights), extent[dim] // shards_of).reshape((-1,) + (1,) * (len(extent) - dim - 1))

    loudness = one(*pieces[0])
    for cut in pieces[1:]:
        loudness = loudness * one(*cut)
    return loudness


def noise(own_key, extent, deviation, reach, cuts=(), dtype=jnp.bfloat16):
    loudness = shard_levels(own_key, extent, cuts, -0.22, 0.18) if cuts else 1.0
    entries = jax.random.normal(own_key, extent, jnp.float32) * deviation * loudness
    return jnp.minimum(jnp.maximum(entries, -reach), reach).astype(dtype)


def setup_inputs(seed: int = 0) -> dict:
    streams_of = jax.random.split(jax.random.key(seed), 5)
    return {
        "hidden": noise(streams_of[0], (TOKENS, GROUPS, FGROUP), 0.03, 0.1796875, ((0, 4), (2, 32))),
        "grad_out": noise(streams_of[1], (TOKENS, D), 1.0, 6.0, ((0, 4), (1, 32))),
        "weight_base": noise(streams_of[2], (FF, D), D ** -0.5, 0.0625, ((0, 4), (1, 32))),
        "block_scale": jnp.clip(jnp.exp(math.log(4.0) - 2.7725887 * jax.random.uniform(streams_of[3], (FF // BLOCK, D // BLOCK), jnp.float32) ** shard_levels(streams_of[3], (FF // BLOCK, D // BLOCK), ((0, 4), (1, 32)), -0.2, 0.2)), 0.25, 4.0).astype(jnp.bfloat16),
    }


def apply_scales(values, scales):
    height, breadth = values.shape
    widened = jnp.repeat(scales, 16, axis=1).astype(jnp.float32)
    blocked = values.reshape(height // 16, 16, breadth).astype(jnp.float32)
    blocked = blocked * widened[:, None, :]
    return blocked.reshape(height, breadth).astype(jnp.bfloat16)


def reference(hidden, grad_out, weight_base, block_scale):
    effective = apply_scales(weight_base, block_scale)
    flat_hidden = hidden.reshape(hidden.shape[0], hidden.shape[1] * hidden.shape[2])
    grad_flat = jnp.dot(grad_out, effective.T, preferred_element_type=jnp.float32)
    grad_hidden = grad_flat.astype(jnp.bfloat16).reshape(hidden.shape)
    grad_weight = jnp.dot(grad_out.T, flat_hidden, preferred_element_type=jnp.float32)
    grad_weight = grad_weight.astype(jnp.bfloat16).reshape(grad_out.shape[1], hidden.shape[1], hidden.shape[2])
    return grad_hidden, grad_weight
```

```python
import functools

import jax
import jax.numpy as jnp
from jax import lax
from jax.experimental import pallas as pl
from jax.experimental.pallas import tpu as pltpu
from jax.sharding import Mesh, PartitionSpec as P

BF = jnp.bfloat16
F32 = jnp.float32
VM = pltpu.VMEM


def first_axis_steps(k):
    pairs = []
    for z in range(4):
        for x in range(4):
            pairs.append(((z * 4 + x) * 2, (z * 4 + (x + k) % 4) * 2))
            pairs.append(((z * 4 + x) * 2 + 1, (((z + k) % 4) * 4 + x) * 2 + 1))
    return pairs


def second_axis_steps(k):
    pairs = []
    for z in range(4):
        for x in range(4):
            pairs.append(((z * 4 + x) * 2, (((z + k) % 4) * 4 + x) * 2))
            pairs.append(((z * 4 + x) * 2 + 1, (z * 4 + (x + k) % 4) * 2 + 1))
    return pairs


def shift(value, pairs):
    return lax.ppermute(value, ("z", "x", "c"), pairs)


def swap(value, axis):
    return lax.ppermute(value, axis, [(0, 1), (1, 0)])


def place(k, i, m):
    p = (m[1] + k) & 3
    c = m[0]
    return c * p + (1 - c) * i, c * i + (1 - c) * p


def scale_body(k, m, w_ref, s_ref, o_ref, wide_ref):
    i = pl.program_id(0)

    @pl.when(i == 0)
    def _():
        row = lax.broadcasted_iota(jnp.int32, (16, 256), 0)
        col = lax.broadcasted_iota(jnp.int32, (16, 256), 1)
        spread = jnp.where(col // 16 == row, 1.0, 0.0).astype(BF)
        wide_ref[...] = lax.dot_general(
            s_ref[...], spread, (((0,), (0,)), ((), ())), preferred_element_type=F32
        )

    z, x = place(k, i, m)
    for yl in range(2):
        r = pl.multiple_of((z * 8 + yl * 4 + x) * 16, 16)
        s = wide_ref[pl.ds(r, 16), :]
        w = w_ref[0, yl, 0].astype(F32).reshape(16, 16, 256)
        o_ref[pl.ds(yl * 256, 256), :] = (w * s[:, None, :]).reshape(256, 256).astype(BF)


def scaled_rows(k, meta, w5, scales_t):
    def w_map(i, m):
        z, x = place(k, i, m)
        return z, 0, x, 0, 0

    return pl.pallas_call(
        functools.partial(scale_body, k),
        out_shape=jax.ShapeDtypeStruct((2048, 256), BF),
        grid_spec=pltpu.PrefetchScalarGridSpec(
            num_scalar_prefetch=1,
            grid=(4,),
            in_specs=[
                pl.BlockSpec((1, 2, 1, 256, 256), w_map),
                pl.BlockSpec((16, 512), lambda i, m: (0, 0)),
            ],
            out_specs=pl.BlockSpec((512, 256), lambda i, m: (i, 0)),
            scratch_shapes=[VM((512, 256), F32)],
        ),
        name=f"scale{k}",
    )(meta, w5, scales_t)


def partial_body(m, *refs):
    g, w, o_ref = refs[:4], refs[4:8], refs[8]
    total = None
    for a, b in zip(g, w):
        part = lax.dot_general(
            a[...], b[...], (((1,), (1,)), ((), ())), preferred_element_type=F32
        )
        total = part if total is None else total + part
    o_ref[...] = total.astype(o_ref.dtype)


def partial_sums(k, meta, grads, weights, dtype):
    return pl.pallas_call(
        partial_body,
        out_shape=jax.ShapeDtypeStruct((512, 512), dtype),
        grid_spec=pltpu.PrefetchScalarGridSpec(
            num_scalar_prefetch=1,
            grid=(1,),
            in_specs=[pl.BlockSpec((512, 256), lambda i, m: (0, 0))] * 4
            + [pl.BlockSpec((512, 256), lambda i, m: ((m[2] + k) & 3, 0))] * 4,
            out_specs=pl.BlockSpec((512, 512), lambda i, m: (0, 0)),
        ),
        name=f"partial{k}",
    )(meta, *grads, *weights)


def gather_body(a, b, c, d, o_ref):
    total = a[...] + b[...].astype(F32) + c[...].astype(F32) + d[...].astype(F32)
    total = total.astype(BF)
    for yl in range(2):
        for n in range(4):
            o_ref[yl * 4 + n] = total[n * 128 : (n + 1) * 128, yl * 256 : (yl + 1) * 256]


def summed_blocks(parts):
    return pl.pallas_call(
        gather_body,
        out_shape=jax.ShapeDtypeStruct((8, 128, 256), BF),
        name="summed",
    )(*parts)


def finish_body(r_ref, o_ref):
    for n in range(4):
        o_ref[:, n, :] = (r_ref[n].astype(F32) + r_ref[4 + n].astype(F32)).astype(BF)


def finished(blocks):
    return pl.pallas_call(
        finish_body,
        out_shape=jax.ShapeDtypeStruct((128, 4, 256), BF),
        name="finish",
    )(blocks)


def outer_body(m, *refs):
    mine, theirs, h_ref, o_ref = refs[:4], refs[4], refs[5], refs[6]
    i = pl.program_id(0)

    def block(g):
        r = lax.dot_general(
            g, h_ref[...], (((0,), (0,)), ((), ())), preferred_element_type=F32
        ).astype(BF)
        for n in range(4):
            o_ref[:, n, :] = r[:, n * 256 : (n + 1) * 256]

    for k in range(4):

        @pl.when(i == k)
        def _():
            block(mine[k][...])

    @pl.when(i >= 4)
    def _():
        block(theirs[i - 4])


def outer_product(meta, mine, theirs, hidden):
    def o_map(i, m):
        yl = jnp.where(i < 4, m[3], 1 - m[3])
        return yl * 4 + ((m[4] - i) & 3), 0, 0

    full = pl.BlockSpec((512, 256), lambda i, m: (0, 0))
    return pl.pallas_call(
        outer_body,
        out_shape=jax.ShapeDtypeStruct((2048, 4, 256), BF),
        grid_spec=pltpu.PrefetchScalarGridSpec(
            num_scalar_prefetch=1,
            grid=(8,),
            in_specs=[full] * 4
            + [
                pl.BlockSpec((4, 512, 256), lambda i, m: (0, 0, 0)),
                pl.BlockSpec((512, 1024), lambda i, m: (0, 0)),
            ],
            out_specs=pl.BlockSpec((256, 4, 256), o_map),
        ),
        name="outer",
    )(meta, *mine, theirs, hidden)


def joined(a, b, first):
    return jnp.where(first, jnp.concatenate([a, b], 0), jnp.concatenate([b, a], 0))


def per_device(hidden, grad_out, weight_base, block_scale):
    z, yl, x = lax.axis_index("z"), lax.axis_index("yl"), lax.axis_index("x")
    yh, c = lax.axis_index("yh"), lax.axis_index("c")
    pos = jnp.where(c == 0, x, z)
    other = jnp.where(c == 0, z, x)
    meta = jnp.stack([c, pos, other, yl, x]).astype(jnp.int32)

    g2 = joined(grad_out, swap(grad_out, "c"), c == 0)
    g4 = joined(g2, swap(g2, "yh"), yh == 0)

    w5 = weight_base.reshape(4, 2, 4, 256, 256)
    scales_t = block_scale.T
    rows = [None] * 4
    for k in (2, 1, 3):
        rows[k] = shift(scaled_rows(k, meta, w5, scales_t), first_axis_steps(k))
    rows[0] = scaled_rows(0, meta, w5, scales_t)
    grads = [g4] + [shift(g4, first_axis_steps(k)) for k in (1, 2, 3)]

    parts = [None] * 4
    for k in (2, 1, 3):
        parts[k] = shift(partial_sums(k, meta, grads, rows, BF), second_axis_steps(k))
    parts[0] = partial_sums(0, meta, grads, rows, F32)
    blocks = summed_blocks(parts)
    blocks = lax.all_to_all(blocks, ("yl", "yh", "c"), 0, 0, tiled=True)
    grad_hidden = finished(blocks)

    h = hidden.reshape(128, 1024)
    h2 = joined(h, swap(h, "c"), c == 0)
    h4 = joined(h2, swap(h2, "yh"), yh == 0)
    stacked = jnp.stack(grads)
    want = jnp.where(c == 0, yh * 2, yh * 2 + 1)
    give = lax.dynamic_index_in_dim(stacked, (z - yh * 2) & 3, 0, keepdims=False)
    keep = lax.dynamic_index_in_dim(stacked, (z - want) & 3, 0, keepdims=False)
    got = lax.ppermute(give, "c", [(1, 0)])
    seed = jnp.where(c == 0, got, keep)
    ring = lambda k: [(i, (i + k) % 4) for i in range(4)]
    mine = [seed] + [lax.ppermute(seed, "x", ring(k)) for k in (1, 2, 3)]
    theirs = swap(jnp.stack(mine), "yl")
    grad_weight = outer_product(meta, mine, theirs, h4)
    return grad_hidden, grad_weight


def solution(mesh):
    fine = Mesh(mesh.devices.reshape(4, 2, 4, 2, 2), ("z", "yl", "x", "yh", "c"))
    narrow, wide = ("yh", "c"), ("z", "yl", "x")
    return jax.shard_map(
        per_device,
        mesh=fine,
        in_specs=(
            P(narrow, None, wide),
            P(narrow, wide),
            P(narrow, wide),
            P(narrow, wide),
        ),
        out_specs=(P(narrow, None, wide), P(narrow, None, wide)),
        check_vma=False,
    )
```

```python
import functools

import jax
import jax.numpy as jnp
from jax import lax
from jax.experimental import pallas as pl
from jax.experimental.pallas import tpu as pltpu
from jax.sharding import Mesh, PartitionSpec as P

BF = jnp.bfloat16
F32 = jnp.float32
VM = pltpu.VMEM


def first_axis_steps(k):
    pairs = []
    for z in range(4):
        for x in range(4):
            pairs.append(((z * 4 + x) * 2, (z * 4 + (x + k) % 4) * 2))
            pairs.append(((z * 4 + x) * 2 + 1, (((z + k) % 4) * 4 + x) * 2 + 1))
    return pairs


def second_axis_steps(k):
    pairs = []
    for z in range(4):
        for x in range(4):
            pairs.append(((z * 4 + x) * 2, (((z + k) % 4) * 4 + x) * 2))
            pairs.append(((z * 4 + x) * 2 + 1, (z * 4 + (x + k) % 4) * 2 + 1))
    return pairs


def shift(value, pairs):
    return lax.ppermute(value, ("z", "x", "c"), pairs)


def swap(value, axis):
    return lax.ppermute(value, axis, [(0, 1), (1, 0)])


LIMIT = pltpu.CompilerParams(vmem_limit_bytes=12 << 20)
IN = pl.BlockSpec(memory_space=VM)
HBM = pl.BlockSpec(memory_space=pltpu.HBM)


def kept(*values):
    return [pltpu.with_memory_space_constraint(v, VM) for v in values]


def roles():
    c, x, z = lax.axis_index("c"), lax.axis_index("x"), lax.axis_index("z")
    return c, jnp.where(c == 0, x, z), jnp.where(c == 0, z, x)


ORDER = (2, 1, 3, 0)


def scale_body(w_ref, s_ref, *refs):
    outs, wide_ref, sems = refs[:4], refs[4], refs[5]
    c, first, _ = roles()
    copies = []
    for k in ORDER:
        p = (first + k) & 3
        for i in range(4):
            z, x = c * p + (1 - c) * i, c * i + (1 - c) * p
            copy = pltpu.make_async_copy(w_ref.at[z, :, x], outs[k].at[i], sems.at[k * 4 + i])
            copy.start()
            copies.append((copy, outs[k].at[i], z, x))
    row = lax.broadcasted_iota(jnp.int32, (16, 256), 0)
    col = lax.broadcasted_iota(jnp.int32, (16, 256), 1)
    spread = jnp.where(col // 16 == row, 1.0, 0.0).astype(BF)
    wide_ref[...] = lax.dot_general(
        s_ref[...], spread, (((0,), (0,)), ((), ())), preferred_element_type=F32
    )
    for copy, o_ref, z, x in copies:
        copy.wait()
        for yl in range(2):
            r = pl.multiple_of((z * 8 + yl * 4 + x) * 16, 16)
            s = wide_ref[pl.ds(r, 16), :]
            w = o_ref[yl].astype(F32).reshape(16, 16, 256)
            o_ref[yl] = (w * s[:, None, :]).reshape(256, 256).astype(BF)


def scaled_rows(w5, scales_t):
    outs = pl.pallas_call(
        scale_body,
        out_shape=[VM((4, 2, 256, 256), BF)] * 4,
        in_specs=[HBM, IN],
        out_specs=[IN] * 4,
        scratch_shapes=[VM((512, 256), F32), pltpu.SemaphoreType.DMA((16,))],
        compiler_params=LIMIT,
        name="scale",
    )(w5, scales_t)
    return [o.reshape(2048, 256) for o in outs]


def partial_body(*refs):
    g, w, outs = refs[:4], refs[4:8], refs[8:12]
    _, _, second = roles()
    for k in ORDER:
        r = pl.multiple_of(((second + k) & 3) * 512, 512)
        total = None
        for a, b in zip(g, w):
            part = lax.dot_general(
                a[...], b[pl.ds(r, 512), :], (((1,), (1,)), ((), ())), preferred_element_type=F32
            )
            total = part if total is None else total + part
        outs[k][...] = total.astype(outs[k].dtype)


def partial_sums(grads, weights):
    return pl.pallas_call(
        partial_body,
        out_shape=[VM((512, 512), F32)] + [VM((512, 512), BF)] * 3,
        in_specs=[IN] * 8,
        out_specs=[IN] * 4,
        compiler_params=LIMIT,
        name="partial",
    )(*kept(*grads, *weights))


def gather_body(a, b, c, d, o_ref):
    total = a[...] + b[...].astype(F32) + c[...].astype(F32) + d[...].astype(F32)
    total = total.astype(BF)
    for yl in range(2):
        for n in range(4):
            t = ((n & 1) * 2 + (n >> 1)) * 128
            o_ref[yl * 4 + n] = total[t : t + 128, yl * 256 : (yl + 1) * 256]


def summed_blocks(parts):
    return pl.pallas_call(
        gather_body,
        out_shape=VM((8, 128, 256), BF),
        in_specs=[IN] * 4,
        out_specs=IN,
        compiler_params=LIMIT,
        name="summed",
    )(*kept(*parts))


def finish_body(r_ref, o_ref):
    r = [(r_ref[n].astype(F32) + r_ref[4 + n].astype(F32)).astype(BF) for n in range(4)]
    o_ref[...] = jnp.concatenate(r, axis=1).reshape(128, 4, 256)


def finished(blocks):
    return pl.pallas_call(
        finish_body,
        out_shape=jax.ShapeDtypeStruct((128, 4, 256), BF),
        in_specs=[IN],
        out_specs=IN,
        compiler_params=LIMIT,
        name="finish",
    )(*kept(blocks))


def outer_body(*refs):
    g, h_ref, o_ref, buf, sems = refs[:8], refs[8], refs[9], refs[10], refs[11]
    yl, x = lax.axis_index("yl"), lax.axis_index("x")
    copies = []
    for i in range(8):
        here = yl if i < 4 else 1 - yl
        r = pl.multiple_of((here * 4 + ((x - i) & 3)) * 256, 256)
        p = lax.dot_general(
            g[i][...], h_ref[...], (((0,), (0,)), ((), ())), preferred_element_type=F32
        )
        buf[i] = p.astype(BF).reshape(256, 4, 256)
        copy = pltpu.make_async_copy(buf.at[i], o_ref.at[pl.ds(r, 256)], sems.at[i])
        copy.start()
        copies.append(copy)
    for copy in copies:
        copy.wait()


def outer_product(blocks, hidden):
    return pl.pallas_call(
        outer_body,
        out_shape=jax.ShapeDtypeStruct((2048, 4, 256), BF),
        in_specs=[IN] * 9,
        out_specs=HBM,
        scratch_shapes=[VM((8, 256, 4, 256), BF), pltpu.SemaphoreType.DMA((8,))],
        compiler_params=LIMIT,
        name="outer",
    )(*kept(*blocks, hidden))


def joined(a, b, first):
    return jnp.where(first, jnp.concatenate([a, b], 0), jnp.concatenate([b, a], 0))


def per_device(hidden, grad_out, weight_base, block_scale):
    z, x = lax.axis_index("z"), lax.axis_index("x")
    yh, c = lax.axis_index("yh"), lax.axis_index("c")

    w5 = weight_base.reshape(4, 2, 4, 256, 256)
    sent = scaled_rows(w5, block_scale.T)
    rows = [sent[0]] + [None] * 3
    for k in (2, 1, 3):
        rows[k] = shift(sent[k], first_axis_steps(k))

    g2 = joined(grad_out, swap(grad_out, "yh"), yh == 0)
    g4 = joined(g2, swap(g2, "c"), c == 0)
    grads = [g4] + [shift(g4, first_axis_steps(k)) for k in (1, 2, 3)]

    sums = partial_sums(grads, rows)
    parts = [sums[0]] + [None] * 3
    for k in (2, 1, 3):
        parts[k] = shift(sums[k], second_axis_steps(k))
    blocks = summed_blocks(parts)
    blocks = lax.all_to_all(blocks, ("yl", "yh", "c"), 0, 0, tiled=True)
    grad_hidden = finished(blocks)

    h = hidden.reshape(128, 1024)
    h2 = joined(h, swap(h, "yh"), yh == 0)
    h4 = joined(h2, swap(h2, "c"), c == 0)

    def of_plane(p):
        k = (z - p) & 3
        return jnp.where(k < 2, jnp.where(k == 0, grads[0], grads[1]), jnp.where(k == 2, grads[2], grads[3]))

    got = lax.ppermute(of_plane(yh * 2), "c", [(1, 0)])
    seed = jnp.where(c == 0, got, of_plane(yh * 2 + 1))
    ring = lambda k: [(i, (i + k) % 4) for i in range(4)]
    mine = [seed] + [lax.ppermute(seed, "x", ring(k)) for k in (1, 2, 3)]
    theirs = [swap(m, "yl") for m in mine]
    grad_weight = outer_product(mine + theirs, h4)
    return grad_hidden, grad_weight


def solution(mesh):
    fine = Mesh(mesh.devices.reshape(4, 2, 4, 2, 2), ("z", "yl", "x", "yh", "c"))
    narrow, wide = ("yh", "c"), ("z", "yl", "x")
    return jax.shard_map(
        per_device,
        mesh=fine,
        in_specs=(
            P(narrow, None, wide),
            P(narrow, wide),
            P(narrow, wide),
            P(narrow, wide),
        ),
        out_specs=(P(narrow, None, wide), P(narrow, None, wide)),
        check_vma=False,
    )
```

```python
import functools

import jax
import jax.numpy as jnp
from jax import lax
from jax.experimental import pallas as pl
from jax.experimental.pallas import tpu as pltpu
from jax.sharding import Mesh, PartitionSpec as P

BF = jnp.bfloat16
F32 = jnp.float32
VM = pltpu.VMEM


def first_axis_steps(k):
    pairs = []
    for z in range(4):
        for x in range(4):
            pairs.append(((z * 4 + x) * 2, (z * 4 + (x + k) % 4) * 2))
            pairs.append(((z * 4 + x) * 2 + 1, (((z + k) % 4) * 4 + x) * 2 + 1))
    return pairs


def second_axis_steps(k):
    pairs = []
    for z in range(4):
        for x in range(4):
            pairs.append(((z * 4 + x) * 2, (((z + k) % 4) * 4 + x) * 2))
            pairs.append(((z * 4 + x) * 2 + 1, (z * 4 + (x + k) % 4) * 2 + 1))
    return pairs


def shift(value, pairs):
    return lax.ppermute(value, ("z", "x", "c"), pairs)


def swap(value, axis):
    return lax.ppermute(value, axis, [(0, 1), (1, 0)])


LIMIT = pltpu.CompilerParams(vmem_limit_bytes=12 << 20)
EARLY = int(2e9)
NEAR = int(20e9)
IN = pl.BlockSpec(memory_space=VM)
HBM = pl.BlockSpec(memory_space=pltpu.HBM)


def kept(*values):
    return [pltpu.with_memory_space_constraint(v, VM) for v in values]


def roles():
    c, x, z = lax.axis_index("c"), lax.axis_index("x"), lax.axis_index("z")
    return c, jnp.where(c == 0, x, z), jnp.where(c == 0, z, x)


def spread_scales(s_ref, wide_ref):
    row = lax.broadcasted_iota(jnp.int32, (16, 256), 0)
    col = lax.broadcasted_iota(jnp.int32, (16, 256), 1)
    spread = jnp.where(col // 16 == row, 1.0, 0.0).astype(BF)
    wide_ref[...] = lax.dot_general(
        s_ref[...], spread, (((0,), (0,)), ((), ())), preferred_element_type=F32
    )


def scale_into(outs, w_ref, s_ref, wide_ref, sems, between=None):
    c, first, _ = roles()
    copies = []
    for j, (k, o_ref) in enumerate(outs):
        p = (first + k) & 3
        for i in range(4):
            z, x = c * p + (1 - c) * i, c * i + (1 - c) * p
            copy = pltpu.make_async_copy(
                w_ref.at[z, :, x], o_ref.at[pl.ds(2 * i, 2)], sems.at[j * 4 + i]
            )
            copy.start()
            copies.append((copy, o_ref, i, z, x))
    spread_scales(s_ref, wide_ref)
    if between is not None:
        between()
    for copy, o_ref, i, z, x in copies:
        copy.wait()
        for yl in range(2):
            r = pl.multiple_of((z * 8 + yl * 4 + x) * 16, 16)
            s = wide_ref[pl.ds(r, 16), :]
            w = o_ref[2 * i + yl].astype(F32).reshape(16, 16, 256)
            o_ref[2 * i + yl] = (w * s[:, None, :]).reshape(256, 256).astype(BF)


def far_body(w_ref, s_ref, o_ref, wide_ref, sems):
    scale_into([(2, o_ref)], w_ref, s_ref, wide_ref, sems)


def far_rows(w5, scales_t):
    return pl.pallas_call(
        far_body,
        out_shape=VM((8, 256, 256), BF),
        in_specs=[HBM, IN],
        out_specs=IN,
        scratch_shapes=[VM((512, 256), F32), pltpu.SemaphoreType.DMA((4,))],
        compiler_params=LIMIT,
        name="far",
    )(w5, scales_t)


def near_body(w_ref, s_ref, g0, g1, g2, g3, o1, o3, o0, og, wide_ref, sems):
    n = lax.axis_index("yh") * 2 + lax.axis_index("c")

    def tokens():
        for r, g in enumerate((g0, g1, g2, g3)):
            t = n ^ r
            og[t >> 1, pl.ds(pl.multiple_of((t & 1) * 128, 128), 128), :] = g[...]
        o1[8:10] = og[...]
        o3[8:10] = og[...]

    scale_into([(1, o1), (3, o3), (0, o0)], w_ref, s_ref, wide_ref, sems, tokens)


def near_rows(w5, scales_t, pieces):
    return pl.pallas_call(
        near_body,
        out_shape=[VM((10, 256, 256), BF)] * 2 + [VM((8, 256, 256), BF), VM((2, 256, 256), BF)],
        in_specs=[HBM] + [IN] * 5,
        out_specs=[IN] * 4,
        scratch_shapes=[VM((512, 256), F32), pltpu.SemaphoreType.DMA((12,))],
        compiler_params=LIMIT,
        cost_estimate=pl.CostEstimate(flops=NEAR, bytes_accessed=8 << 20, transcendentals=0),
        name="near",
    )(w5, scales_t, *pieces)


def block_product(g, w, q):
    return lax.dot_general(
        g[...].reshape(512, 256),
        w[pl.ds(q, 2)].reshape(512, 256),
        (((1,), (1,)), ((), ())),
        preferred_element_type=F32,
    )


def early_body(r0, r2, g0, g2, acc):
    for q in range(4):
        acc[q] = block_product(g0, r0, 2 * q) + block_product(g2, r2, 2 * q)


def early_sums(*operands):
    return pl.pallas_call(
        early_body,
        out_shape=VM((4, 512, 512), F32),
        in_specs=[IN] * 4,
        out_specs=IN,
        compiler_params=LIMIT,
        cost_estimate=pl.CostEstimate(flops=EARLY, bytes_accessed=6 << 20, transcendentals=0),
        name="early",
    )(*kept(*operands))


def partial_body(acc, r1, r3, g0, g2, *outs):
    keep, give = outs[4:]
    _, _, second = roles()
    z, yh = lax.axis_index("z"), lax.axis_index("yh")
    g = (g0, r1.at[8:10], g2, r3.at[8:10])
    for k in range(4):

        @pl.when(((z - 2 * yh) & 3) == k)
        def _():
            give[...] = g[k][...]

        @pl.when(((z - 2 * yh - 1) & 3) == k)
        def _():
            keep[...] = g[k][...]

    for k in (2, 1, 3, 0):
        q = (second + k) & 3
        total = acc[q] + block_product(g[1], r1, 2 * q) + block_product(g[3], r3, 2 * q)
        outs[k][...] = total.astype(outs[k].dtype)


def partial_sums(*operands):
    return pl.pallas_call(
        partial_body,
        out_shape=[VM((512, 512), F32)]
        + [VM((512, 512), BF)] * 3
        + [VM((2, 256, 256), BF)] * 2,
        in_specs=[IN] * 5,
        out_specs=[IN] * 6,
        compiler_params=LIMIT,
        name="partial",
    )(*kept(*operands))


def gather_body(a, b, c, d, o_ref):
    total = a[...] + b[...].astype(F32) + c[...].astype(F32) + d[...].astype(F32)
    total = total.astype(BF)
    for yl in range(2):
        for n in range(4):
            t = n * 128
            o_ref[yl * 4 + n] = total[t : t + 128, yl * 256 : (yl + 1) * 256]


def summed_blocks(parts):
    return pl.pallas_call(
        gather_body,
        out_shape=VM((8, 128, 256), BF),
        in_specs=[IN] * 4,
        out_specs=IN,
        compiler_params=LIMIT,
        name="summed",
    )(parts[0], *kept(*parts[1:]))


def finish_body(r_ref, o_ref):
    r = [(r_ref[n].astype(F32) + r_ref[4 + n].astype(F32)).astype(BF) for n in range(4)]
    o_ref[...] = jnp.concatenate(r, axis=1).reshape(128, 4, 256)


def finished(blocks):
    return pl.pallas_call(
        finish_body,
        out_shape=jax.ShapeDtypeStruct((128, 4, 256), BF),
        in_specs=[IN],
        out_specs=IN,
        compiler_params=LIMIT,
        name="finish",
    )(*kept(blocks))


def picked_body(a_ref, b_ref, o_ref):
    @pl.when(lax.axis_index("c") == 0)
    def _():
        o_ref[...] = a_ref[...]

    @pl.when(lax.axis_index("c") == 1)
    def _():
        o_ref[...] = b_ref[...]


def picked(for_core_0, for_core_1):
    return pl.pallas_call(
        picked_body,
        out_shape=VM((2, 256, 256), BF),
        in_specs=[IN] * 2,
        out_specs=IN,
        compiler_params=LIMIT,
        name="picked",
    )(for_core_0, for_core_1)


def outer_body(*refs):
    g, pieces, o_ref, h_ref, buf, sems = refs[:8], refs[8:12], *refs[12:]
    yl, x = lax.axis_index("yl"), lax.axis_index("x")
    n = lax.axis_index("yh") * 2 + lax.axis_index("c")
    for r, piece in enumerate(pieces):
        h_ref[pl.ds(pl.multiple_of((n ^ r) * 128, 128), 128), :] = piece[...]
    copies = []
    for i in range(8):
        here = yl if i < 4 else 1 - yl
        r = pl.multiple_of((here * 4 + ((x - i) & 3)) * 256, 256)
        p = lax.dot_general(
            g[i][...].reshape(512, 256),
            h_ref[...],
            (((0,), (0,)), ((), ())),
            preferred_element_type=F32,
        )
        buf[i] = p.astype(BF).reshape(256, 4, 256)
        copy = pltpu.make_async_copy(buf.at[i], o_ref.at[pl.ds(r, 256)], sems.at[i])
        copy.start()
        copies.append(copy)
    for copy in copies:
        copy.wait()


def outer_product(blocks, pieces):
    return pl.pallas_call(
        outer_body,
        out_shape=jax.ShapeDtypeStruct((2048, 4, 256), BF),
        in_specs=[IN] * 12,
        out_specs=HBM,
        scratch_shapes=[
            VM((512, 1024), BF),
            VM((8, 256, 4, 256), BF),
            pltpu.SemaphoreType.DMA((8,)),
        ],
        compiler_params=LIMIT,
        name="outer",
    )(*kept(*blocks, *pieces))


def token_pieces(own):
    far = swap(own, "yh")
    return [own, swap(own, "c"), far, swap(far, "c")]


def per_device(hidden, grad_out, weight_base, block_scale):
    w5 = pltpu.with_memory_space_constraint(weight_base.reshape(4, 2, 4, 256, 256), pltpu.HBM)
    scales_t = block_scale.T

    tokens = token_pieces(grad_out)
    sent2 = far_rows(w5, scales_t)
    r2 = shift(sent2, first_axis_steps(2))
    tokens, _ = lax.optimization_barrier((tokens, sent2))
    sent1, sent3, r0, g0 = near_rows(w5, scales_t, tokens)
    r1 = shift(sent1, first_axis_steps(1))
    r3 = shift(sent3, first_axis_steps(3))
    g2 = shift(g0, first_axis_steps(2))

    acc = early_sums(r0, r2, g0, g2)
    h, acc = lax.optimization_barrier((hidden, acc))
    pieces = token_pieces(h.reshape(128, 1024))
    acc, pieces = lax.optimization_barrier((acc, pieces))
    *sums, keep, give = partial_sums(acc, r1, r3, g0, g2)
    parts = [sums[0]] + [None] * 3
    for k in (2, 1, 3):
        parts[k] = shift(sums[k], second_axis_steps(k))
    blocks = summed_blocks(parts)
    blocks = lax.all_to_all(blocks, ("yl", "yh", "c"), 0, 0, tiled=True)
    grad_hidden = finished(blocks)

    seed = picked(lax.ppermute(give, "c", [(1, 0)]), keep)
    ring = lambda k: [(i, (i + k) % 4) for i in range(4)]
    mine = [seed] + [lax.ppermute(seed, "x", ring(k)) for k in (1, 2, 3)]
    theirs = [swap(m, "yl") for m in mine]
    grad_weight = outer_product(mine + theirs, pieces)
    return grad_hidden, grad_weight


def solution(mesh):
    fine = Mesh(mesh.devices.reshape(4, 2, 4, 2, 2), ("z", "yl", "x", "yh", "c"))
    narrow, wide = ("yh", "c"), ("z", "yl", "x")
    return jax.shard_map(
        per_device,
        mesh=fine,
        in_specs=(
            P(narrow, None, wide),
            P(narrow, wide),
            P(narrow, wide),
            P(narrow, wide),
        ),
        out_specs=(P(narrow, None, wide), P(narrow, None, wide)),
        check_vma=False,
    )
```

```python
import functools

import jax
import jax.numpy as jnp
from jax import lax
from jax.experimental import pallas as pl
from jax.experimental.pallas import tpu as pltpu
from jax.sharding import Mesh, PartitionSpec as P

BF = jnp.bfloat16
F32 = jnp.float32
VM = pltpu.VMEM


def first_axis_steps(k):
    pairs = []
    for z in range(4):
        for x in range(4):
            pairs.append(((z * 4 + x) * 2, (z * 4 + (x + k) % 4) * 2))
            pairs.append(((z * 4 + x) * 2 + 1, (((z + k) % 4) * 4 + x) * 2 + 1))
    return pairs


def second_axis_steps(k):
    pairs = []
    for z in range(4):
        for x in range(4):
            pairs.append(((z * 4 + x) * 2, (((z + k) % 4) * 4 + x) * 2))
            pairs.append(((z * 4 + x) * 2 + 1, (z * 4 + (x + k) % 4) * 2 + 1))
    return pairs


def shift(value, pairs):
    return lax.ppermute(value, ("z", "x", "c"), pairs)


def swap(value, axis):
    return lax.ppermute(value, axis, [(0, 1), (1, 0)])


LIMIT = pltpu.CompilerParams(vmem_limit_bytes=12 << 20)
EARLY = int(2e9)
IN = pl.BlockSpec(memory_space=VM)
HBM = pl.BlockSpec(memory_space=pltpu.HBM)


def kept(*values):
    return [pltpu.with_memory_space_constraint(v, VM) for v in values]


def roles():
    c, x, z = lax.axis_index("c"), lax.axis_index("x"), lax.axis_index("z")
    return c, jnp.where(c == 0, x, z), jnp.where(c == 0, z, x)


def spread_scales(s_ref, wide_ref):
    row = lax.broadcasted_iota(jnp.int32, (16, 256), 0)
    col = lax.broadcasted_iota(jnp.int32, (16, 256), 1)
    spread = jnp.where(col // 16 == row, 1.0, 0.0).astype(BF)
    wide_ref[...] = lax.dot_general(
        s_ref[...], spread, (((0,), (0,)), ((), ())), preferred_element_type=F32
    )


def scale_into(outs, w_ref, s_ref, wide_ref, sems):
    c, first, _ = roles()
    copies = []
    for j, (k, o_ref) in enumerate(outs):
        p = (first + k) & 3
        for i in range(4):
            z, x = c * p + (1 - c) * i, c * i + (1 - c) * p
            copy = pltpu.make_async_copy(
                w_ref.at[z, :, x], o_ref.at[pl.ds(2 * i, 2)], sems.at[j * 4 + i]
            )
            copy.start()
            copies.append((copy, o_ref, i, z, x))
    spread_scales(s_ref, wide_ref)
    for copy, o_ref, i, z, x in copies:
        copy.wait()
        for yl in range(2):
            r = pl.multiple_of((z * 8 + yl * 4 + x) * 16, 16)
            s = wide_ref[pl.ds(r, 16), :]
            w = o_ref[2 * i + yl].astype(F32).reshape(16, 16, 256)
            o_ref[2 * i + yl] = (w * s[:, None, :]).reshape(256, 256).astype(BF)


def scale_body(w_ref, s_ref, *refs):
    outs, wide_ref, sems = refs[:4], refs[4], refs[5]
    scale_into([(k, outs[k]) for k in (2, 1, 3, 0)], w_ref, s_ref, wide_ref, sems)


def scaled_rows(w5, scales_t):
    return pl.pallas_call(
        scale_body,
        out_shape=[VM((8, 256, 256), BF)] * 4,
        in_specs=[HBM, IN],
        out_specs=[IN] * 4,
        scratch_shapes=[VM((512, 256), F32), pltpu.SemaphoreType.DMA((16,))],
        compiler_params=LIMIT,
        name="scale",
    )(w5, scales_t)


def packed_body(g_ref, h_ref, o_ref):
    o_ref[0] = g_ref[...]
    h = h_ref[...].reshape(128, 1024)
    for n in range(4):
        o_ref[1 + n] = h[:, n * 256 : (n + 1) * 256]


def packed(grad_out, hidden):
    return pl.pallas_call(
        packed_body,
        out_shape=VM((5, 128, 256), BF),
        in_specs=[IN] * 2,
        out_specs=IN,
        compiler_params=LIMIT,
        name="packed",
    )(grad_out, hidden)


def tokens_body(p0, p1, p2, p3, g_ref, h_ref):
    n = lax.axis_index("yh") * 2 + lax.axis_index("c")
    for r, p in enumerate((p0, p1, p2, p3)):
        t = n ^ r
        g_ref[t >> 1, pl.ds(pl.multiple_of((t & 1) * 128, 128), 128), :] = p[0]
        rows = pl.ds(pl.multiple_of(t * 128, 128), 128)
        for m in range(4):
            h_ref[rows, m * 256 : (m + 1) * 256] = p[1 + m]


def all_tokens(own):
    far = swap(own, "yh")
    pieces = [own, swap(own, "c"), far, swap(far, "c")]
    return pl.pallas_call(
        tokens_body,
        out_shape=[VM((2, 256, 256), BF), VM((512, 1024), BF)],
        in_specs=[IN] * 4,
        out_specs=[IN] * 2,
        compiler_params=LIMIT,
        name="tokens",
    )(*kept(*pieces))


def block_product(g, w, q):
    return lax.dot_general(
        g[...].reshape(512, 256),
        w[pl.ds(q, 2)].reshape(512, 256),
        (((1,), (1,)), ((), ())),
        preferred_element_type=F32,
    )


def early_body(r0, r2, g0, g2, acc):
    for q in range(4):
        acc[q] = block_product(g0, r0, 2 * q) + block_product(g2, r2, 2 * q)


def early_sums(*operands):
    return pl.pallas_call(
        early_body,
        out_shape=VM((4, 512, 512), F32),
        in_specs=[IN] * 4,
        out_specs=IN,
        compiler_params=LIMIT,
        cost_estimate=pl.CostEstimate(flops=EARLY, bytes_accessed=6 << 20, transcendentals=0),
        name="early",
    )(*kept(*operands))


def partial_body(acc, r1, r3, g0, g1, g2, g3, *outs):
    keep, give = outs[4:]
    _, _, second = roles()
    z, yh = lax.axis_index("z"), lax.axis_index("yh")
    g = (g0, g1, g2, g3)
    for k in range(4):

        @pl.when(((z - 2 * yh) & 3) == k)
        def _():
            give[...] = g[k][...]

        @pl.when(((z - 2 * yh - 1) & 3) == k)
        def _():
            keep[...] = g[k][...]

    for k in (2, 1, 3, 0):
        q = (second + k) & 3
        total = acc[q] + block_product(g[1], r1, 2 * q) + block_product(g[3], r3, 2 * q)
        outs[k][...] = total.astype(outs[k].dtype)


def partial_sums(*operands):
    return pl.pallas_call(
        partial_body,
        out_shape=[VM((512, 512), F32)]
        + [VM((512, 512), BF)] * 3
        + [VM((2, 256, 256), BF)] * 2,
        in_specs=[IN] * 7,
        out_specs=[IN] * 6,
        compiler_params=LIMIT,
        name="partial",
    )(*kept(*operands))


def gather_body(a, b, c, d, o_ref):
    total = a[...] + b[...].astype(F32) + c[...].astype(F32) + d[...].astype(F32)
    total = total.astype(BF)
    for yl in range(2):
        for n in range(4):
            t = n * 128
            o_ref[yl * 4 + n] = total[t : t + 128, yl * 256 : (yl + 1) * 256]


def summed_blocks(parts):
    return pl.pallas_call(
        gather_body,
        out_shape=VM((8, 128, 256), BF),
        in_specs=[IN] * 4,
        out_specs=IN,
        compiler_params=LIMIT,
        name="summed",
    )(parts[0], *kept(*parts[1:]))


def finish_body(r_ref, o_ref):
    r = [(r_ref[n].astype(F32) + r_ref[4 + n].astype(F32)).astype(BF) for n in range(4)]
    o_ref[...] = jnp.concatenate(r, axis=1).reshape(128, 4, 256)


def finished(blocks):
    return pl.pallas_call(
        finish_body,
        out_shape=jax.ShapeDtypeStruct((128, 4, 256), BF),
        in_specs=[IN],
        out_specs=IN,
        compiler_params=LIMIT,
        name="finish",
    )(*kept(blocks))


def picked_body(a_ref, b_ref, o_ref):
    @pl.when(lax.axis_index("c") == 0)
    def _():
        o_ref[...] = a_ref[...]

    @pl.when(lax.axis_index("c") == 1)
    def _():
        o_ref[...] = b_ref[...]


def picked(for_core_0, for_core_1):
    return pl.pallas_call(
        picked_body,
        out_shape=VM((2, 256, 256), BF),
        in_specs=[IN] * 2,
        out_specs=IN,
        compiler_params=LIMIT,
        name="picked",
    )(for_core_0, for_core_1)


def outer_body(*refs):
    g, (h_ref, o_ref, buf, sems) = refs[:8], refs[8:]
    yl, x = lax.axis_index("yl"), lax.axis_index("x")
    copies = []
    for i in range(8):
        here = yl if i < 4 else 1 - yl
        r = pl.multiple_of((here * 4 + ((x - i) & 3)) * 256, 256)
        p = lax.dot_general(
            g[i][...].reshape(512, 256),
            h_ref[...],
            (((0,), (0,)), ((), ())),
            preferred_element_type=F32,
        )
        buf[i] = p.astype(BF).reshape(256, 4, 256)
        copy = pltpu.make_async_copy(buf.at[i], o_ref.at[pl.ds(r, 256)], sems.at[i])
        copy.start()
        copies.append(copy)
    for copy in copies:
        copy.wait()


def outer_product(blocks, hidden):
    return pl.pallas_call(
        outer_body,
        out_shape=jax.ShapeDtypeStruct((2048, 4, 256), BF),
        in_specs=[IN] * 9,
        out_specs=HBM,
        scratch_shapes=[
            VM((8, 256, 4, 256), BF),
            pltpu.SemaphoreType.DMA((8,)),
        ],
        compiler_params=LIMIT,
        name="outer",
    )(*kept(*blocks, hidden))


def per_device(hidden, grad_out, weight_base, block_scale):
    w5 = pltpu.with_memory_space_constraint(weight_base.reshape(4, 2, 4, 256, 256), pltpu.HBM)
    scales_t = block_scale.T

    sent = scaled_rows(w5, scales_t)
    r0 = sent[0]
    r1, r2, r3 = [shift(sent[k], first_axis_steps(k)) for k in (1, 2, 3)]

    grad_out, hidden, _ = lax.optimization_barrier((grad_out, hidden, r0))
    g0, h = all_tokens(packed(grad_out, hidden))
    g1, g2, g3 = [shift(g0, first_axis_steps(k)) for k in (1, 2, 3)]

    acc = early_sums(r0, r2, g0, g2)
    *sums, keep, give = partial_sums(acc, r1, r3, g0, g1, g2, g3)
    parts = [sums[0]] + [None] * 3
    for k in (2, 1, 3):
        parts[k] = shift(sums[k], second_axis_steps(k))
    blocks = summed_blocks(parts)
    blocks = lax.all_to_all(blocks, ("yl", "yh", "c"), 0, 0, tiled=True)
    grad_hidden = finished(blocks)

    seed = picked(lax.ppermute(give, "c", [(1, 0)]), keep)
    ring = lambda k: [(i, (i + k) % 4) for i in range(4)]
    mine = [seed] + [lax.ppermute(seed, "x", ring(k)) for k in (1, 2, 3)]
    theirs = [swap(m, "yl") for m in mine]
    grad_weight = outer_product(mine + theirs, h)
    return grad_hidden, grad_weight


def solution(mesh):
    fine = Mesh(mesh.devices.reshape(4, 2, 4, 2, 2), ("z", "yl", "x", "yh", "c"))
    narrow, wide = ("yh", "c"), ("z", "yl", "x")
    return jax.shard_map(
        per_device,
        mesh=fine,
        in_specs=(
            P(narrow, None, wide),
            P(narrow, wide),
            P(narrow, wide),
            P(narrow, wide),
        ),
        out_specs=(P(narrow, None, wide), P(narrow, None, wide)),
        check_vma=False,
    )
```

```python
import functools

import jax
import jax.numpy as jnp
from jax import lax
from jax.experimental import pallas as pl
from jax.experimental.pallas import tpu as pltpu
from jax.sharding import Mesh, PartitionSpec as P

BF = jnp.bfloat16
F32 = jnp.float32
VM = pltpu.VMEM


def first_axis_steps(k):
    pairs = []
    for z in range(4):
        for x in range(4):
            pairs.append(((z * 4 + x) * 2, (z * 4 + (x + k) % 4) * 2))
            pairs.append(((z * 4 + x) * 2 + 1, (((z + k) % 4) * 4 + x) * 2 + 1))
    return pairs


def second_axis_steps(k):
    pairs = []
    for z in range(4):
        for x in range(4):
            pairs.append(((z * 4 + x) * 2, (((z + k) % 4) * 4 + x) * 2))
            pairs.append(((z * 4 + x) * 2 + 1, (z * 4 + (x + k) % 4) * 2 + 1))
    return pairs


def shift(value, pairs):
    return lax.ppermute(value, ("z", "x", "c"), pairs)


def swap(value, axis):
    return lax.ppermute(value, axis, [(0, 1), (1, 0)])


LIMIT = pltpu.CompilerParams(vmem_limit_bytes=12 << 20)
EARLY = int(2e9)
IN = pl.BlockSpec(memory_space=VM)
HBM = pl.BlockSpec(memory_space=pltpu.HBM)


def kept(*values):
    return [pltpu.with_memory_space_constraint(v, VM) for v in values]


def roles():
    c, x, z = lax.axis_index("c"), lax.axis_index("x"), lax.axis_index("z")
    return c, jnp.where(c == 0, x, z), jnp.where(c == 0, z, x)


def spread_scales(s_ref, wide_ref):
    row = lax.broadcasted_iota(jnp.int32, (16, 256), 0)
    col = lax.broadcasted_iota(jnp.int32, (16, 256), 1)
    spread = jnp.where(col // 16 == row, 1.0, 0.0).astype(BF)
    wide_ref[...] = lax.dot_general(
        s_ref[...], spread, (((0,), (0,)), ((), ())), preferred_element_type=F32
    )


def scale_into(outs, w_ref, s_ref, wide_ref, sems):
    c, first, _ = roles()
    copies = []
    for j, (k, o_ref) in enumerate(outs):
        p = (first + k) & 3
        for i in range(4):
            z, x = c * p + (1 - c) * i, c * i + (1 - c) * p
            copy = pltpu.make_async_copy(
                w_ref.at[z, :, x], o_ref.at[pl.ds(2 * i, 2)], sems.at[j * 4 + i]
            )
            copy.start()
            copies.append((copy, o_ref, i, z, x))
    spread_scales(s_ref, wide_ref)
    for copy, o_ref, i, z, x in copies:
        copy.wait()
        for yl in range(2):
            r = pl.multiple_of((z * 8 + yl * 4 + x) * 16, 16)
            s = wide_ref[pl.ds(r, 16), :]
            w = o_ref[2 * i + yl].astype(F32).reshape(16, 16, 256)
            o_ref[2 * i + yl] = (w * s[:, None, :]).reshape(256, 256).astype(BF)


def scale_body(w_ref, s_ref, *refs):
    outs, wide_ref, sems = refs[:4], refs[4], refs[5]
    scale_into([(k, outs[k]) for k in (2, 1, 3, 0)], w_ref, s_ref, wide_ref, sems)


def scaled_rows(w5, scales_t):
    return pl.pallas_call(
        scale_body,
        out_shape=[VM((8, 256, 256), BF)] * 4,
        in_specs=[HBM, IN],
        out_specs=[IN] * 4,
        scratch_shapes=[VM((512, 256), F32), pltpu.SemaphoreType.DMA((16,))],
        compiler_params=LIMIT,
        name="scale",
    )(w5, scales_t)


def packed_body(g_ref, h_ref, o_ref):
    o_ref[0] = g_ref[...]
    h = h_ref[...].reshape(128, 1024)
    for n in range(4):
        o_ref[1 + n] = h[:, n * 256 : (n + 1) * 256]


def packed(grad_out, hidden):
    return pl.pallas_call(
        packed_body,
        out_shape=VM((5, 128, 256), BF),
        in_specs=[IN] * 2,
        out_specs=IN,
        compiler_params=LIMIT,
        name="packed",
    )(grad_out, hidden)


def tokens_body(p0, p1, p2, p3, g_ref, h_ref):
    n = lax.axis_index("yh") * 2 + lax.axis_index("c")
    for r, p in enumerate((p0, p1, p2, p3)):
        t = n ^ r
        g_ref[t >> 1, pl.ds(pl.multiple_of((t & 1) * 128, 128), 128), :] = p[0]
        rows = pl.ds(pl.multiple_of(t * 128, 128), 128)
        for m in range(4):
            h_ref[rows, m * 256 : (m + 1) * 256] = p[1 + m]


def all_tokens(own):
    far = swap(own, "yh")
    pieces = [own, swap(own, "c"), far, swap(far, "c")]
    return pl.pallas_call(
        tokens_body,
        out_shape=[VM((2, 256, 256), BF), VM((512, 1024), BF)],
        in_specs=[IN] * 4,
        out_specs=[IN] * 2,
        compiler_params=LIMIT,
        name="tokens",
    )(*kept(*pieces))


def block_product(g, w, q):
    return lax.dot_general(
        g[...].reshape(512, 256),
        w[pl.ds(q, 2)].reshape(512, 256),
        (((1,), (1,)), ((), ())),
        preferred_element_type=F32,
    )


def early_body(r0, r2, g0, g2, acc):
    for q in range(4):
        acc[q] = block_product(g0, r0, 2 * q) + block_product(g2, r2, 2 * q)


def early_sums(*operands):
    return pl.pallas_call(
        early_body,
        out_shape=VM((4, 512, 512), F32),
        in_specs=[IN] * 4,
        out_specs=IN,
        compiler_params=LIMIT,
        cost_estimate=pl.CostEstimate(flops=EARLY, bytes_accessed=6 << 20, transcendentals=0),
        name="early",
    )(*kept(*operands))


def partial_body(acc, r1, r3, g0, g1, g2, g3, *outs):
    keep, give = outs[4:]
    _, _, second = roles()
    z, yh = lax.axis_index("z"), lax.axis_index("yh")
    g = (g0, g1, g2, g3)
    for k in range(4):

        @pl.when(((z - 2 * yh) & 3) == k)
        def _():
            give[...] = g[k][...]

        @pl.when(((z - 2 * yh - 1) & 3) == k)
        def _():
            keep[...] = g[k][...]

    for k in (2, 1, 3, 0):
        q = (second + k) & 3
        total = acc[q] + block_product(g[1], r1, 2 * q) + block_product(g[3], r3, 2 * q)
        outs[k][...] = total.astype(outs[k].dtype)


def partial_sums(*operands):
    return pl.pallas_call(
        partial_body,
        out_shape=[VM((512, 512), F32)]
        + [VM((512, 512), BF)] * 3
        + [VM((2, 256, 256), BF)] * 2,
        in_specs=[IN] * 7,
        out_specs=[IN] * 6,
        compiler_params=LIMIT,
        name="partial",
    )(*kept(*operands))


def gather_body(a, b, c, d, o_ref):
    total = a[...] + b[...].astype(F32) + c[...].astype(F32) + d[...].astype(F32)
    total = total.astype(BF)
    for yl in range(2):
        for n in range(4):
            t = n * 128
            o_ref[yl * 4 + n] = total[t : t + 128, yl * 256 : (yl + 1) * 256]


def summed_blocks(parts):
    return pl.pallas_call(
        gather_body,
        out_shape=VM((8, 128, 256), BF),
        in_specs=[IN] * 4,
        out_specs=IN,
        compiler_params=LIMIT,
        name="summed",
    )(parts[0], *kept(*parts[1:]))


def finish_body(r_ref, o_ref):
    r = [(r_ref[n].astype(F32) + r_ref[4 + n].astype(F32)).astype(BF) for n in range(4)]
    o_ref[...] = jnp.concatenate(r, axis=1).reshape(128, 4, 256)


def finished(blocks):
    return pl.pallas_call(
        finish_body,
        out_shape=jax.ShapeDtypeStruct((128, 4, 256), BF),
        in_specs=[IN],
        out_specs=IN,
        compiler_params=LIMIT,
        name="finish",
    )(*kept(blocks))


def picked_body(a_ref, b_ref, o_ref):
    @pl.when(lax.axis_index("c") == 0)
    def _():
        o_ref[...] = a_ref[...]

    @pl.when(lax.axis_index("c") == 1)
    def _():
        o_ref[...] = b_ref[...]


def picked(for_core_0, for_core_1):
    return pl.pallas_call(
        picked_body,
        out_shape=VM((2, 256, 256), BF),
        in_specs=[IN] * 2,
        out_specs=IN,
        compiler_params=LIMIT,
        name="picked",
    )(for_core_0, for_core_1)


def paired_body(a_ref, b_ref, o_ref):
    o_ref[0:2] = a_ref[...]
    o_ref[2:4] = b_ref[...]


def paired(a, b):
    return pl.pallas_call(
        paired_body,
        out_shape=VM((4, 256, 256), BF),
        in_specs=[IN] * 2,
        out_specs=IN,
        compiler_params=LIMIT,
        name="paired",
    )(*kept(a, b))


def outer_body(h_ref, far_ref, *refs):
    near, (o_ref, buf, sems) = refs[:6], refs[6:]
    yl, x = lax.axis_index("yl"), lax.axis_index("x")
    blocks = [(yl, k, r) for k, r in zip((0, 1, 3), near[:3])]
    blocks += [(1 - yl, k, r) for k, r in zip((0, 1, 3), near[3:])]
    blocks += [(yl, 2, far_ref.at[0:2]), (1 - yl, 2, far_ref.at[2:4])]
    copies = []
    for i, (here, k, g) in enumerate(blocks):
        r = pl.multiple_of((here * 4 + ((x - k) & 3)) * 256, 256)
        p = lax.dot_general(
            g[...].reshape(512, 256),
            h_ref[...],
            (((0,), (0,)), ((), ())),
            preferred_element_type=F32,
        )
        buf[i] = p.astype(BF).reshape(256, 4, 256)
        copy = pltpu.make_async_copy(buf.at[i], o_ref.at[pl.ds(r, 256)], sems.at[i])
        copy.start()
        copies.append(copy)
    for copy in copies:
        copy.wait()


def outer_product(*operands):
    return pl.pallas_call(
        outer_body,
        out_shape=jax.ShapeDtypeStruct((2048, 4, 256), BF),
        in_specs=[IN] * 8,
        out_specs=HBM,
        scratch_shapes=[
            VM((8, 256, 4, 256), BF),
            pltpu.SemaphoreType.DMA((8,)),
        ],
        compiler_params=LIMIT,
        name="outer",
    )(*kept(*operands))


def per_device(hidden, grad_out, weight_base, block_scale):
    w5 = pltpu.with_memory_space_constraint(weight_base.reshape(4, 2, 4, 256, 256), pltpu.HBM)
    scales_t = block_scale.T

    sent = scaled_rows(w5, scales_t)
    r0 = sent[0]
    r1, r2, r3 = [shift(sent[k], first_axis_steps(k)) for k in (1, 2, 3)]

    grad_out, hidden, _ = lax.optimization_barrier((grad_out, hidden, r0))
    g0, h = all_tokens(packed(grad_out, hidden))
    g2, g3 = [shift(g0, first_axis_steps(k)) for k in (2, 3)]
    later, r2 = lax.optimization_barrier((g0, r2))
    g1 = shift(later, first_axis_steps(1))

    acc = early_sums(r0, r2, g0, g2)
    *sums, keep, give = partial_sums(acc, r1, r3, g0, g1, g2, g3)
    parts = [sums[0]] + [None] * 3
    for k in (2, 1, 3):
        parts[k] = shift(sums[k], second_axis_steps(k))
    blocks = summed_blocks(parts)
    blocks = lax.all_to_all(blocks, ("yl", "yh", "c"), 0, 0, tiled=True)
    grad_hidden = finished(blocks)

    seed = picked(lax.ppermute(give, "c", [(1, 0)]), keep)
    ring = lambda k: [(i, (i + k) % 4) for i in range(4)]
    other = swap(seed, "yl")
    x1, x3 = [lax.ppermute(seed, "x", ring(k)) for k in (1, 3)]
    x2 = lax.ppermute(paired(seed, other), "x", ring(2))
    grad_weight = outer_product(h, x2, seed, x1, x3, other, swap(x1, "yl"), swap(x3, "yl"))
    return grad_hidden, grad_weight


def solution(mesh):
    fine = Mesh(mesh.devices.reshape(4, 2, 4, 2, 2), ("z", "yl", "x", "yh", "c"))
    narrow, wide = ("yh", "c"), ("z", "yl", "x")
    return jax.shard_map(
        per_device,
        mesh=fine,
        in_specs=(
            P(narrow, None, wide),
            P(narrow, wide),
            P(narrow, wide),
            P(narrow, wide),
        ),
        out_specs=(P(narrow, None, wide), P(narrow, None, wide)),
        check_vma=False,
    )
```

```python
import functools

import jax
import jax.numpy as jnp
from jax import lax
from jax.experimental import pallas as pl
from jax.experimental.pallas import tpu as pltpu
from jax.sharding import Mesh, PartitionSpec as P

BF = jnp.bfloat16
F32 = jnp.float32
VM = pltpu.VMEM


def first_axis_steps(k):
    pairs = []
    for z in range(4):
        for x in range(4):
            pairs.append(((z * 4 + x) * 2, (z * 4 + (x + k) % 4) * 2))
            pairs.append(((z * 4 + x) * 2 + 1, (((z + k) % 4) * 4 + x) * 2 + 1))
    return pairs


def second_axis_steps(k):
    pairs = []
    for z in range(4):
        for x in range(4):
            pairs.append(((z * 4 + x) * 2, (((z + k) % 4) * 4 + x) * 2))
            pairs.append(((z * 4 + x) * 2 + 1, (z * 4 + (x + k) % 4) * 2 + 1))
    return pairs


def shift(value, pairs):
    return lax.ppermute(value, ("z", "x", "c"), pairs)


def swap(value, axis):
    return lax.ppermute(value, axis, [(0, 1), (1, 0)])


LIMIT = pltpu.CompilerParams(vmem_limit_bytes=12 << 20)
EARLY = int(2e9)
IN = pl.BlockSpec(memory_space=VM)
HBM = pl.BlockSpec(memory_space=pltpu.HBM)


def kept(*values):
    return [pltpu.with_memory_space_constraint(v, VM) for v in values]


def roles():
    c, x, z = lax.axis_index("c"), lax.axis_index("x"), lax.axis_index("z")
    return c, jnp.where(c == 0, x, z), jnp.where(c == 0, z, x)


def spread_scales(s_ref, wide_ref):
    row = lax.broadcasted_iota(jnp.int32, (16, 256), 0)
    col = lax.broadcasted_iota(jnp.int32, (16, 256), 1)
    spread = jnp.where(col // 16 == row, 1.0, 0.0).astype(BF)
    wide_ref[...] = lax.dot_general(
        s_ref[...], spread, (((0,), (0,)), ((), ())), preferred_element_type=F32
    )


def scale_into(outs, w_ref, s_ref, narrow_ref, wide_ref, sems):
    c, first, _ = roles()
    scales = pltpu.make_async_copy(s_ref, narrow_ref, sems.at[16])
    scales.start()
    copies = []
    for j, (k, o_ref) in enumerate(outs):
        p = (first + k) & 3
        for i in range(4):
            z, x = c * p + (1 - c) * i, c * i + (1 - c) * p
            copy = pltpu.make_async_copy(
                w_ref.at[z, :, x], o_ref.at[pl.ds(2 * i, 2)], sems.at[j * 4 + i]
            )
            copy.start()
            copies.append((copy, o_ref, i, z, x))
    scales.wait()
    spread_scales(narrow_ref, wide_ref)
    for copy, o_ref, i, z, x in copies:
        copy.wait()
        for yl in range(2):
            r = pl.multiple_of((z * 8 + yl * 4 + x) * 16, 16)
            s = wide_ref[pl.ds(r, 16), :]
            w = o_ref[2 * i + yl].astype(F32).reshape(16, 16, 256)
            o_ref[2 * i + yl] = (w * s[:, None, :]).reshape(256, 256).astype(BF)


def scale_body(w_ref, s_ref, *refs):
    outs, scratch = refs[:4], refs[4:]
    scale_into([(k, outs[k]) for k in (1, 3, 2, 0)], w_ref, s_ref, *scratch)


def scaled_rows(w5, scales_t):
    return pl.pallas_call(
        scale_body,
        out_shape=[VM((8, 256, 256), BF)] * 4,
        in_specs=[HBM, HBM],
        out_specs=[IN] * 4,
        scratch_shapes=[VM((16, 512), BF), VM((512, 256), F32), pltpu.SemaphoreType.DMA((17,))],
        compiler_params=LIMIT,
        name="scale",
    )(w5, scales_t)


def packed_body(g_ref, h_ref, o_ref):
    o_ref[0] = g_ref[...]
    h = h_ref[...].reshape(128, 1024)
    for n in range(4):
        o_ref[1 + n] = h[:, n * 256 : (n + 1) * 256]


def packed(grad_out, hidden):
    return pl.pallas_call(
        packed_body,
        out_shape=VM((5, 128, 256), BF),
        in_specs=[IN] * 2,
        out_specs=IN,
        compiler_params=LIMIT,
        name="packed",
    )(grad_out, hidden)


def tokens_body(p0, p1, p2, p3, g_ref, h_ref):
    n = lax.axis_index("yh") * 2 + lax.axis_index("c")
    for r, p in enumerate((p0, p1, p2, p3)):
        t = n ^ r
        g_ref[t >> 1, pl.ds(pl.multiple_of((t & 1) * 128, 128), 128), :] = p[0]
        rows = pl.ds(pl.multiple_of(t * 128, 128), 128)
        for m in range(4):
            h_ref[rows, m * 256 : (m + 1) * 256] = p[1 + m]


def all_tokens(own):
    far = swap(own, "yh")
    pieces = [own, swap(own, "c"), far, swap(far, "c")]
    return pl.pallas_call(
        tokens_body,
        out_shape=[VM((2, 256, 256), BF), VM((512, 1024), BF)],
        in_specs=[IN] * 4,
        out_specs=[IN] * 2,
        compiler_params=LIMIT,
        name="tokens",
    )(*kept(*pieces))


def block_product(g, w, q):
    return lax.dot_general(
        g[...].reshape(512, 256),
        w[pl.ds(q, 2)].reshape(512, 256),
        (((1,), (1,)), ((), ())),
        preferred_element_type=F32,
    )


def early_body(r0, r3, g0, g3, acc):
    for q in range(4):
        acc[q] = block_product(g0, r0, 2 * q) + block_product(g3, r3, 2 * q)


def early_sums(*operands):
    return pl.pallas_call(
        early_body,
        out_shape=VM((4, 512, 512), F32),
        in_specs=[IN] * 4,
        out_specs=IN,
        compiler_params=LIMIT,
        cost_estimate=pl.CostEstimate(flops=EARLY, bytes_accessed=6 << 20, transcendentals=0),
        name="early",
    )(*kept(*operands))


def partial_body(acc, r1, r2, g0, g1, g2, g3, *outs):
    keep, give = outs[4:]
    _, _, second = roles()
    z, yh = lax.axis_index("z"), lax.axis_index("yh")
    g = (g0, g1, g2, g3)
    for k in range(4):

        @pl.when(((z - 2 * yh) & 3) == k)
        def _():
            give[...] = g[k][...]

        @pl.when(((z - 2 * yh - 1) & 3) == k)
        def _():
            keep[...] = g[k][...]

    for k in (2, 1, 3, 0):
        q = (second + k) & 3
        total = acc[q] + block_product(g[1], r1, 2 * q) + block_product(g[2], r2, 2 * q)
        outs[k][...] = total.astype(outs[k].dtype)


def partial_sums(*operands):
    return pl.pallas_call(
        partial_body,
        out_shape=[VM((512, 512), F32)]
        + [VM((512, 512), BF)] * 3
        + [VM((2, 256, 256), BF)] * 2,
        in_specs=[IN] * 7,
        out_specs=[IN] * 6,
        compiler_params=LIMIT,
        name="partial",
    )(*kept(*operands))


def gather_body(a, b, c, d, o_ref):
    total = a[...] + b[...].astype(F32) + c[...].astype(F32) + d[...].astype(F32)
    total = total.astype(BF)
    for yl in range(2):
        for n in range(4):
            t = n * 128
            o_ref[yl * 4 + n] = total[t : t + 128, yl * 256 : (yl + 1) * 256]


def summed_blocks(parts):
    return pl.pallas_call(
        gather_body,
        out_shape=VM((8, 128, 256), BF),
        in_specs=[IN] * 4,
        out_specs=IN,
        compiler_params=LIMIT,
        name="summed",
    )(parts[0], *kept(*parts[1:]))


def finish_body(r_ref, o_ref):
    r = [(r_ref[n].astype(F32) + r_ref[4 + n].astype(F32)).astype(BF) for n in range(4)]
    o_ref[...] = jnp.concatenate(r, axis=1).reshape(128, 4, 256)


def finished(blocks):
    return pl.pallas_call(
        finish_body,
        out_shape=jax.ShapeDtypeStruct((128, 4, 256), BF),
        in_specs=[IN],
        out_specs=IN,
        compiler_params=LIMIT,
        name="finish",
    )(*kept(blocks))


def picked_body(a_ref, b_ref, o_ref):
    @pl.when(lax.axis_index("c") == 0)
    def _():
        o_ref[...] = a_ref[...]

    @pl.when(lax.axis_index("c") == 1)
    def _():
        o_ref[...] = b_ref[...]


def picked(for_core_0, for_core_1):
    return pl.pallas_call(
        picked_body,
        out_shape=VM((2, 256, 256), BF),
        in_specs=[IN] * 2,
        out_specs=IN,
        compiler_params=LIMIT,
        name="picked",
    )(for_core_0, for_core_1)


def paired_body(a_ref, b_ref, o_ref):
    o_ref[0:2] = a_ref[...]
    o_ref[2:4] = b_ref[...]


def paired(a, b):
    return pl.pallas_call(
        paired_body,
        out_shape=VM((4, 256, 256), BF),
        in_specs=[IN] * 2,
        out_specs=IN,
        compiler_params=LIMIT,
        name="paired",
    )(*kept(a, b))


def outer_into(blocks, h_ref, o_ref, buf, sems):
    x = lax.axis_index("x")
    copies = []
    for i, (yl, k, g) in enumerate(blocks):
        r = pl.multiple_of((yl * 4 + ((x - k) & 3)) * 256, 256)
        p = lax.dot_general(
            g[...].reshape(512, 256),
            h_ref[...],
            (((0,), (0,)), ((), ())),
            preferred_element_type=F32,
        )
        buf[i] = p.astype(BF).reshape(256, 4, 256)
        copy = pltpu.make_async_copy(buf.at[i], o_ref.at[pl.ds(r, 256)], sems.at[i])
        copy.start()
        copies.append(copy)
    for copy in copies:
        copy.wait()


def first_half_body(h_ref, seed, other, back, back_other, *refs):
    yl, c = lax.axis_index("yl"), lax.axis_index("c")
    k = 3 - 2 * c
    blocks = [(yl, 0, seed), (1 - yl, 0, other), (yl, k, back), (1 - yl, k, back_other)]
    outer_into(blocks, h_ref, *refs)


def second_half_body(o_in, h_ref, ahead, far, *refs):
    yl, c = lax.axis_index("yl"), lax.axis_index("c")
    blocks = []
    for k, ref in ((1 + 2 * c, ahead), (2, far)):
        blocks += [(yl, k, ref.at[0:2]), (1 - yl, k, ref.at[2:4])]
    outer_into(blocks, h_ref, *refs)


def outer_half(body, name, operands, so_far=None):
    aliased = so_far is not None
    return pl.pallas_call(
        body,
        out_shape=jax.ShapeDtypeStruct((2048, 4, 256), BF),
        in_specs=[HBM] * aliased + [IN] * len(operands),
        out_specs=HBM,
        scratch_shapes=[VM((4, 256, 4, 256), BF), pltpu.SemaphoreType.DMA((4,))],
        input_output_aliases={0: 0} if aliased else {},
        compiler_params=LIMIT,
        cost_estimate=pl.CostEstimate(flops=int(2e9), bytes_accessed=5 << 20, transcendentals=0),
        name=name,
    )(*([so_far] if aliased else []), *kept(*operands))


def along_x(value, forward_core):
    pairs = []
    for x in range(4):
        for c in range(2):
            k = 1 if c == forward_core else 3
            pairs.append((x * 2 + c, (x + k) % 4 * 2 + c))
    return lax.ppermute(value, ("x", "c"), pairs)


def per_device(hidden, grad_out, weight_base, block_scale):
    w5 = pltpu.with_memory_space_constraint(weight_base.reshape(4, 2, 4, 256, 256), pltpu.HBM)
    scales_t = pltpu.with_memory_space_constraint(block_scale.T, pltpu.HBM)

    sent = scaled_rows(w5, scales_t)
    r0 = sent[0]
    r1, r2, r3 = [shift(sent[k], first_axis_steps(k)) for k in (1, 2, 3)]

    grad_out, hidden, _ = lax.optimization_barrier((grad_out, hidden, r0))
    g0, h = all_tokens(packed(grad_out, hidden))
    g2, g3 = [shift(g0, first_axis_steps(k)) for k in (2, 3)]
    later, r1 = lax.optimization_barrier((g0, r1))
    g1 = shift(later, first_axis_steps(1))

    acc = early_sums(r0, r3, g0, g3)
    *sums, keep, give = partial_sums(acc, r1, r2, g0, g1, g2, g3)
    parts = [sums[0]] + [None] * 3
    for k in (2, 1, 3):
        parts[k] = shift(sums[k], second_axis_steps(k))
    blocks = summed_blocks(parts)
    blocks = lax.all_to_all(blocks, ("yl", "yh", "c"), 0, 0, tiled=True)
    grad_hidden = finished(blocks)

    seed = picked(lax.ppermute(give, "c", [(1, 0)]), keep)
    other = swap(seed, "yl")
    back = along_x(seed, 1)
    both = paired(seed, other)
    ahead = along_x(both, 0)
    far = lax.ppermute(both, "x", [(i, (i + 2) % 4) for i in range(4)])
    half = outer_half(first_half_body, "first_half", (h, seed, other, back, swap(back, "yl")))
    grad_weight = outer_half(second_half_body, "second_half", (h, ahead, far), half)
    return grad_hidden, grad_weight


def solution(mesh):
    fine = Mesh(mesh.devices.reshape(4, 2, 4, 2, 2), ("z", "yl", "x", "yh", "c"))
    narrow, wide = ("yh", "c"), ("z", "yl", "x")
    return jax.shard_map(
        per_device,
        mesh=fine,
        in_specs=(
            P(narrow, None, wide),
            P(narrow, wide),
            P(narrow, wide),
            P(narrow, wide),
        ),
        out_specs=(P(narrow, None, wide), P(narrow, None, wide)),
        check_vma=False,
    )
```

```python
import functools

import jax
import jax.numpy as jnp
from jax import lax
from jax.experimental import pallas as pl
from jax.experimental.pallas import tpu as pltpu
from jax.sharding import Mesh, PartitionSpec as P

BF = jnp.bfloat16
F32 = jnp.float32
VM = pltpu.VMEM


def first_axis_steps(k):
    pairs = []
    for z in range(4):
        for x in range(4):
            pairs.append(((z * 4 + x) * 2, (z * 4 + (x + k) % 4) * 2))
            pairs.append(((z * 4 + x) * 2 + 1, (((z + k) % 4) * 4 + x) * 2 + 1))
    return pairs


def second_axis_steps(k):
    pairs = []
    for z in range(4):
        for x in range(4):
            pairs.append(((z * 4 + x) * 2, (((z + k) % 4) * 4 + x) * 2))
            pairs.append(((z * 4 + x) * 2 + 1, (z * 4 + (x + k) % 4) * 2 + 1))
    return pairs


def shift(value, pairs):
    return lax.ppermute(value, ("z", "x", "c"), pairs)


def swap(value, axis):
    return lax.ppermute(value, axis, [(0, 1), (1, 0)])


LIMIT = pltpu.CompilerParams(vmem_limit_bytes=12 << 20)
EARLY = int(2e9)
IN = pl.BlockSpec(memory_space=VM)
HBM = pl.BlockSpec(memory_space=pltpu.HBM)


def kept(*values):
    return [pltpu.with_memory_space_constraint(v, VM) for v in values]


def roles():
    c, x, z = lax.axis_index("c"), lax.axis_index("x"), lax.axis_index("z")
    return c, jnp.where(c == 0, x, z), jnp.where(c == 0, z, x)


def spread_scales(s_ref, wide_ref):
    row = lax.broadcasted_iota(jnp.int32, (16, 256), 0)
    col = lax.broadcasted_iota(jnp.int32, (16, 256), 1)
    spread = jnp.where(col // 16 == row, 1.0, 0.0).astype(BF)
    wide_ref[...] = lax.dot_general(
        s_ref[...], spread, (((0,), (0,)), ((), ())), preferred_element_type=F32
    )


def scale_into(outs, w_ref, s_ref, narrow_ref, wide_ref, sems):
    c, first, _ = roles()
    scales = pltpu.make_async_copy(s_ref, narrow_ref, sems.at[16])
    scales.start()
    copies = []
    for j, (k, o_ref) in enumerate(outs):
        p = (first + k) & 3
        for i in range(4):
            z, x = c * p + (1 - c) * i, c * i + (1 - c) * p
            copy = pltpu.make_async_copy(
                w_ref.at[z, :, x], o_ref.at[pl.ds(2 * i, 2)], sems.at[j * 4 + i]
            )
            copy.start()
            copies.append((copy, o_ref, i, z, x))
    scales.wait()
    spread_scales(narrow_ref, wide_ref)
    for copy, o_ref, i, z, x in copies:
        copy.wait()
        for yl in range(2):
            r = pl.multiple_of((z * 8 + yl * 4 + x) * 16, 16)
            s = wide_ref[pl.ds(r, 16), :]
            w = o_ref[2 * i + yl].astype(F32).reshape(16, 16, 256)
            o_ref[2 * i + yl] = (w * s[:, None, :]).reshape(256, 256).astype(BF)


def scale_body(w_ref, s_ref, *refs):
    outs, scratch = refs[:4], refs[4:]
    scale_into([(k, outs[k]) for k in (1, 3, 2, 0)], w_ref, s_ref, *scratch)


def scaled_rows(w5, scales_t):
    return pl.pallas_call(
        scale_body,
        out_shape=[VM((8, 256, 256), BF)] * 4,
        in_specs=[HBM, HBM],
        out_specs=[IN] * 4,
        scratch_shapes=[VM((16, 512), BF), VM((512, 256), F32), pltpu.SemaphoreType.DMA((17,))],
        compiler_params=LIMIT,
        name="scale",
    )(w5, scales_t)


def swapped(own):
    far = swap(own, "yh")
    return [own, swap(own, "c"), far, swap(far, "c")]


def tokens_body(p0, p1, p2, p3, g_ref):
    n = lax.axis_index("yh") * 2 + lax.axis_index("c")
    for r, p in enumerate((p0, p1, p2, p3)):
        t = n ^ r
        g_ref[t >> 1, pl.ds(pl.multiple_of((t & 1) * 128, 128), 128), :] = p[...]


def all_tokens(own):
    return pl.pallas_call(
        tokens_body,
        out_shape=VM((2, 256, 256), BF),
        in_specs=[IN] * 4,
        out_specs=IN,
        compiler_params=LIMIT,
        name="tokens",
    )(*kept(*swapped(own)))


def flat_body(h_ref, o_ref):
    o_ref[...] = h_ref[...].reshape(128, 1024)


def flat(hidden):
    return pl.pallas_call(
        flat_body,
        out_shape=VM((128, 1024), BF),
        in_specs=[IN],
        out_specs=IN,
        compiler_params=LIMIT,
        name="flat",
    )(hidden)


def block_product(g, w, q):
    return lax.dot_general(
        g[...].reshape(512, 256),
        w[pl.ds(q, 2)].reshape(512, 256),
        (((1,), (1,)), ((), ())),
        preferred_element_type=F32,
    )


def early_body(r0, r1, r3, g0, g1, g3, acc):
    for q in range(4):
        acc[q] = (
            block_product(g0, r0, 2 * q)
            + block_product(g1, r1, 2 * q)
            + block_product(g3, r3, 2 * q)
        )


def early_sums(*operands):
    return pl.pallas_call(
        early_body,
        out_shape=VM((4, 512, 512), F32),
        in_specs=[IN] * 6,
        out_specs=IN,
        compiler_params=LIMIT,
        cost_estimate=pl.CostEstimate(flops=EARLY, bytes_accessed=6 << 20, transcendentals=0),
        name="early",
    )(*kept(*operands))


def plane_body(g0, g1, g2, g3, keep, give):
    z, yh = lax.axis_index("z"), lax.axis_index("yh")
    g = (g0, g1, g2, g3)
    for k in range(4):

        @pl.when(((z - 2 * yh) & 3) == k)
        def _():
            give[...] = g[k][...]

        @pl.when(((z - 2 * yh - 1) & 3) == k)
        def _():
            keep[...] = g[k][...]


def plane_blocks(*grads):
    return pl.pallas_call(
        plane_body,
        out_shape=[VM((2, 256, 256), BF)] * 2,
        in_specs=[IN] * 4,
        out_specs=[IN] * 2,
        compiler_params=LIMIT,
        name="plane",
    )(*kept(*grads))


def partial_body(acc, r2, g2, *outs):
    _, _, second = roles()
    for k in (2, 1, 3, 0):
        q = (second + k) & 3
        total = acc[q] + block_product(g2, r2, 2 * q)
        outs[k][...] = total.astype(outs[k].dtype)


def partial_sums(*operands):
    return pl.pallas_call(
        partial_body,
        out_shape=[VM((512, 512), F32)]
        + [VM((512, 512), BF)] * 3,
        in_specs=[IN] * 3,
        out_specs=[IN] * 4,
        compiler_params=LIMIT,
        name="partial",
    )(*kept(*operands))


def gather_body(a, b, c, d, o_ref):
    total = a[...] + b[...].astype(F32) + c[...].astype(F32) + d[...].astype(F32)
    total = total.astype(BF)
    for yl in range(2):
        for n in range(4):
            t = n * 128
            o_ref[yl * 4 + n] = total[t : t + 128, yl * 256 : (yl + 1) * 256]


def summed_blocks(parts):
    return pl.pallas_call(
        gather_body,
        out_shape=VM((8, 128, 256), BF),
        in_specs=[IN] * 4,
        out_specs=IN,
        compiler_params=LIMIT,
        name="summed",
    )(parts[0], *kept(*parts[1:]))


def finish_body(r_ref, o_ref):
    r = [(r_ref[n].astype(F32) + r_ref[4 + n].astype(F32)).astype(BF) for n in range(4)]
    o_ref[...] = jnp.concatenate(r, axis=1).reshape(128, 4, 256)


def finished(blocks):
    return pl.pallas_call(
        finish_body,
        out_shape=jax.ShapeDtypeStruct((128, 4, 256), BF),
        in_specs=[IN],
        out_specs=IN,
        compiler_params=LIMIT,
        name="finish",
    )(*kept(blocks))


def picked_body(a_ref, b_ref, o_ref):
    @pl.when(lax.axis_index("c") == 0)
    def _():
        o_ref[...] = a_ref[...]

    @pl.when(lax.axis_index("c") == 1)
    def _():
        o_ref[...] = b_ref[...]


def picked(for_core_0, for_core_1):
    return pl.pallas_call(
        picked_body,
        out_shape=VM((2, 256, 256), BF),
        in_specs=[IN] * 2,
        out_specs=IN,
        compiler_params=LIMIT,
        name="picked",
    )(for_core_0, for_core_1)


def paired_body(a_ref, b_ref, o_ref):
    o_ref[0:2] = a_ref[...]
    o_ref[2:4] = b_ref[...]


def paired(a, b):
    return pl.pallas_call(
        paired_body,
        out_shape=VM((4, 256, 256), BF),
        in_specs=[IN] * 2,
        out_specs=IN,
        compiler_params=LIMIT,
        name="paired",
    )(*kept(a, b))


def outer_into(blocks, h_ref, o_ref, buf, sems):
    x = lax.axis_index("x")
    copies = []
    for i, (yl, k, g) in enumerate(blocks):
        r = pl.multiple_of((yl * 4 + ((x - k) & 3)) * 256, 256)
        p = lax.dot_general(
            g[...].reshape(512, 256),
            h_ref[...],
            (((0,), (0,)), ((), ())),
            preferred_element_type=F32,
        )
        buf[i] = p.astype(BF).reshape(256, 4, 256)
        copy = pltpu.make_async_copy(buf.at[i], o_ref.at[pl.ds(r, 256)], sems.at[i])
        copy.start()
        copies.append(copy)
    for copy in copies:
        copy.wait()


def first_half_body(p0, p1, p2, p3, seed, other, back, back_other, o_ref, h_ref, *refs):
    yl, c = lax.axis_index("yl"), lax.axis_index("c")
    n = lax.axis_index("yh") * 2 + c
    for r, p in enumerate((p0, p1, p2, p3)):
        h_ref[pl.ds(pl.multiple_of((n ^ r) * 128, 128), 128), :] = p[...]
    k = 3 - 2 * c
    blocks = [(yl, 0, seed), (1 - yl, 0, other), (yl, k, back), (1 - yl, k, back_other)]
    outer_into(blocks, h_ref, o_ref, *refs)


def second_half_body(o_in, h_ref, ahead, far, *refs):
    yl, c = lax.axis_index("yl"), lax.axis_index("c")
    blocks = []
    for k, ref in ((1 + 2 * c, ahead), (2, far)):
        blocks += [(yl, k, ref.at[0:2]), (1 - yl, k, ref.at[2:4])]
    outer_into(blocks, h_ref, *refs)


def outer_half(body, name, operands, so_far=None):
    aliased = so_far is not None
    out = jax.ShapeDtypeStruct((2048, 4, 256), BF)
    return pl.pallas_call(
        body,
        out_shape=[out] if aliased else [out, VM((512, 1024), BF)],
        in_specs=[HBM] * aliased + [IN] * len(operands),
        out_specs=[HBM] if aliased else [HBM, IN],
        scratch_shapes=[VM((4, 256, 4, 256), BF), pltpu.SemaphoreType.DMA((4,))],
        input_output_aliases={0: 0} if aliased else {},
        compiler_params=LIMIT,
        cost_estimate=pl.CostEstimate(flops=int(2e9), bytes_accessed=5 << 20, transcendentals=0),
        name=name,
    )(*([so_far] if aliased else []), *kept(*operands))


def along_x(value, forward_core):
    pairs = []
    for x in range(4):
        for c in range(2):
            k = 1 if c == forward_core else 3
            pairs.append((x * 2 + c, (x + k) % 4 * 2 + c))
    return lax.ppermute(value, ("x", "c"), pairs)


def per_device(hidden, grad_out, weight_base, block_scale):
    w5 = pltpu.with_memory_space_constraint(weight_base.reshape(4, 2, 4, 256, 256), pltpu.HBM)
    scales_t = pltpu.with_memory_space_constraint(block_scale.T, pltpu.HBM)

    sent = scaled_rows(w5, scales_t)
    r0 = sent[0]
    r1, r3 = [shift(sent[k], first_axis_steps(k)) for k in (1, 3)]
    grad_out, hidden, _ = lax.optimization_barrier((grad_out, hidden, r0))
    g0 = all_tokens(grad_out)
    g1, g3 = [shift(g0, first_axis_steps(k)) for k in (1, 3)]
    sent2, _ = lax.optimization_barrier((sent[2], g0))
    r2, g2 = shift(sent2, first_axis_steps(2)), shift(g0, first_axis_steps(2))

    acc = early_sums(r0, r1, r3, g0, g1, g3)
    plane, acc, hidden = lax.optimization_barrier(((g0, g1, g2, g3), acc, hidden))
    keep, give = plane_blocks(*plane)
    seed = picked(lax.ppermute(give, "c", [(1, 0)]), keep)
    other = swap(seed, "yl")
    both = paired(seed, other)
    pieces = swapped(flat(hidden))
    acc, both, seed, pieces = lax.optimization_barrier((acc, both, seed, pieces))

    sums = partial_sums(acc, r2, g2)
    parts = [sums[0]] + [None] * 3
    for k in (1, 3, 2):
        parts[k] = shift(sums[k], second_axis_steps(k))
    seed, both, _ = lax.optimization_barrier((seed, both, sums[0]))
    back = along_x(seed, 1)
    ahead = along_x(both, 0)
    far = lax.ppermute(both, "x", [(i, (i + 2) % 4) for i in range(4)])
    back, parts[0] = lax.optimization_barrier((back, parts[0]))
    back_other = swap(back, "yl")

    blocks = summed_blocks(parts)
    blocks = lax.all_to_all(blocks, ("yl", "yh", "c"), 0, 0, tiled=True)
    grad_hidden = finished(blocks)
    half, h = outer_half(
        first_half_body, "first_half", (*pieces, seed, other, back, back_other)
    )
    grad_weight = outer_half(second_half_body, "second_half", (h, ahead, far), half)[0]
    return grad_hidden, grad_weight


def solution(mesh):
    fine = Mesh(mesh.devices.reshape(4, 2, 4, 2, 2), ("z", "yl", "x", "yh", "c"))
    narrow, wide = ("yh", "c"), ("z", "yl", "x")
    return jax.shard_map(
        per_device,
        mesh=fine,
        in_specs=(
            P(narrow, None, wide),
            P(narrow, wide),
            P(narrow, wide),
            P(narrow, wide),
        ),
        out_specs=(P(narrow, None, wide), P(narrow, None, wide)),
        check_vma=False,
    )
```

```python
import functools

import jax
import jax.numpy as jnp
from jax import lax
from jax.experimental import pallas as pl
from jax.experimental.pallas import tpu as pltpu
from jax.sharding import Mesh, PartitionSpec as P

BF = jnp.bfloat16
F32 = jnp.float32
VM = pltpu.VMEM


def first_axis_steps(k):
    pairs = []
    for z in range(4):
        for x in range(4):
            pairs.append(((z * 4 + x) * 2, (z * 4 + (x + k) % 4) * 2))
            pairs.append(((z * 4 + x) * 2 + 1, (((z + k) % 4) * 4 + x) * 2 + 1))
    return pairs


def second_axis_steps(k):
    pairs = []
    for z in range(4):
        for x in range(4):
            pairs.append(((z * 4 + x) * 2, (((z + k) % 4) * 4 + x) * 2))
            pairs.append(((z * 4 + x) * 2 + 1, (z * 4 + (x + k) % 4) * 2 + 1))
    return pairs


def shift(value, pairs):
    return lax.ppermute(value, ("z", "x", "c"), pairs)


def swap(value, axis):
    return lax.ppermute(value, axis, [(0, 1), (1, 0)])


LIMIT = pltpu.CompilerParams(vmem_limit_bytes=12 << 20)
EARLY = int(2e9)
IN = pl.BlockSpec(memory_space=VM)
HBM = pl.BlockSpec(memory_space=pltpu.HBM)


def kept(*values):
    return [pltpu.with_memory_space_constraint(v, VM) for v in values]


def roles():
    c, x, z = lax.axis_index("c"), lax.axis_index("x"), lax.axis_index("z")
    return c, jnp.where(c == 0, x, z), jnp.where(c == 0, z, x)


def spread_scales(s_ref, wide_ref):
    row = lax.broadcasted_iota(jnp.int32, (16, 256), 0)
    col = lax.broadcasted_iota(jnp.int32, (16, 256), 1)
    spread = jnp.where(col // 16 == row, 1.0, 0.0).astype(BF)
    wide_ref[...] = lax.dot_general(
        s_ref[...], spread, (((0,), (0,)), ((), ())), preferred_element_type=F32
    )


def scale_into(outs, w_ref, s_ref, narrow_ref, wide_ref, sems):
    c, first, _ = roles()
    scales = pltpu.make_async_copy(s_ref, narrow_ref, sems.at[16])
    scales.start()
    copies = []
    for j, (k, o_ref) in enumerate(outs):
        p = (first + k) & 3
        for i in range(4):
            z, x = c * p + (1 - c) * i, c * i + (1 - c) * p
            copy = pltpu.make_async_copy(
                w_ref.at[z, :, x], o_ref.at[pl.ds(2 * i, 2)], sems.at[j * 4 + i]
            )
            copy.start()
            copies.append((copy, o_ref, i, z, x))
    scales.wait()
    spread_scales(narrow_ref, wide_ref)
    for copy, o_ref, i, z, x in copies:
        copy.wait()
        for yl in range(2):
            r = pl.multiple_of((z * 8 + yl * 4 + x) * 16, 16)
            s = wide_ref[pl.ds(r, 16), :]
            w = o_ref[2 * i + yl].astype(F32).reshape(16, 16, 256)
            o_ref[2 * i + yl] = (w * s[:, None, :]).reshape(256, 256).astype(BF)


def scale_body(w_ref, s_ref, *refs):
    outs, scratch = refs[:4], refs[4:]
    scale_into([(k, outs[k]) for k in (1, 3, 2, 0)], w_ref, s_ref, *scratch)


def scaled_rows(w5, scales_t):
    return pl.pallas_call(
        scale_body,
        out_shape=[VM((8, 256, 256), BF)] * 4,
        in_specs=[HBM, HBM],
        out_specs=[IN] * 4,
        scratch_shapes=[VM((16, 512), BF), VM((512, 256), F32), pltpu.SemaphoreType.DMA((17,))],
        compiler_params=LIMIT,
        name="scale",
    )(w5, scales_t)


def packed_body(g_ref, h_ref, o_ref):
    o_ref[0] = g_ref[...]
    h = h_ref[...].reshape(128, 1024)
    for n in range(4):
        o_ref[1 + n] = h[:, n * 256 : (n + 1) * 256]


def packed(grad_out, hidden):
    return pl.pallas_call(
        packed_body,
        out_shape=VM((5, 128, 256), BF),
        in_specs=[IN] * 2,
        out_specs=IN,
        compiler_params=LIMIT,
        name="packed",
    )(grad_out, hidden)


def tokens_body(p0, p1, p2, p3, g_ref, h_ref):
    n = lax.axis_index("yh") * 2 + lax.axis_index("c")
    for r, p in enumerate((p0, p1, p2, p3)):
        t = n ^ r
        g_ref[t >> 1, pl.ds(pl.multiple_of((t & 1) * 128, 128), 128), :] = p[0]
        rows = pl.ds(pl.multiple_of(t * 128, 128), 128)
        for m in range(4):
            h_ref[rows, m * 256 : (m + 1) * 256] = p[1 + m]


def all_tokens(own):
    far = swap(own, "yh")
    pieces = [own, swap(own, "c"), far, swap(far, "c")]
    return pl.pallas_call(
        tokens_body,
        out_shape=[VM((2, 256, 256), BF), VM((512, 1024), BF)],
        in_specs=[IN] * 4,
        out_specs=[IN] * 2,
        compiler_params=LIMIT,
        name="tokens",
    )(*kept(*pieces))


def block_product(g, w, q):
    return lax.dot_general(
        g[...].reshape(512, 256),
        w[pl.ds(q, 2)].reshape(512, 256),
        (((1,), (1,)), ((), ())),
        preferred_element_type=F32,
    )


def early_body(r0, r3, g0, g3, acc):
    for q in range(4):
        acc[q] = block_product(g0, r0, 2 * q) + block_product(g3, r3, 2 * q)


def early_sums(*operands):
    return pl.pallas_call(
        early_body,
        out_shape=VM((4, 512, 512), F32),
        in_specs=[IN] * 4,
        out_specs=IN,
        compiler_params=LIMIT,
        cost_estimate=pl.CostEstimate(flops=EARLY, bytes_accessed=6 << 20, transcendentals=0),
        name="early",
    )(*kept(*operands))


def plane_body(g0, g1, g2, g3, keep, give):
    z, yh = lax.axis_index("z"), lax.axis_index("yh")
    g = (g0, g1, g2, g3)
    for k in range(4):

        @pl.when(((z - 2 * yh) & 3) == k)
        def _():
            give[...] = g[k][...]

        @pl.when(((z - 2 * yh - 1) & 3) == k)
        def _():
            keep[...] = g[k][...]


def plane_blocks(*grads):
    return pl.pallas_call(
        plane_body,
        out_shape=[VM((2, 256, 256), BF)] * 2,
        in_specs=[IN] * 4,
        out_specs=[IN] * 2,
        compiler_params=LIMIT,
        name="plane",
    )(*kept(*grads))


def partial_body(acc, r1, r2, g1, g2, *outs):
    _, _, second = roles()
    for k in (2, 1, 3, 0):
        q = (second + k) & 3
        total = acc[q] + block_product(g1, r1, 2 * q) + block_product(g2, r2, 2 * q)
        outs[k][...] = total.astype(outs[k].dtype)


def partial_sums(*operands):
    return pl.pallas_call(
        partial_body,
        out_shape=[VM((512, 512), F32)]
        + [VM((512, 512), BF)] * 3,
        in_specs=[IN] * 5,
        out_specs=[IN] * 4,
        compiler_params=LIMIT,
        name="partial",
    )(*kept(*operands))


def gather_body(a, b, c, d, o_ref):
    total = a[...] + b[...].astype(F32) + c[...].astype(F32) + d[...].astype(F32)
    total = total.astype(BF)
    for yl in range(2):
        for n in range(4):
            t = n * 128
            o_ref[yl * 4 + n] = total[t : t + 128, yl * 256 : (yl + 1) * 256]


def summed_blocks(parts):
    return pl.pallas_call(
        gather_body,
        out_shape=VM((8, 128, 256), BF),
        in_specs=[IN] * 4,
        out_specs=IN,
        compiler_params=LIMIT,
        name="summed",
    )(parts[0], *kept(*parts[1:]))


def finish_body(r_ref, o_ref):
    r = [(r_ref[n].astype(F32) + r_ref[4 + n].astype(F32)).astype(BF) for n in range(4)]
    o_ref[...] = jnp.concatenate(r, axis=1).reshape(128, 4, 256)


def finished(blocks):
    return pl.pallas_call(
        finish_body,
        out_shape=jax.ShapeDtypeStruct((128, 4, 256), BF),
        in_specs=[IN],
        out_specs=IN,
        compiler_params=LIMIT,
        name="finish",
    )(*kept(blocks))


def picked_body(a_ref, b_ref, o_ref):
    @pl.when(lax.axis_index("c") == 0)
    def _():
        o_ref[...] = a_ref[...]

    @pl.when(lax.axis_index("c") == 1)
    def _():
        o_ref[...] = b_ref[...]


def picked(for_core_0, for_core_1):
    return pl.pallas_call(
        picked_body,
        out_shape=VM((2, 256, 256), BF),
        in_specs=[IN] * 2,
        out_specs=IN,
        compiler_params=LIMIT,
        name="picked",
    )(for_core_0, for_core_1)


def paired_body(a_ref, b_ref, o_ref):
    o_ref[0:2] = a_ref[...]
    o_ref[2:4] = b_ref[...]


def paired(a, b):
    return pl.pallas_call(
        paired_body,
        out_shape=VM((4, 256, 256), BF),
        in_specs=[IN] * 2,
        out_specs=IN,
        compiler_params=LIMIT,
        name="paired",
    )(*kept(a, b))


def outer_into(blocks, h_ref, o_ref, buf, sems):
    x = lax.axis_index("x")
    copies = []
    for i, (yl, k, g) in enumerate(blocks):
        r = pl.multiple_of((yl * 4 + ((x - k) & 3)) * 256, 256)
        p = lax.dot_general(
            g[...].reshape(512, 256),
            h_ref[...],
            (((0,), (0,)), ((), ())),
            preferred_element_type=F32,
        )
        buf[i] = p.astype(BF).reshape(256, 4, 256)
        copy = pltpu.make_async_copy(buf.at[i], o_ref.at[pl.ds(r, 256)], sems.at[i])
        copy.start()
        copies.append(copy)
    for copy in copies:
        copy.wait()


def first_half_body(h_ref, seed, other, back, back_other, *refs):
    yl, c = lax.axis_index("yl"), lax.axis_index("c")
    k = 3 - 2 * c
    blocks = [(yl, 0, seed), (1 - yl, 0, other), (yl, k, back), (1 - yl, k, back_other)]
    outer_into(blocks, h_ref, *refs)


def second_half_body(o_in, h_ref, ahead, far, *refs):
    yl, c = lax.axis_index("yl"), lax.axis_index("c")
    blocks = []
    for k, ref in ((1 + 2 * c, ahead), (2, far)):
        blocks += [(yl, k, ref.at[0:2]), (1 - yl, k, ref.at[2:4])]
    outer_into(blocks, h_ref, *refs)


def outer_half(body, name, operands, so_far=None):
    aliased = so_far is not None
    return pl.pallas_call(
        body,
        out_shape=jax.ShapeDtypeStruct((2048, 4, 256), BF),
        in_specs=[HBM] * aliased + [IN] * len(operands),
        out_specs=HBM,
        scratch_shapes=[VM((4, 256, 4, 256), BF), pltpu.SemaphoreType.DMA((4,))],
        input_output_aliases={0: 0} if aliased else {},
        compiler_params=LIMIT,
        cost_estimate=pl.CostEstimate(flops=int(2e9), bytes_accessed=5 << 20, transcendentals=0),
        name=name,
    )(*([so_far] if aliased else []), *kept(*operands))


def along_x(value, forward_core):
    pairs = []
    for x in range(4):
        for c in range(2):
            k = 1 if c == forward_core else 3
            pairs.append((x * 2 + c, (x + k) % 4 * 2 + c))
    return lax.ppermute(value, ("x", "c"), pairs)


def per_device(hidden, grad_out, weight_base, block_scale):
    w5 = pltpu.with_memory_space_constraint(weight_base.reshape(4, 2, 4, 256, 256), pltpu.HBM)
    scales_t = pltpu.with_memory_space_constraint(block_scale.T, pltpu.HBM)

    sent = scaled_rows(w5, scales_t)
    r0 = sent[0]
    r1, r2, r3 = [shift(sent[k], first_axis_steps(k)) for k in (1, 2, 3)]
    grad_out, hidden, _ = lax.optimization_barrier((grad_out, hidden, r0))
    g0, h = all_tokens(packed(grad_out, hidden))
    g2, g3 = [shift(g0, first_axis_steps(k)) for k in (2, 3)]
    later, r1 = lax.optimization_barrier((g0, r1))
    g1 = shift(later, first_axis_steps(1))

    acc = early_sums(r0, r3, g0, g3)
    plane, acc = lax.optimization_barrier(((g0, g1, g2, g3), acc))
    keep, give = plane_blocks(*plane)
    acc, keep, give = lax.optimization_barrier((acc, keep, give))
    sums = partial_sums(acc, r1, r2, g1, g2)
    parts = [sums[0]] + [None] * 3
    for k in (1, 3, 2):
        parts[k] = shift(sums[k], second_axis_steps(k))
    seed = picked(lax.ppermute(give, "c", [(1, 0)]), keep)
    other = swap(seed, "yl")
    both = paired(seed, other)
    back = along_x(seed, 1)
    ahead = along_x(both, 0)
    far = lax.ppermute(both, "x", [(i, (i + 2) % 4) for i in range(4)])
    back, parts[0] = lax.optimization_barrier((back, parts[0]))
    back_other = swap(back, "yl")

    blocks = summed_blocks(parts)
    blocks = lax.all_to_all(blocks, ("yl", "yh", "c"), 0, 0, tiled=True)
    grad_hidden = finished(blocks)
    half = outer_half(first_half_body, "first_half", (h, seed, other, back, back_other))
    grad_weight = outer_half(second_half_body, "second_half", (h, ahead, far), half)
    return grad_hidden, grad_weight


def solution(mesh):
    fine = Mesh(mesh.devices.reshape(4, 2, 4, 2, 2), ("z", "yl", "x", "yh", "c"))
    narrow, wide = ("yh", "c"), ("z", "yl", "x")
    return jax.shard_map(
        per_device,
        mesh=fine,
        in_specs=(
            P(narrow, None, wide),
            P(narrow, wide),
            P(narrow, wide),
            P(narrow, wide),
        ),
        out_specs=(P(narrow, None, wide), P(narrow, None, wide)),
        check_vma=False,
    )
```

```python
import functools

import jax
import jax.numpy as jnp
from jax import lax
from jax.experimental import pallas as pl
from jax.experimental.pallas import tpu as pltpu
from jax.sharding import Mesh, PartitionSpec as P

BF = jnp.bfloat16
F32 = jnp.float32
VM = pltpu.VMEM


def first_axis_steps(k):
    pairs = []
    for z in range(4):
        for x in range(4):
            pairs.append(((z * 4 + x) * 2, (z * 4 + (x + k) % 4) * 2))
            pairs.append(((z * 4 + x) * 2 + 1, (((z + k) % 4) * 4 + x) * 2 + 1))
    return pairs


def second_axis_steps(k):
    pairs = []
    for z in range(4):
        for x in range(4):
            pairs.append(((z * 4 + x) * 2, (((z + k) % 4) * 4 + x) * 2))
            pairs.append(((z * 4 + x) * 2 + 1, (z * 4 + (x + k) % 4) * 2 + 1))
    return pairs


def shift(value, pairs):
    return lax.ppermute(value, ("z", "x", "c"), pairs)


def swap(value, axis):
    return lax.ppermute(value, axis, [(0, 1), (1, 0)])


LIMIT = pltpu.CompilerParams(vmem_limit_bytes=12 << 20)
EARLY = int(2e9)
IN = pl.BlockSpec(memory_space=VM)
HBM = pl.BlockSpec(memory_space=pltpu.HBM)


def kept(*values):
    return [pltpu.with_memory_space_constraint(v, VM) for v in values]


def roles():
    c, x, z = lax.axis_index("c"), lax.axis_index("x"), lax.axis_index("z")
    return c, jnp.where(c == 0, x, z), jnp.where(c == 0, z, x)


def spread_scales(s_ref, wide_ref):
    row = lax.broadcasted_iota(jnp.int32, (16, 256), 0)
    col = lax.broadcasted_iota(jnp.int32, (16, 256), 1)
    spread = jnp.where(col // 16 == row, 1.0, 0.0).astype(BF)
    wide_ref[...] = lax.dot_general(
        s_ref[...], spread, (((0,), (0,)), ((), ())), preferred_element_type=F32
    )


def scale_into(outs, w_ref, s_ref, narrow_ref, wide_ref, sems):
    c, first, _ = roles()
    scales = pltpu.make_async_copy(s_ref, narrow_ref, sems.at[16])
    scales.start()
    copies = []
    for j, (k, o_ref) in enumerate(outs):
        p = (first + k) & 3
        for i in range(4):
            z, x = c * p + (1 - c) * i, c * i + (1 - c) * p
            copy = pltpu.make_async_copy(
                w_ref.at[z, :, x], o_ref.at[pl.ds(2 * i, 2)], sems.at[j * 4 + i]
            )
            copy.start()
            copies.append((copy, o_ref, i, z, x))
    scales.wait()
    spread_scales(narrow_ref, wide_ref)
    for copy, o_ref, i, z, x in copies:
        copy.wait()
        for yl in range(2):
            r = pl.multiple_of((z * 8 + yl * 4 + x) * 16, 16)
            s = wide_ref[pl.ds(r, 16), :]
            w = o_ref[2 * i + yl].astype(F32).reshape(16, 16, 256)
            o_ref[2 * i + yl] = (w * s[:, None, :]).reshape(256, 256).astype(BF)


def scale_body(w_ref, s_ref, *refs):
    outs, scratch = refs[:4], refs[4:]
    scale_into([(k, outs[k]) for k in (1, 3, 2, 0)], w_ref, s_ref, *scratch)


def scaled_rows(w5, scales_t):
    return pl.pallas_call(
        scale_body,
        out_shape=[VM((8, 256, 256), BF)] * 4,
        in_specs=[HBM, HBM],
        out_specs=[IN] * 4,
        scratch_shapes=[VM((16, 512), BF), VM((512, 256), F32), pltpu.SemaphoreType.DMA((17,))],
        compiler_params=LIMIT,
        name="scale",
    )(w5, scales_t)


def packed_body(g_ref, h_ref, o_ref):
    o_ref[0] = g_ref[...]
    h = h_ref[...].reshape(128, 1024)
    for n in range(4):
        o_ref[1 + n] = h[:, n * 256 : (n + 1) * 256]


def packed(grad_out, hidden):
    return pl.pallas_call(
        packed_body,
        out_shape=VM((5, 128, 256), BF),
        in_specs=[IN] * 2,
        out_specs=IN,
        compiler_params=LIMIT,
        name="packed",
    )(grad_out, hidden)


def tokens_body(p0, p1, p2, p3, g_ref, h_ref):
    n = lax.axis_index("yh") * 2 + lax.axis_index("c")
    for r, p in enumerate((p0, p1, p2, p3)):
        t = n ^ r
        g_ref[t >> 1, pl.ds(pl.multiple_of((t & 1) * 128, 128), 128), :] = p[0]
        rows = pl.ds(pl.multiple_of(t * 128, 128), 128)
        for m in range(4):
            h_ref[rows, m * 256 : (m + 1) * 256] = p[1 + m]


def all_tokens(own):
    far = swap(own, "yh")
    pieces = [own, swap(own, "c"), far, swap(far, "c")]
    return pl.pallas_call(
        tokens_body,
        out_shape=[VM((2, 256, 256), BF), VM((512, 1024), BF)],
        in_specs=[IN] * 4,
        out_specs=[IN] * 2,
        compiler_params=LIMIT,
        name="tokens",
    )(*kept(*pieces))


def block_product(g, w, q):
    return lax.dot_general(
        g[...].reshape(512, 256),
        w[pl.ds(q, 2)].reshape(512, 256),
        (((1,), (1,)), ((), ())),
        preferred_element_type=F32,
    )


def early_body(r0, r3, g0, g3, acc):
    for q in range(4):
        acc[q] = block_product(g0, r0, 2 * q) + block_product(g3, r3, 2 * q)


def early_sums(*operands):
    return pl.pallas_call(
        early_body,
        out_shape=VM((4, 512, 512), F32),
        in_specs=[IN] * 4,
        out_specs=IN,
        compiler_params=LIMIT,
        cost_estimate=pl.CostEstimate(flops=EARLY, bytes_accessed=6 << 20, transcendentals=0),
        name="early",
    )(*kept(*operands))


def plane_body(g0, g1, g2, g3, keep, give):
    z, yh = lax.axis_index("z"), lax.axis_index("yh")
    g = (g0, g1, g2, g3)
    for k in range(4):

        @pl.when(((z - 2 * yh) & 3) == k)
        def _():
            give[...] = g[k][...]

        @pl.when(((z - 2 * yh - 1) & 3) == k)
        def _():
            keep[...] = g[k][...]


def plane_blocks(*grads):
    return pl.pallas_call(
        plane_body,
        out_shape=[VM((2, 256, 256), BF)] * 2,
        in_specs=[IN] * 4,
        out_specs=[IN] * 2,
        compiler_params=LIMIT,
        name="plane",
    )(*kept(*grads))


def partial_body(acc, r1, r2, g1, g2, *outs):
    _, _, second = roles()
    for k in (2, 1, 3, 0):
        q = (second + k) & 3
        total = acc[q] + block_product(g1, r1, 2 * q) + block_product(g2, r2, 2 * q)
        outs[k][...] = total.astype(outs[k].dtype)


def partial_sums(*operands):
    return pl.pallas_call(
        partial_body,
        out_shape=[VM((512, 512), F32)]
        + [VM((512, 512), BF)] * 3,
        in_specs=[IN] * 5,
        out_specs=[IN] * 4,
        compiler_params=LIMIT,
        name="partial",
    )(*kept(*operands))


def gather_body(a, b, c, d, o_ref):
    total = a[...] + b[...].astype(F32) + c[...].astype(F32) + d[...].astype(F32)
    total = total.astype(BF)
    for yl in range(2):
        for n in range(4):
            t = n * 128
            o_ref[yl * 4 + n] = total[t : t + 128, yl * 256 : (yl + 1) * 256]


def summed_blocks(parts):
    return pl.pallas_call(
        gather_body,
        out_shape=VM((8, 128, 256), BF),
        in_specs=[IN] * 4,
        out_specs=IN,
        compiler_params=LIMIT,
        name="summed",
    )(parts[0], *kept(*parts[1:]))


def finish_body(r_ref, o_ref):
    r = [(r_ref[n].astype(F32) + r_ref[4 + n].astype(F32)).astype(BF) for n in range(4)]
    o_ref[...] = jnp.concatenate(r, axis=1).reshape(128, 4, 256)


def finished(blocks):
    return pl.pallas_call(
        finish_body,
        out_shape=jax.ShapeDtypeStruct((128, 4, 256), BF),
        in_specs=[IN],
        out_specs=IN,
        compiler_params=LIMIT,
        name="finish",
    )(*kept(blocks))


def picked_body(a_ref, b_ref, o_ref):
    @pl.when(lax.axis_index("c") == 0)
    def _():
        o_ref[...] = a_ref[...]

    @pl.when(lax.axis_index("c") == 1)
    def _():
        o_ref[...] = b_ref[...]


def picked(for_core_0, for_core_1):
    return pl.pallas_call(
        picked_body,
        out_shape=VM((2, 256, 256), BF),
        in_specs=[IN] * 2,
        out_specs=IN,
        compiler_params=LIMIT,
        name="picked",
    )(for_core_0, for_core_1)


def paired_body(a_ref, b_ref, o_ref):
    o_ref[0:2] = a_ref[...]
    o_ref[2:4] = b_ref[...]


def paired(a, b):
    return pl.pallas_call(
        paired_body,
        out_shape=VM((4, 256, 256), BF),
        in_specs=[IN] * 2,
        out_specs=IN,
        compiler_params=LIMIT,
        name="paired",
    )(*kept(a, b))


def outer_into(blocks, h_ref, o_ref, buf, sems):
    x = lax.axis_index("x")
    copies = []
    for i, (yl, k, g) in enumerate(blocks):
        r = pl.multiple_of((yl * 4 + ((x - k) & 3)) * 256, 256)
        p = lax.dot_general(
            g[...].reshape(512, 256),
            h_ref[...],
            (((0,), (0,)), ((), ())),
            preferred_element_type=F32,
        )
        buf[i] = p.astype(BF).reshape(256, 4, 256)
        copy = pltpu.make_async_copy(buf.at[i], o_ref.at[pl.ds(r, 256)], sems.at[i])
        copy.start()
        copies.append(copy)
    for copy in copies:
        copy.wait()


def first_half_body(h_ref, seed, other, up, *refs):
    yl = lax.axis_index("yl")
    blocks = [(yl, 0, seed), (1 - yl, 0, other), (yl, 1, up.at[0:2]), (1 - yl, 1, up.at[2:4])]
    outer_into(blocks, h_ref, *refs)


def second_half_body(o_in, h_ref, far, down, *refs):
    yl = lax.axis_index("yl")
    blocks = []
    for k, ref in ((3, down), (2, far)):
        blocks += [(yl, k, ref.at[0:2]), (1 - yl, k, ref.at[2:4])]
    outer_into(blocks, h_ref, *refs)


def outer_half(body, name, operands, so_far=None):
    aliased = so_far is not None
    return pl.pallas_call(
        body,
        out_shape=jax.ShapeDtypeStruct((2048, 4, 256), BF),
        in_specs=[HBM] * aliased + [IN] * len(operands),
        out_specs=HBM,
        scratch_shapes=[VM((4, 256, 4, 256), BF), pltpu.SemaphoreType.DMA((4,))],
        input_output_aliases={0: 0} if aliased else {},
        compiler_params=LIMIT,
        cost_estimate=pl.CostEstimate(flops=int(1e6), bytes_accessed=1 << 10, transcendentals=0),
        name=name,
    )(*([so_far] if aliased else []), *kept(*operands))


def per_device(hidden, grad_out, weight_base, block_scale):
    w5 = pltpu.with_memory_space_constraint(weight_base.reshape(4, 2, 4, 256, 256), pltpu.HBM)
    scales_t = pltpu.with_memory_space_constraint(block_scale.T, pltpu.HBM)

    sent = scaled_rows(w5, scales_t)
    r0 = sent[0]
    r1, r2, r3 = [shift(sent[k], first_axis_steps(k)) for k in (1, 2, 3)]
    grad_out, hidden, _ = lax.optimization_barrier((grad_out, hidden, r0))
    g0, h = all_tokens(packed(grad_out, hidden))
    g2, g3 = [shift(g0, first_axis_steps(k)) for k in (2, 3)]
    later, r1 = lax.optimization_barrier((g0, r1))
    g1 = shift(later, first_axis_steps(1))

    acc = early_sums(r0, r3, g0, g3)
    plane, acc = lax.optimization_barrier(((g0, g1, g2, g3), acc))
    keep, give = plane_blocks(*plane)
    acc, keep, give = lax.optimization_barrier((acc, keep, give))
    sums = partial_sums(acc, r1, r2, g1, g2)
    parts = [sums[0]] + [None] * 3
    for k in (1, 3, 2):
        parts[k] = shift(sums[k], second_axis_steps(k))
    seed = picked(lax.ppermute(give, "c", [(1, 0)]), keep)
    other = swap(seed, "yl")
    both = paired(seed, other)
    up, far, down = [
        lax.ppermute(both, "x", [(i, (i + k) % 4) for i in range(4)]) for k in (1, 2, 3)
    ]

    blocks = summed_blocks(parts)
    blocks = lax.all_to_all(blocks, ("yl", "yh", "c"), 0, 0, tiled=True)
    half = outer_half(first_half_body, "first_half", (h, seed, other, up))
    grad_weight = outer_half(second_half_body, "second_half", (h, far, down), half)
    blocks, grad_weight = lax.optimization_barrier((blocks, grad_weight))
    return finished(blocks), grad_weight


def solution(mesh):
    fine = Mesh(mesh.devices.reshape(4, 2, 4, 2, 2), ("z", "yl", "x", "yh", "c"))
    narrow, wide = ("yh", "c"), ("z", "yl", "x")
    return jax.shard_map(
        per_device,
        mesh=fine,
        in_specs=(
            P(narrow, None, wide),
            P(narrow, wide),
            P(narrow, wide),
            P(narrow, wide),
        ),
        out_specs=(P(narrow, None, wide), P(narrow, None, wide)),
        check_vma=False,
    )
```

```python
import functools

import jax
import jax.numpy as jnp
from jax import lax
from jax.experimental import pallas as pl
from jax.experimental.pallas import tpu as pltpu
from jax.sharding import Mesh, PartitionSpec as P

BF = jnp.bfloat16
F32 = jnp.float32
VM = pltpu.VMEM


def first_axis_steps(k):
    pairs = []
    for z in range(4):
        for x in range(4):
            pairs.append(((z * 4 + x) * 2, (z * 4 + (x + k) % 4) * 2))
            pairs.append(((z * 4 + x) * 2 + 1, (((z + k) % 4) * 4 + x) * 2 + 1))
    return pairs


def second_axis_steps(k):
    pairs = []
    for z in range(4):
        for x in range(4):
            pairs.append(((z * 4 + x) * 2, (((z + k) % 4) * 4 + x) * 2))
            pairs.append(((z * 4 + x) * 2 + 1, (z * 4 + (x + k) % 4) * 2 + 1))
    return pairs


def shift(value, pairs):
    return lax.ppermute(value, ("z", "x", "c"), pairs)


def swap(value, axis):
    return lax.ppermute(value, axis, [(0, 1), (1, 0)])


LIMIT = pltpu.CompilerParams(vmem_limit_bytes=12 << 20)
EARLY = int(2e9)
IN = pl.BlockSpec(memory_space=VM)
HBM = pl.BlockSpec(memory_space=pltpu.HBM)


def kept(*values):
    return [pltpu.with_memory_space_constraint(v, VM) for v in values]


def roles():
    c, x, z = lax.axis_index("c"), lax.axis_index("x"), lax.axis_index("z")
    return c, jnp.where(c == 0, x, z), jnp.where(c == 0, z, x)


def spread_scales(s_ref, wide_ref):
    row = lax.broadcasted_iota(jnp.int32, (16, 256), 0)
    col = lax.broadcasted_iota(jnp.int32, (16, 256), 1)
    spread = jnp.where(col // 16 == row, 1.0, 0.0).astype(BF)
    wide_ref[...] = lax.dot_general(
        s_ref[...], spread, (((0,), (0,)), ((), ())), preferred_element_type=F32
    )


def scale_into(outs, w_ref, s_ref, narrow_ref, wide_ref, sems):
    c, first, _ = roles()
    scales = pltpu.make_async_copy(s_ref, narrow_ref, sems.at[16])
    scales.start()
    copies = []
    for j, (k, o_ref) in enumerate(outs):
        p = (first + k) & 3
        for i in range(4):
            z, x = c * p + (1 - c) * i, c * i + (1 - c) * p
            copy = pltpu.make_async_copy(
                w_ref.at[z, :, x], o_ref.at[pl.ds(2 * i, 2)], sems.at[j * 4 + i]
            )
            copy.start()
            copies.append((copy, o_ref, i, z, x))
    scales.wait()
    spread_scales(narrow_ref, wide_ref)
    for copy, o_ref, i, z, x in copies:
        copy.wait()
        for yl in range(2):
            r = pl.multiple_of((z * 8 + yl * 4 + x) * 16, 16)
            s = wide_ref[pl.ds(r, 16), :]
            w = o_ref[2 * i + yl].astype(F32).reshape(16, 16, 256)
            o_ref[2 * i + yl] = (w * s[:, None, :]).reshape(256, 256).astype(BF)


def scale_body(w_ref, s_ref, *refs):
    outs, scratch = refs[:4], refs[4:]
    scale_into([(k, outs[k]) for k in (1, 3, 2, 0)], w_ref, s_ref, *scratch)


def scaled_rows(w5, scales_t):
    return pl.pallas_call(
        scale_body,
        out_shape=[VM((8, 256, 256), BF)] * 4,
        in_specs=[HBM, HBM],
        out_specs=[IN] * 4,
        scratch_shapes=[VM((16, 512), BF), VM((512, 256), F32), pltpu.SemaphoreType.DMA((17,))],
        compiler_params=LIMIT,
        name="scale",
    )(w5, scales_t)


def packed_body(g_ref, h_ref, o_ref):
    o_ref[0] = g_ref[...]
    h = h_ref[...].reshape(128, 1024)
    for n in range(4):
        o_ref[1 + n] = h[:, n * 256 : (n + 1) * 256]


def packed(grad_out, hidden):
    return pl.pallas_call(
        packed_body,
        out_shape=VM((5, 128, 256), BF),
        in_specs=[IN] * 2,
        out_specs=IN,
        compiler_params=LIMIT,
        name="packed",
    )(grad_out, hidden)


def tokens_body(p0, p1, p2, p3, g_ref, h_ref):
    n = lax.axis_index("yh") * 2 + lax.axis_index("c")
    for r, p in enumerate((p0, p1, p2, p3)):
        t = n ^ r
        g_ref[t >> 1, pl.ds(pl.multiple_of((t & 1) * 128, 128), 128), :] = p[0]
        rows = pl.ds(pl.multiple_of(t * 128, 128), 128)
        for m in range(4):
            h_ref[rows, m * 256 : (m + 1) * 256] = p[1 + m]


def all_tokens(own):
    far = swap(own, "yh")
    pieces = [own, swap(own, "c"), far, swap(far, "c")]
    return pl.pallas_call(
        tokens_body,
        out_shape=[VM((2, 256, 256), BF), VM((512, 1024), BF)],
        in_specs=[IN] * 4,
        out_specs=[IN] * 2,
        compiler_params=LIMIT,
        name="tokens",
    )(*kept(*pieces))


def block_product(g, w, q):
    return lax.dot_general(
        g[...].reshape(512, 256),
        w[pl.ds(q, 2)].reshape(512, 256),
        (((1,), (1,)), ((), ())),
        preferred_element_type=F32,
    )


def early_body(r0, r3, g0, g3, acc):
    for q in range(4):
        acc[q] = block_product(g0, r0, 2 * q) + block_product(g3, r3, 2 * q)


def early_sums(*operands):
    return pl.pallas_call(
        early_body,
        out_shape=VM((4, 512, 512), F32),
        in_specs=[IN] * 4,
        out_specs=IN,
        compiler_params=LIMIT,
        cost_estimate=pl.CostEstimate(flops=EARLY, bytes_accessed=6 << 20, transcendentals=0),
        name="early",
    )(*kept(*operands))


def plane_body(g0, g1, g2, g3, keep, give):
    z, yh = lax.axis_index("z"), lax.axis_index("yh")
    g = (g0, g1, g2, g3)
    for k in range(4):

        @pl.when(((z - 2 * yh) & 3) == k)
        def _():
            give[...] = g[k][...]

        @pl.when(((z - 2 * yh - 1) & 3) == k)
        def _():
            keep[...] = g[k][...]


def plane_blocks(*grads):
    return pl.pallas_call(
        plane_body,
        out_shape=[VM((2, 256, 256), BF)] * 2,
        in_specs=[IN] * 4,
        out_specs=[IN] * 2,
        compiler_params=LIMIT,
        name="plane",
    )(*kept(*grads))


def partial_body(acc, r1, r2, g1, g2, *outs):
    _, _, second = roles()
    for k in (2, 1, 3, 0):
        q = (second + k) & 3
        total = acc[q] + block_product(g1, r1, 2 * q) + block_product(g2, r2, 2 * q)
        outs[k][...] = total.astype(outs[k].dtype)


def partial_sums(*operands):
    return pl.pallas_call(
        partial_body,
        out_shape=[VM((512, 512), F32)]
        + [VM((512, 512), BF)] * 3,
        in_specs=[IN] * 5,
        out_specs=[IN] * 4,
        compiler_params=LIMIT,
        name="partial",
    )(*kept(*operands))


def gather_body(a, b, c, d, o_ref):
    total = a[...] + b[...].astype(F32) + c[...].astype(F32) + d[...].astype(F32)
    total = total.astype(BF)
    for yl in range(2):
        for n in range(4):
            t = n * 128
            o_ref[yl * 4 + n] = total[t : t + 128, yl * 256 : (yl + 1) * 256]


def summed_blocks(parts):
    return pl.pallas_call(
        gather_body,
        out_shape=VM((8, 128, 256), BF),
        in_specs=[IN] * 4,
        out_specs=IN,
        compiler_params=LIMIT,
        name="summed",
    )(parts[0], *kept(*parts[1:]))


def finish_body(r_ref, o_ref):
    r = [(r_ref[n].astype(F32) + r_ref[4 + n].astype(F32)).astype(BF) for n in range(4)]
    o_ref[...] = jnp.concatenate(r, axis=1).reshape(128, 4, 256)


def finished(blocks):
    return pl.pallas_call(
        finish_body,
        out_shape=jax.ShapeDtypeStruct((128, 4, 256), BF),
        in_specs=[IN],
        out_specs=IN,
        compiler_params=LIMIT,
        name="finish",
    )(*kept(blocks))


def picked_body(a_ref, b_ref, o_ref):
    @pl.when(lax.axis_index("c") == 0)
    def _():
        o_ref[...] = a_ref[...]

    @pl.when(lax.axis_index("c") == 1)
    def _():
        o_ref[...] = b_ref[...]


def picked(for_core_0, for_core_1):
    return pl.pallas_call(
        picked_body,
        out_shape=VM((2, 256, 256), BF),
        in_specs=[IN] * 2,
        out_specs=IN,
        compiler_params=LIMIT,
        name="picked",
    )(for_core_0, for_core_1)


def paired_body(a_ref, b_ref, o_ref, one_ref):
    o_ref[0:2] = a_ref[...]
    o_ref[2:4] = b_ref[...]
    odd = lax.axis_index("z") & 1
    one_ref[...] = o_ref[pl.ds(2 * odd, 2)]


def paired(a, b):
    return pl.pallas_call(
        paired_body,
        out_shape=[VM((4, 256, 256), BF), VM((2, 256, 256), BF)],
        in_specs=[IN] * 2,
        out_specs=[IN] * 2,
        compiler_params=LIMIT,
        cost_estimate=pl.CostEstimate(flops=int(5e9), bytes_accessed=1 << 20, transcendentals=0),
        name="paired",
    )(*kept(a, b))


def z_pairs(value):
    pairs = []
    for z in range(4):
        pairs.append((z * 2, (z ^ 1) * 2))
        pairs.append((z * 2 + 1, (z + 1 if z & 1 else z + 3) % 4 * 2 + 1))
    return lax.ppermute(value, ("z", "c"), pairs)


def outer_into(blocks, h_ref, o_ref, buf, sems):
    x = lax.axis_index("x")
    copies = []
    for i, (yl, k, g) in enumerate(blocks):
        r = pl.multiple_of((yl * 4 + ((x - k) & 3)) * 256, 256)
        p = lax.dot_general(
            g[...].reshape(512, 256),
            h_ref[...],
            (((0,), (0,)), ((), ())),
            preferred_element_type=F32,
        )
        buf[i] = p.astype(BF).reshape(256, 4, 256)
        copy = pltpu.make_async_copy(buf.at[i], o_ref.at[pl.ds(r, 256)], sems.at[i])
        copy.start()
        copies.append(copy)
    for copy in copies:
        copy.wait()


def first_half_body(h_ref, seed, other, far, far_pair, *refs):
    yl = lax.axis_index("yl")
    here = yl ^ (lax.axis_index("z") & 1)
    blocks = [(yl, 0, seed), (1 - yl, 0, other), (here, 2, far), (1 - here, 2, far_pair)]
    outer_into(blocks, h_ref, *refs)


def second_half_body(o_in, h_ref, up, down, *refs):
    yl = lax.axis_index("yl")
    blocks = []
    for k, ref in ((1, up), (3, down)):
        blocks += [(yl, k, ref.at[0:2]), (1 - yl, k, ref.at[2:4])]
    outer_into(blocks, h_ref, *refs)


def outer_half(body, name, operands, so_far=None):
    aliased = so_far is not None
    return pl.pallas_call(
        body,
        out_shape=jax.ShapeDtypeStruct((2048, 4, 256), BF),
        in_specs=[HBM] * aliased + [IN] * len(operands),
        out_specs=HBM,
        scratch_shapes=[VM((4, 256, 4, 256), BF), pltpu.SemaphoreType.DMA((4,))],
        input_output_aliases={0: 0} if aliased else {},
        compiler_params=LIMIT,
        cost_estimate=pl.CostEstimate(flops=int(1e6), bytes_accessed=1 << 10, transcendentals=0),
        name=name,
    )(*([so_far] if aliased else []), *kept(*operands))


def per_device(hidden, grad_out, weight_base, block_scale):
    w5 = pltpu.with_memory_space_constraint(weight_base.reshape(4, 2, 4, 256, 256), pltpu.HBM)
    scales_t = pltpu.with_memory_space_constraint(block_scale.T, pltpu.HBM)

    sent = scaled_rows(w5, scales_t)
    r0 = sent[0]
    r1, r2, r3 = [shift(sent[k], first_axis_steps(k)) for k in (1, 2, 3)]
    grad_out, hidden, _ = lax.optimization_barrier((grad_out, hidden, r0))
    g0, h = all_tokens(packed(grad_out, hidden))
    g2, g3 = [shift(g0, first_axis_steps(k)) for k in (2, 3)]
    later, r1 = lax.optimization_barrier((g0, r1))
    g1 = shift(later, first_axis_steps(1))

    acc = early_sums(r0, r3, g0, g3)
    plane, acc = lax.optimization_barrier(((g0, g1, g2, g3), acc))
    keep, give = plane_blocks(*plane)
    acc, keep, give = lax.optimization_barrier((acc, keep, give))
    sums = partial_sums(acc, r1, r2, g1, g2)
    seed = picked(lax.ppermute(give, "c", [(1, 0)]), keep)
    sums, seed = lax.optimization_barrier((sums, seed))
    other = swap(seed, "yl")
    parts = [sums[0]] + [None] * 3
    for k in (1, 3, 2):
        parts[k] = shift(sums[k], second_axis_steps(k))
    both, one = paired(seed, other)
    along_x = lambda value, k: lax.ppermute(value, "x", [(i, (i + k) % 4) for i in range(4)])
    far = along_x(one, 2)
    up, down = along_x(both, 1), along_x(both, 3)
    far_pair = z_pairs(far)

    blocks = summed_blocks(parts)
    blocks = lax.all_to_all(blocks, ("yl", "yh", "c"), 0, 0, tiled=True)
    half = outer_half(first_half_body, "first_half", (h, seed, other, far, far_pair))
    blocks, half = lax.optimization_barrier((blocks, half))
    grad_weight = outer_half(second_half_body, "second_half", (h, up, down), half)
    return finished(blocks), grad_weight


def solution(mesh):
    fine = Mesh(mesh.devices.reshape(4, 2, 4, 2, 2), ("z", "yl", "x", "yh", "c"))
    narrow, wide = ("yh", "c"), ("z", "yl", "x")
    return jax.shard_map(
        per_device,
        mesh=fine,
        in_specs=(
            P(narrow, None, wide),
            P(narrow, wide),
            P(narrow, wide),
            P(narrow, wide),
        ),
        out_specs=(P(narrow, None, wide), P(narrow, None, wide)),
        check_vma=False,
    )
```

```python
import functools

import jax
import jax.numpy as jnp
from jax import lax
from jax.experimental import pallas as pl
from jax.experimental.pallas import tpu as pltpu
from jax.sharding import Mesh, PartitionSpec as P

BF = jnp.bfloat16
F32 = jnp.float32
VM = pltpu.VMEM


def first_axis_steps(k):
    pairs = []
    for z in range(4):
        for x in range(4):
            pairs.append(((z * 4 + x) * 2, (z * 4 + (x + k) % 4) * 2))
            pairs.append(((z * 4 + x) * 2 + 1, (((z + k) % 4) * 4 + x) * 2 + 1))
    return pairs


def second_axis_steps(k):
    pairs = []
    for z in range(4):
        for x in range(4):
            pairs.append(((z * 4 + x) * 2, (((z + k) % 4) * 4 + x) * 2))
            pairs.append(((z * 4 + x) * 2 + 1, (z * 4 + (x + k) % 4) * 2 + 1))
    return pairs


def shift(value, pairs):
    return lax.ppermute(value, ("z", "x", "c"), pairs)


def swap(value, axis):
    return lax.ppermute(value, axis, [(0, 1), (1, 0)])


LIMIT = pltpu.CompilerParams(vmem_limit_bytes=12 << 20)
EARLY = int(2e9)
IN = pl.BlockSpec(memory_space=VM)
HBM = pl.BlockSpec(memory_space=pltpu.HBM)


def kept(*values):
    return [pltpu.with_memory_space_constraint(v, VM) for v in values]


def roles():
    c, x, z = lax.axis_index("c"), lax.axis_index("x"), lax.axis_index("z")
    return c, jnp.where(c == 0, x, z), jnp.where(c == 0, z, x)


def spread_scales(s_ref, wide_ref):
    row = lax.broadcasted_iota(jnp.int32, (16, 256), 0)
    col = lax.broadcasted_iota(jnp.int32, (16, 256), 1)
    spread = jnp.where(col // 16 == row, 1.0, 0.0).astype(BF)
    wide_ref[...] = lax.dot_general(
        s_ref[...], spread, (((0,), (0,)), ((), ())), preferred_element_type=F32
    )


def scale_into(outs, w_ref, s_ref, narrow_ref, wide_ref, sems):
    c, first, _ = roles()
    scales = pltpu.make_async_copy(s_ref, narrow_ref, sems.at[16])
    scales.start()
    copies = []
    for j, (k, o_ref) in enumerate(outs):
        p = (first + k) & 3
        for i in range(4):
            z, x = c * p + (1 - c) * i, c * i + (1 - c) * p
            copy = pltpu.make_async_copy(
                w_ref.at[z, :, x], o_ref.at[pl.ds(2 * i, 2)], sems.at[j * 4 + i]
            )
            copy.start()
            copies.append((copy, o_ref, i, z, x))
    scales.wait()
    spread_scales(narrow_ref, wide_ref)
    for copy, o_ref, i, z, x in copies:
        copy.wait()
        for yl in range(2):
            r = pl.multiple_of((z * 8 + yl * 4 + x) * 16, 16)
            s = wide_ref[pl.ds(r, 16), :]
            w = o_ref[2 * i + yl].astype(F32).reshape(16, 16, 256)
            o_ref[2 * i + yl] = (w * s[:, None, :]).reshape(256, 256).astype(BF)


def scale_body(w_ref, s_ref, *refs):
    outs, scratch = refs[:4], refs[4:]
    scale_into([(k, outs[k]) for k in (1, 3, 2, 0)], w_ref, s_ref, *scratch)


def scaled_rows(w5, scales_t):
    return pl.pallas_call(
        scale_body,
        out_shape=[VM((8, 256, 256), BF)] * 4,
        in_specs=[HBM, HBM],
        out_specs=[IN] * 4,
        scratch_shapes=[VM((16, 512), BF), VM((512, 256), F32), pltpu.SemaphoreType.DMA((17,))],
        compiler_params=LIMIT,
        name="scale",
    )(w5, scales_t)


def packed_body(g_ref, h_ref, o_ref):
    o_ref[0] = g_ref[...]
    h = h_ref[...].reshape(128, 1024)
    for n in range(4):
        o_ref[1 + n] = h[:, n * 256 : (n + 1) * 256]


def packed(grad_out, hidden):
    return pl.pallas_call(
        packed_body,
        out_shape=VM((5, 128, 256), BF),
        in_specs=[IN] * 2,
        out_specs=IN,
        compiler_params=LIMIT,
        name="packed",
    )(grad_out, hidden)


def tokens_body(p0, p1, p2, p3, g_ref, h_ref):
    n = lax.axis_index("yh") * 2 + lax.axis_index("c")
    for r, p in enumerate((p0, p1, p2, p3)):
        t = n ^ r
        g_ref[t >> 1, pl.ds(pl.multiple_of((t & 1) * 128, 128), 128), :] = p[0]
        rows = pl.ds(pl.multiple_of(t * 128, 128), 128)
        for m in range(4):
            h_ref[rows, m * 256 : (m + 1) * 256] = p[1 + m]


def all_tokens(own):
    far = swap(own, "yh")
    pieces = [own, swap(own, "c"), far, swap(far, "c")]
    return pl.pallas_call(
        tokens_body,
        out_shape=[VM((2, 256, 256), BF), VM((512, 1024), BF)],
        in_specs=[IN] * 4,
        out_specs=[IN] * 2,
        compiler_params=LIMIT,
        name="tokens",
    )(*kept(*pieces))


def block_product(g, w, q):
    return lax.dot_general(
        g[...].reshape(512, 256),
        w[pl.ds(q, 2)].reshape(512, 256),
        (((1,), (1,)), ((), ())),
        preferred_element_type=F32,
    )


def early_body(r0, r3, g0, g3, acc):
    for q in range(4):
        acc[q] = block_product(g0, r0, 2 * q) + block_product(g3, r3, 2 * q)


def early_sums(*operands):
    return pl.pallas_call(
        early_body,
        out_shape=VM((4, 512, 512), F32),
        in_specs=[IN] * 4,
        out_specs=IN,
        compiler_params=LIMIT,
        cost_estimate=pl.CostEstimate(flops=EARLY, bytes_accessed=6 << 20, transcendentals=0),
        name="early",
    )(*kept(*operands))


def plane_body(g0, g1, g2, g3, keep, give):
    z, yh = lax.axis_index("z"), lax.axis_index("yh")
    g = (g0, g1, g2, g3)
    for k in range(4):

        @pl.when(((z - 2 * yh) & 3) == k)
        def _():
            give[...] = g[k][...]

        @pl.when(((z - 2 * yh - 1) & 3) == k)
        def _():
            keep[...] = g[k][...]


def plane_blocks(*grads):
    return pl.pallas_call(
        plane_body,
        out_shape=[VM((2, 256, 256), BF)] * 2,
        in_specs=[IN] * 4,
        out_specs=[IN] * 2,
        compiler_params=LIMIT,
        name="plane",
    )(*kept(*grads))


def partial_body(acc, r1, r2, g1, g2, *outs):
    _, _, second = roles()
    for k in (2, 1, 3, 0):
        q = (second + k) & 3
        total = acc[q] + block_product(g1, r1, 2 * q) + block_product(g2, r2, 2 * q)
        outs[k][...] = total.astype(outs[k].dtype)


def partial_sums(*operands):
    return pl.pallas_call(
        partial_body,
        out_shape=[VM((512, 512), F32)]
        + [VM((512, 512), BF)] * 3,
        in_specs=[IN] * 5,
        out_specs=[IN] * 4,
        compiler_params=LIMIT,
        name="partial",
    )(*kept(*operands))


def gather_body(a, b, c, d, o_ref):
    total = a[...] + b[...].astype(F32) + c[...].astype(F32) + d[...].astype(F32)
    total = total.astype(BF)
    for yl in range(2):
        for n in range(4):
            t = n * 128
            o_ref[yl * 4 + n] = total[t : t + 128, yl * 256 : (yl + 1) * 256]


def summed_blocks(parts):
    return pl.pallas_call(
        gather_body,
        out_shape=VM((8, 128, 256), BF),
        in_specs=[IN] * 4,
        out_specs=IN,
        compiler_params=LIMIT,
        name="summed",
    )(parts[0], *kept(*parts[1:]))


def finish_body(r_ref, o_ref):
    r = [(r_ref[n].astype(F32) + r_ref[4 + n].astype(F32)).astype(BF) for n in range(4)]
    o_ref[...] = jnp.concatenate(r, axis=1).reshape(128, 4, 256)


def finished(blocks):
    return pl.pallas_call(
        finish_body,
        out_shape=jax.ShapeDtypeStruct((128, 4, 256), BF),
        in_specs=[IN],
        out_specs=IN,
        compiler_params=LIMIT,
        name="finish",
    )(*kept(blocks))


def picked_body(a_ref, b_ref, o_ref):
    @pl.when(lax.axis_index("c") == 0)
    def _():
        o_ref[...] = a_ref[...]

    @pl.when(lax.axis_index("c") == 1)
    def _():
        o_ref[...] = b_ref[...]


def picked(for_core_0, for_core_1):
    return pl.pallas_call(
        picked_body,
        out_shape=VM((2, 256, 256), BF),
        in_specs=[IN] * 2,
        out_specs=IN,
        compiler_params=LIMIT,
        name="picked",
    )(for_core_0, for_core_1)


def paired_body(a_ref, b_ref, o_ref, one_ref):
    o_ref[0:2] = a_ref[...]
    o_ref[2:4] = b_ref[...]
    odd = lax.axis_index("z") & 1
    one_ref[...] = o_ref[pl.ds(2 * odd, 2)]


def paired(a, b):
    return pl.pallas_call(
        paired_body,
        out_shape=[VM((4, 256, 256), BF), VM((2, 256, 256), BF)],
        in_specs=[IN] * 2,
        out_specs=[IN] * 2,
        compiler_params=LIMIT,
        cost_estimate=pl.CostEstimate(flops=int(5e9), bytes_accessed=1 << 20, transcendentals=0),
        name="paired",
    )(*kept(a, b))


def z_pairs(value):
    pairs = []
    for z in range(4):
        pairs.append((z * 2, (z ^ 1) * 2))
        pairs.append((z * 2 + 1, (z + 1 if z & 1 else z + 3) % 4 * 2 + 1))
    return lax.ppermute(value, ("z", "c"), pairs)


def outer_into(blocks, h_ref, o_ref, buf, sems):
    x = lax.axis_index("x")
    copies = []
    for i, (yl, k, g) in enumerate(blocks):
        r = pl.multiple_of((yl * 4 + ((x - k) & 3)) * 256, 256)
        p = lax.dot_general(
            g[...].reshape(512, 256),
            h_ref[...],
            (((0,), (0,)), ((), ())),
            preferred_element_type=F32,
        )
        buf[i] = p.astype(BF).reshape(256, 4, 256)
        copy = pltpu.make_async_copy(buf.at[i], o_ref.at[pl.ds(r, 256)], sems.at[i])
        copy.start()
        copies.append(copy)
    for copy in copies:
        copy.wait()


def first_half_body(h_ref, seed, other, far, far_pair, *refs):
    yl = lax.axis_index("yl")
    here = yl ^ (lax.axis_index("z") & 1)
    blocks = [(yl, 0, seed), (1 - yl, 0, other), (here, 2, far), (1 - here, 2, far_pair)]
    outer_into(blocks, h_ref, *refs)


def second_half_body(o_in, h_ref, up, down, *refs):
    yl = lax.axis_index("yl")
    blocks = []
    for k, ref in ((1, up), (3, down)):
        blocks += [(yl, k, ref.at[0:2]), (1 - yl, k, ref.at[2:4])]
    outer_into(blocks, h_ref, *refs)


def outer_half(body, name, operands, so_far=None, flops=int(1e6)):
    aliased = so_far is not None
    return pl.pallas_call(
        body,
        out_shape=jax.ShapeDtypeStruct((2048, 4, 256), BF),
        in_specs=[HBM] * aliased + [IN] * len(operands),
        out_specs=HBM,
        scratch_shapes=[VM((4, 256, 4, 256), BF), pltpu.SemaphoreType.DMA((4,))],
        input_output_aliases={0: 0} if aliased else {},
        compiler_params=LIMIT,
        cost_estimate=pl.CostEstimate(flops=flops, bytes_accessed=1 << 10, transcendentals=0),
        name=name,
    )(*([so_far] if aliased else []), *kept(*operands))


def per_device(hidden, grad_out, weight_base, block_scale):
    w5 = pltpu.with_memory_space_constraint(weight_base.reshape(4, 2, 4, 256, 256), pltpu.HBM)
    scales_t = pltpu.with_memory_space_constraint(block_scale.T, pltpu.HBM)

    sent = scaled_rows(w5, scales_t)
    r0 = sent[0]
    r1, r2, r3 = [shift(sent[k], first_axis_steps(k)) for k in (1, 2, 3)]
    grad_out, hidden, _ = lax.optimization_barrier((grad_out, hidden, r0))
    g0, h = all_tokens(packed(grad_out, hidden))
    g2, g3 = [shift(g0, first_axis_steps(k)) for k in (2, 3)]
    later, r1 = lax.optimization_barrier((g0, r1))
    g1 = shift(later, first_axis_steps(1))

    acc = early_sums(r0, r3, g0, g3)
    plane, acc = lax.optimization_barrier(((g0, g1, g2, g3), acc))
    keep, give = plane_blocks(*plane)
    acc, keep, give = lax.optimization_barrier((acc, keep, give))
    sums = partial_sums(acc, r1, r2, g1, g2)
    seed = picked(lax.ppermute(give, "c", [(1, 0)]), keep)
    sums, seed = lax.optimization_barrier((sums, seed))
    other = swap(seed, "yl")
    parts = [sums[0]] + [None] * 3
    for k in (1, 3, 2):
        parts[k] = shift(sums[k], second_axis_steps(k))
    both, one = paired(seed, other)
    along_x = lambda value, k: lax.ppermute(value, "x", [(i, (i + k) % 4) for i in range(4)])
    far = along_x(one, 2)
    both, *parts = lax.optimization_barrier((both, *parts))
    up, down = along_x(both, 1), along_x(both, 3)
    far_pair = z_pairs(far)

    blocks = summed_blocks(parts)
    blocks = lax.all_to_all(blocks, ("yl", "yh", "c"), 0, 0, tiled=True)
    half = outer_half(first_half_body, "first_half", (h, seed, other, far, far_pair), flops=int(4e9))
    blocks, half = lax.optimization_barrier((blocks, half))
    grad_weight = outer_half(second_half_body, "second_half", (h, up, down), half)
    return finished(blocks), grad_weight


def solution(mesh):
    fine = Mesh(mesh.devices.reshape(4, 2, 4, 2, 2), ("z", "yl", "x", "yh", "c"))
    narrow, wide = ("yh", "c"), ("z", "yl", "x")
    return jax.shard_map(
        per_device,
        mesh=fine,
        in_specs=(
            P(narrow, None, wide),
            P(narrow, wide),
            P(narrow, wide),
            P(narrow, wide),
        ),
        out_specs=(P(narrow, None, wide), P(narrow, None, wide)),
        check_vma=False,
    )
```

```python
import functools

import jax
import jax.numpy as jnp
from jax import lax
from jax.experimental import pallas as pl
from jax.experimental.pallas import tpu as pltpu
from jax.sharding import Mesh, PartitionSpec as P

BF = jnp.bfloat16
F32 = jnp.float32
VM = pltpu.VMEM


def first_axis_steps(k):
    pairs = []
    for z in range(4):
        for x in range(4):
            pairs.append(((z * 4 + x) * 2, (z * 4 + (x + k) % 4) * 2))
            pairs.append(((z * 4 + x) * 2 + 1, (((z + k) % 4) * 4 + x) * 2 + 1))
    return pairs


def second_axis_steps(k):
    pairs = []
    for z in range(4):
        for x in range(4):
            pairs.append(((z * 4 + x) * 2, (((z + k) % 4) * 4 + x) * 2))
            pairs.append(((z * 4 + x) * 2 + 1, (z * 4 + (x + k) % 4) * 2 + 1))
    return pairs


def shift(value, pairs):
    return lax.ppermute(value, ("z", "x", "c"), pairs)


def swap(value, axis):
    return lax.ppermute(value, axis, [(0, 1), (1, 0)])


LIMIT = pltpu.CompilerParams(vmem_limit_bytes=12 << 20)
EARLY = int(2e9)
IN = pl.BlockSpec(memory_space=VM)
HBM = pl.BlockSpec(memory_space=pltpu.HBM)


def kept(*values):
    return [pltpu.with_memory_space_constraint(v, VM) for v in values]


def roles():
    c, x, z = lax.axis_index("c"), lax.axis_index("x"), lax.axis_index("z")
    return c, jnp.where(c == 0, x, z), jnp.where(c == 0, z, x)


def spread_scales(s_ref, wide_ref):
    row = lax.broadcasted_iota(jnp.int32, (16, 256), 0)
    col = lax.broadcasted_iota(jnp.int32, (16, 256), 1)
    spread = jnp.where(col // 16 == row, 1.0, 0.0).astype(BF)
    wide_ref[...] = lax.dot_general(
        s_ref[...], spread, (((0,), (0,)), ((), ())), preferred_element_type=F32
    )


def scale_into(outs, w_ref, s_ref, narrow_ref, wide_ref, sems):
    c, first, _ = roles()
    scales = pltpu.make_async_copy(s_ref, narrow_ref, sems.at[16])
    scales.start()
    copies = []
    for j, (k, o_ref) in enumerate(outs):
        p = (first + k) & 3
        for i in range(4):
            z, x = c * p + (1 - c) * i, c * i + (1 - c) * p
            copy = pltpu.make_async_copy(
                w_ref.at[z, :, x], o_ref.at[pl.ds(2 * i, 2)], sems.at[j * 4 + i]
            )
            copy.start()
            copies.append((copy, o_ref, i, z, x))
    scales.wait()
    spread_scales(narrow_ref, wide_ref)
    for copy, o_ref, i, z, x in copies:
        copy.wait()
        for yl in range(2):
            r = pl.multiple_of((z * 8 + yl * 4 + x) * 16, 16)
            s = wide_ref[pl.ds(r, 16), :]
            w = o_ref[2 * i + yl].astype(F32).reshape(16, 16, 256)
            o_ref[2 * i + yl] = (w * s[:, None, :]).reshape(256, 256).astype(BF)


def scale_body(w_ref, s_ref, *refs):
    outs, scratch = refs[:4], refs[4:]
    scale_into([(k, outs[k]) for k in (1, 3, 2, 0)], w_ref, s_ref, *scratch)


def scaled_rows(w5, scales_t):
    return pl.pallas_call(
        scale_body,
        out_shape=[VM((8, 256, 256), BF)] * 4,
        in_specs=[HBM, HBM],
        out_specs=[IN] * 4,
        scratch_shapes=[VM((16, 512), BF), VM((512, 256), F32), pltpu.SemaphoreType.DMA((17,))],
        compiler_params=LIMIT,
        name="scale",
    )(w5, scales_t)


def packed_body(g_ref, h_ref, o_ref):
    o_ref[0] = g_ref[...]
    h = h_ref[...].reshape(128, 1024)
    for n in range(4):
        o_ref[1 + n] = h[:, n * 256 : (n + 1) * 256]


def packed(grad_out, hidden):
    return pl.pallas_call(
        packed_body,
        out_shape=VM((5, 128, 256), BF),
        in_specs=[IN] * 2,
        out_specs=IN,
        compiler_params=LIMIT,
        name="packed",
    )(grad_out, hidden)


def tokens_body(p0, p1, p2, p3, g_ref, h_ref):
    n = lax.axis_index("yh") * 2 + lax.axis_index("c")
    for r, p in enumerate((p0, p1, p2, p3)):
        t = n ^ r
        g_ref[t >> 1, pl.ds(pl.multiple_of((t & 1) * 128, 128), 128), :] = p[0]
        rows = pl.ds(pl.multiple_of(t * 128, 128), 128)
        for m in range(4):
            h_ref[rows, m * 256 : (m + 1) * 256] = p[1 + m]


def all_tokens(own):
    far = swap(own, "yh")
    pieces = [own, swap(own, "c"), far, swap(far, "c")]
    return pl.pallas_call(
        tokens_body,
        out_shape=[VM((2, 256, 256), BF), VM((512, 1024), BF)],
        in_specs=[IN] * 4,
        out_specs=[IN] * 2,
        compiler_params=LIMIT,
        name="tokens",
    )(*kept(*pieces))


def block_product(g, w, q):
    return lax.dot_general(
        g[...].reshape(512, 256),
        w[pl.ds(q, 2)].reshape(512, 256),
        (((1,), (1,)), ((), ())),
        preferred_element_type=F32,
    )


def early_body(r0, r3, g0, g3, acc):
    for q in range(4):
        acc[q] = block_product(g0, r0, 2 * q) + block_product(g3, r3, 2 * q)


def early_sums(*operands):
    return pl.pallas_call(
        early_body,
        out_shape=VM((4, 512, 512), F32),
        in_specs=[IN] * 4,
        out_specs=IN,
        compiler_params=LIMIT,
        cost_estimate=pl.CostEstimate(flops=EARLY, bytes_accessed=6 << 20, transcendentals=0),
        name="early",
    )(*kept(*operands))


def plane_body(g0, g1, g2, g3, keep, give):
    z, yh = lax.axis_index("z"), lax.axis_index("yh")
    g = (g0, g1, g2, g3)
    for k in range(4):

        @pl.when(((z - 2 * yh) & 3) == k)
        def _():
            give[...] = g[k][...]

        @pl.when(((z - 2 * yh - 1) & 3) == k)
        def _():
            keep[...] = g[k][...]


def plane_blocks(*grads):
    return pl.pallas_call(
        plane_body,
        out_shape=[VM((2, 256, 256), BF)] * 2,
        in_specs=[IN] * 4,
        out_specs=[IN] * 2,
        compiler_params=LIMIT,
        name="plane",
    )(*kept(*grads))


def partial_body(acc, r1, r2, g1, g2, *outs):
    _, _, second = roles()
    for k in (2, 1, 3, 0):
        q = (second + k) & 3
        total = acc[q] + block_product(g1, r1, 2 * q) + block_product(g2, r2, 2 * q)
        outs[k][...] = total.astype(outs[k].dtype)


def partial_sums(*operands):
    return pl.pallas_call(
        partial_body,
        out_shape=[VM((512, 512), F32)]
        + [VM((512, 512), BF)] * 3,
        in_specs=[IN] * 5,
        out_specs=[IN] * 4,
        compiler_params=LIMIT,
        name="partial",
    )(*kept(*operands))


def gather_body(a, b, c, d, o_ref):
    total = a[...] + b[...].astype(F32) + c[...].astype(F32) + d[...].astype(F32)
    total = total.astype(BF)
    for yl in range(2):
        for n in range(4):
            t = n * 128
            o_ref[yl * 4 + n] = total[t : t + 128, yl * 256 : (yl + 1) * 256]


def summed_blocks(parts):
    return pl.pallas_call(
        gather_body,
        out_shape=VM((8, 128, 256), BF),
        in_specs=[IN] * 4,
        out_specs=IN,
        compiler_params=LIMIT,
        name="summed",
    )(parts[0], *kept(*parts[1:]))


def finish_body(r_ref, o_ref):
    r = [(r_ref[n].astype(F32) + r_ref[4 + n].astype(F32)).astype(BF) for n in range(4)]
    o_ref[...] = jnp.concatenate(r, axis=1).reshape(128, 4, 256)


def finished(blocks):
    return pl.pallas_call(
        finish_body,
        out_shape=jax.ShapeDtypeStruct((128, 4, 256), BF),
        in_specs=[IN],
        out_specs=IN,
        compiler_params=LIMIT,
        name="finish",
    )(*kept(blocks))


def picked_body(a_ref, b_ref, o_ref):
    @pl.when(lax.axis_index("c") == 0)
    def _():
        o_ref[...] = a_ref[...]

    @pl.when(lax.axis_index("c") == 1)
    def _():
        o_ref[...] = b_ref[...]


def picked(for_core_0, for_core_1):
    return pl.pallas_call(
        picked_body,
        out_shape=VM((2, 256, 256), BF),
        in_specs=[IN] * 2,
        out_specs=IN,
        compiler_params=LIMIT,
        name="picked",
    )(for_core_0, for_core_1)


def paired_body(a_ref, b_ref, o_ref, one_ref):
    o_ref[0:2] = a_ref[...]
    o_ref[2:4] = b_ref[...]
    odd = lax.axis_index("z") & 1
    one_ref[...] = o_ref[pl.ds(2 * odd, 2)]


def paired(a, b):
    return pl.pallas_call(
        paired_body,
        out_shape=[VM((4, 256, 256), BF), VM((2, 256, 256), BF)],
        in_specs=[IN] * 2,
        out_specs=[IN] * 2,
        compiler_params=LIMIT,
        name="paired",
    )(*kept(a, b))


def z_pairs(value):
    pairs = []
    for z in range(4):
        pairs.append((z * 2, (z ^ 1) * 2))
        pairs.append((z * 2 + 1, (z + 1 if z & 1 else z + 3) % 4 * 2 + 1))
    return lax.ppermute(value, ("z", "c"), pairs)


def outer_into(blocks, h_ref, o_ref, buf, sems):
    x = lax.axis_index("x")
    copies = []
    for i, (yl, k, g) in enumerate(blocks):
        r = pl.multiple_of((yl * 4 + ((x - k) & 3)) * 256, 256)
        p = lax.dot_general(
            g[...].reshape(512, 256),
            h_ref[...],
            (((0,), (0,)), ((), ())),
            preferred_element_type=F32,
        )
        buf[i] = p.astype(BF).reshape(256, 4, 256)
        copy = pltpu.make_async_copy(buf.at[i], o_ref.at[pl.ds(r, 256)], sems.at[i])
        copy.start()
        copies.append(copy)
    for copy in copies:
        copy.wait()


def first_part_body(h_ref, seed, other, *refs):
    yl = lax.axis_index("yl")
    outer_into([(yl, 0, seed), (1 - yl, 0, other)], h_ref, *refs)


def second_part_body(o_in, h_ref, up, down, far, far_pair, *refs):
    yl = lax.axis_index("yl")
    here = yl ^ (lax.axis_index("z") & 1)
    blocks = []
    for k, ref in ((1, up), (3, down)):
        blocks += [(yl, k, ref.at[0:2]), (1 - yl, k, ref.at[2:4])]
    outer_into(blocks + [(here, 2, far), (1 - here, 2, far_pair)], h_ref, *refs)


def outer_part(body, name, operands, so_far=None):
    aliased = so_far is not None
    return pl.pallas_call(
        body,
        out_shape=jax.ShapeDtypeStruct((2048, 4, 256), BF),
        in_specs=[HBM] * aliased + [IN] * len(operands),
        out_specs=HBM,
        scratch_shapes=[VM((6, 256, 4, 256), BF), pltpu.SemaphoreType.DMA((6,))],
        input_output_aliases={0: 0} if aliased else {},
        compiler_params=LIMIT,
        cost_estimate=pl.CostEstimate(flops=int(1e6), bytes_accessed=1 << 10, transcendentals=0),
        name=name,
    )(*([so_far] if aliased else []), *kept(*operands))


def per_device(hidden, grad_out, weight_base, block_scale):
    w5 = pltpu.with_memory_space_constraint(weight_base.reshape(4, 2, 4, 256, 256), pltpu.HBM)
    scales_t = pltpu.with_memory_space_constraint(block_scale.T, pltpu.HBM)

    sent = scaled_rows(w5, scales_t)
    r0 = sent[0]
    r1, r2, r3 = [shift(sent[k], first_axis_steps(k)) for k in (1, 2, 3)]
    grad_out, hidden, _ = lax.optimization_barrier((grad_out, hidden, r0))
    g0, h = all_tokens(packed(grad_out, hidden))
    g2, g3 = [shift(g0, first_axis_steps(k)) for k in (2, 3)]
    later, r1 = lax.optimization_barrier((g0, r1))
    g1 = shift(later, first_axis_steps(1))

    acc = early_sums(r0, r3, g0, g3)
    plane, acc = lax.optimization_barrier(((g0, g1, g2, g3), acc))
    keep, give = plane_blocks(*plane)
    acc, keep, give = lax.optimization_barrier((acc, keep, give))
    sums = partial_sums(acc, r1, r2, g1, g2)
    seed = picked(lax.ppermute(give, "c", [(1, 0)]), keep)
    other = swap(seed, "yl")
    parts = [sums[0]] + [None] * 3
    for k in (1, 3, 2):
        parts[k] = shift(sums[k], second_axis_steps(k))
    both, one = paired(seed, other)
    along_x = lambda value, k: lax.ppermute(value, "x", [(i, (i + k) % 4) for i in range(4)])
    far = along_x(one, 2)
    up, down = along_x(both, 1), along_x(both, 3)
    far_pair = z_pairs(far)

    blocks = summed_blocks(parts)
    blocks = lax.all_to_all(blocks, ("yl", "yh", "c"), 0, 0, tiled=True)
    part = outer_part(first_part_body, "first_part", (h, seed, other))
    blocks, part = lax.optimization_barrier((blocks, part))
    grad_weight = outer_part(second_part_body, "second_part", (h, up, down, far, far_pair), part)
    return finished(blocks), grad_weight


def solution(mesh):
    fine = Mesh(mesh.devices.reshape(4, 2, 4, 2, 2), ("z", "yl", "x", "yh", "c"))
    narrow, wide = ("yh", "c"), ("z", "yl", "x")
    return jax.shard_map(
        per_device,
        mesh=fine,
        in_specs=(
            P(narrow, None, wide),
            P(narrow, wide),
            P(narrow, wide),
            P(narrow, wide),
        ),
        out_specs=(P(narrow, None, wide), P(narrow, None, wide)),
        check_vma=False,
    )
```

```python
import functools

import jax
import jax.numpy as jnp
from jax import lax
from jax.experimental import pallas as pl
from jax.experimental.pallas import tpu as pltpu
from jax.sharding import Mesh, PartitionSpec as P

BF = jnp.bfloat16
F32 = jnp.float32
VM = pltpu.VMEM


def first_axis_steps(k):
    pairs = []
    for z in range(4):
        for x in range(4):
            pairs.append(((z * 4 + x) * 2, (z * 4 + (x + k) % 4) * 2))
            pairs.append(((z * 4 + x) * 2 + 1, (((z + k) % 4) * 4 + x) * 2 + 1))
    return pairs


def second_axis_steps(k):
    pairs = []
    for z in range(4):
        for x in range(4):
            pairs.append(((z * 4 + x) * 2, (((z + k) % 4) * 4 + x) * 2))
            pairs.append(((z * 4 + x) * 2 + 1, (z * 4 + (x + k) % 4) * 2 + 1))
    return pairs


def shift(value, pairs):
    return lax.ppermute(value, ("z", "x", "c"), pairs)


def swap(value, axis):
    return lax.ppermute(value, axis, [(0, 1), (1, 0)])


LIMIT = pltpu.CompilerParams(vmem_limit_bytes=12 << 20)
EARLY = int(2e9)
IN = pl.BlockSpec(memory_space=VM)
HBM = pl.BlockSpec(memory_space=pltpu.HBM)


def kept(*values):
    return [pltpu.with_memory_space_constraint(v, VM) for v in values]


def roles():
    c, x, z = lax.axis_index("c"), lax.axis_index("x"), lax.axis_index("z")
    return c, jnp.where(c == 0, x, z), jnp.where(c == 0, z, x)


def spread_scales(s_ref, wide_ref):
    row = lax.broadcasted_iota(jnp.int32, (16, 256), 0)
    col = lax.broadcasted_iota(jnp.int32, (16, 256), 1)
    spread = jnp.where(col // 16 == row, 1.0, 0.0).astype(BF)
    wide_ref[...] = lax.dot_general(
        s_ref[...], spread, (((0,), (0,)), ((), ())), preferred_element_type=F32
    )


def scale_into(outs, w_ref, s_ref, narrow_ref, wide_ref, sems):
    c, first, _ = roles()
    scales = pltpu.make_async_copy(s_ref, narrow_ref, sems.at[16])
    scales.start()
    copies = []
    for j, (k, o_ref) in enumerate(outs):
        p = (first + k) & 3
        for i in range(4):
            z, x = c * p + (1 - c) * i, c * i + (1 - c) * p
            copy = pltpu.make_async_copy(
                w_ref.at[z, :, x], o_ref.at[pl.ds(2 * i, 2)], sems.at[j * 4 + i]
            )
            copy.start()
            copies.append((copy, o_ref, i, z, x))
    scales.wait()
    spread_scales(narrow_ref, wide_ref)
    for copy, o_ref, i, z, x in copies:
        copy.wait()
        for yl in range(2):
            r = pl.multiple_of((z * 8 + yl * 4 + x) * 16, 16)
            s = wide_ref[pl.ds(r, 16), :]
            w = o_ref[2 * i + yl].astype(F32).reshape(16, 16, 256)
            o_ref[2 * i + yl] = (w * s[:, None, :]).reshape(256, 256).astype(BF)


def scale_body(w_ref, s_ref, *refs):
    outs, scratch = refs[:4], refs[4:]
    scale_into([(k, outs[k]) for k in (1, 3, 2, 0)], w_ref, s_ref, *scratch)


def scaled_rows(w5, scales_t):
    return pl.pallas_call(
        scale_body,
        out_shape=[VM((8, 256, 256), BF)] * 4,
        in_specs=[HBM, HBM],
        out_specs=[IN] * 4,
        scratch_shapes=[VM((16, 512), BF), VM((512, 256), F32), pltpu.SemaphoreType.DMA((17,))],
        compiler_params=LIMIT,
        name="scale",
    )(w5, scales_t)


def packed_body(g_ref, h_ref, o_ref):
    o_ref[0] = g_ref[...]
    h = h_ref[...].reshape(128, 1024)
    for n in range(4):
        o_ref[1 + n] = h[:, n * 256 : (n + 1) * 256]


def packed(grad_out, hidden):
    return pl.pallas_call(
        packed_body,
        out_shape=VM((5, 128, 256), BF),
        in_specs=[IN] * 2,
        out_specs=IN,
        compiler_params=LIMIT,
        name="packed",
    )(grad_out, hidden)


def tokens_body(p0, p1, p2, p3, g_ref, h_ref):
    n = lax.axis_index("yh") * 2 + lax.axis_index("c")
    for r, p in enumerate((p0, p1, p2, p3)):
        t = n ^ r
        g_ref[t >> 1, pl.ds(pl.multiple_of((t & 1) * 128, 128), 128), :] = p[0]
        rows = pl.ds(pl.multiple_of(t * 128, 128), 128)
        for m in range(4):
            h_ref[rows, m * 256 : (m + 1) * 256] = p[1 + m]


def all_tokens(own):
    far = swap(own, "yh")
    pieces = [own, swap(own, "c"), far, swap(far, "c")]
    return pl.pallas_call(
        tokens_body,
        out_shape=[VM((2, 256, 256), BF), VM((512, 1024), BF)],
        in_specs=[IN] * 4,
        out_specs=[IN] * 2,
        compiler_params=LIMIT,
        name="tokens",
    )(*kept(*pieces))


def block_product(g, w, q):
    return lax.dot_general(
        g[...].reshape(512, 256),
        w[pl.ds(q, 2)].reshape(512, 256),
        (((1,), (1,)), ((), ())),
        preferred_element_type=F32,
    )


def early_body(r0, r3, g0, g3, acc):
    for q in range(4):
        acc[q] = block_product(g0, r0, 2 * q) + block_product(g3, r3, 2 * q)


def early_sums(*operands):
    return pl.pallas_call(
        early_body,
        out_shape=VM((4, 512, 512), F32),
        in_specs=[IN] * 4,
        out_specs=IN,
        compiler_params=LIMIT,
        cost_estimate=pl.CostEstimate(flops=EARLY, bytes_accessed=6 << 20, transcendentals=0),
        name="early",
    )(*kept(*operands))


def plane_body(g0, g1, g2, g3, keep, give):
    z, yh = lax.axis_index("z"), lax.axis_index("yh")
    g = (g0, g1, g2, g3)
    for k in range(4):

        @pl.when(((z - 2 * yh) & 3) == k)
        def _():
            give[...] = g[k][...]

        @pl.when(((z - 2 * yh - 1) & 3) == k)
        def _():
            keep[...] = g[k][...]


def plane_blocks(*grads):
    return pl.pallas_call(
        plane_body,
        out_shape=[VM((2, 256, 256), BF)] * 2,
        in_specs=[IN] * 4,
        out_specs=[IN] * 2,
        compiler_params=LIMIT,
        name="plane",
    )(*kept(*grads))


def partial_body(acc, r1, r2, g1, g2, *outs):
    _, _, second = roles()
    for k in (2, 1, 3, 0):
        q = (second + k) & 3
        total = acc[q] + block_product(g1, r1, 2 * q) + block_product(g2, r2, 2 * q)
        outs[k][...] = total.astype(outs[k].dtype)


def partial_sums(*operands):
    return pl.pallas_call(
        partial_body,
        out_shape=[VM((512, 512), F32)]
        + [VM((512, 512), BF)] * 3,
        in_specs=[IN] * 5,
        out_specs=[IN] * 4,
        compiler_params=LIMIT,
        name="partial",
    )(*kept(*operands))


def gather_body(a, b, c, d, o_ref):
    total = a[...] + b[...].astype(F32) + c[...].astype(F32) + d[...].astype(F32)
    total = total.astype(BF)
    for yl in range(2):
        for n in range(4):
            t = n * 128
            o_ref[yl * 4 + n] = total[t : t + 128, yl * 256 : (yl + 1) * 256]


def summed_blocks(parts):
    return pl.pallas_call(
        gather_body,
        out_shape=VM((8, 128, 256), BF),
        in_specs=[IN] * 4,
        out_specs=IN,
        compiler_params=LIMIT,
        name="summed",
    )(parts[0], *kept(*parts[1:]))


def finish_body(r_ref, o_ref):
    r = [(r_ref[n].astype(F32) + r_ref[4 + n].astype(F32)).astype(BF) for n in range(4)]
    o_ref[...] = jnp.concatenate(r, axis=1).reshape(128, 4, 256)


def finished(blocks):
    return pl.pallas_call(
        finish_body,
        out_shape=jax.ShapeDtypeStruct((128, 4, 256), BF),
        in_specs=[IN],
        out_specs=IN,
        compiler_params=LIMIT,
        name="finish",
    )(*kept(blocks))


def picked_body(a_ref, b_ref, o_ref):
    @pl.when(lax.axis_index("c") == 0)
    def _():
        o_ref[...] = a_ref[...]

    @pl.when(lax.axis_index("c") == 1)
    def _():
        o_ref[...] = b_ref[...]


def picked(for_core_0, for_core_1):
    return pl.pallas_call(
        picked_body,
        out_shape=VM((2, 256, 256), BF),
        in_specs=[IN] * 2,
        out_specs=IN,
        compiler_params=LIMIT,
        name="picked",
    )(for_core_0, for_core_1)


def paired_body(a_ref, b_ref, o_ref, one_ref):
    o_ref[0:2] = a_ref[...]
    o_ref[2:4] = b_ref[...]
    odd = lax.axis_index("z") & 1
    one_ref[...] = o_ref[pl.ds(2 * odd, 2)]


def paired(a, b):
    return pl.pallas_call(
        paired_body,
        out_shape=[VM((4, 256, 256), BF), VM((2, 256, 256), BF)],
        in_specs=[IN] * 2,
        out_specs=[IN] * 2,
        compiler_params=LIMIT,
        name="paired",
    )(*kept(a, b))


def z_pairs(value):
    pairs = []
    for z in range(4):
        pairs.append((z * 2, (z ^ 1) * 2))
        pairs.append((z * 2 + 1, (z + 1 if z & 1 else z + 3) % 4 * 2 + 1))
    return lax.ppermute(value, ("z", "c"), pairs)


def outer_into(blocks, h_ref, o_ref, buf, sems):
    x = lax.axis_index("x")
    copies = []
    for i, (yl, k, g) in enumerate(blocks):
        r = pl.multiple_of((yl * 4 + ((x - k) & 3)) * 256, 256)
        p = lax.dot_general(
            g[...].reshape(512, 256),
            h_ref[...],
            (((0,), (0,)), ((), ())),
            preferred_element_type=F32,
        )
        buf[i] = p.astype(BF).reshape(256, 4, 256)
        copy = pltpu.make_async_copy(buf.at[i], o_ref.at[pl.ds(r, 256)], sems.at[i])
        copy.start()
        copies.append(copy)
    for copy in copies:
        copy.wait()


def first_part_body(h_ref, seed, other, *refs):
    yl = lax.axis_index("yl")
    outer_into([(yl, 0, seed), (1 - yl, 0, other)], h_ref, *refs)


def second_part_body(o_in, h_ref, far, far_pair, *refs):
    here = lax.axis_index("yl") ^ (lax.axis_index("z") & 1)
    outer_into([(here, 2, far), (1 - here, 2, far_pair)], h_ref, *refs)


def third_part_body(o_in, h_ref, up, down, *refs):
    yl = lax.axis_index("yl")
    blocks = []
    for k, ref in ((1, up), (3, down)):
        blocks += [(yl, k, ref.at[0:2]), (1 - yl, k, ref.at[2:4])]
    outer_into(blocks, h_ref, *refs)


def outer_part(body, name, operands, so_far=None):
    aliased = so_far is not None
    return pl.pallas_call(
        body,
        out_shape=jax.ShapeDtypeStruct((2048, 4, 256), BF),
        in_specs=[HBM] * aliased + [IN] * len(operands),
        out_specs=HBM,
        scratch_shapes=[VM((4, 256, 4, 256), BF), pltpu.SemaphoreType.DMA((4,))],
        input_output_aliases={0: 0} if aliased else {},
        compiler_params=LIMIT,
        cost_estimate=pl.CostEstimate(flops=int(1e6), bytes_accessed=1 << 10, transcendentals=0),
        name=name,
    )(*([so_far] if aliased else []), *kept(*operands))


def per_device(hidden, grad_out, weight_base, block_scale):
    w5 = pltpu.with_memory_space_constraint(weight_base.reshape(4, 2, 4, 256, 256), pltpu.HBM)
    scales_t = pltpu.with_memory_space_constraint(block_scale.T, pltpu.HBM)

    sent = scaled_rows(w5, scales_t)
    r0 = sent[0]
    r1, r2, r3 = [shift(sent[k], first_axis_steps(k)) for k in (1, 2, 3)]
    grad_out, hidden, _ = lax.optimization_barrier((grad_out, hidden, r0))
    g0, h = all_tokens(packed(grad_out, hidden))
    g2, g3 = [shift(g0, first_axis_steps(k)) for k in (2, 3)]
    later, r1 = lax.optimization_barrier((g0, r1))
    g1 = shift(later, first_axis_steps(1))

    acc = early_sums(r0, r3, g0, g3)
    plane, acc = lax.optimization_barrier(((g0, g1, g2, g3), acc))
    keep, give = plane_blocks(*plane)
    acc, keep, give = lax.optimization_barrier((acc, keep, give))
    sums = partial_sums(acc, r1, r2, g1, g2)
    seed = picked(lax.ppermute(give, "c", [(1, 0)]), keep)
    other = swap(seed, "yl")
    parts = [sums[0]] + [None] * 3
    for k in (1, 3, 2):
        parts[k] = shift(sums[k], second_axis_steps(k))
    both, one = paired(seed, other)
    along_x = lambda value, k: lax.ppermute(value, "x", [(i, (i + k) % 4) for i in range(4)])
    far = along_x(one, 2)
    up, down = along_x(both, 1), along_x(both, 3)
    far_pair = z_pairs(far)

    blocks = summed_blocks(parts)
    blocks = lax.all_to_all(blocks, ("yl", "yh", "c"), 0, 0, tiled=True)
    part = outer_part(first_part_body, "first_part", (h, seed, other))
    part = outer_part(second_part_body, "second_part", (h, far, far_pair), part)
    blocks, part = lax.optimization_barrier((blocks, part))
    grad_weight = outer_part(third_part_body, "third_part", (h, up, down), part)
    return finished(blocks), grad_weight


def solution(mesh):
    fine = Mesh(mesh.devices.reshape(4, 2, 4, 2, 2), ("z", "yl", "x", "yh", "c"))
    narrow, wide = ("yh", "c"), ("z", "yl", "x")
    return jax.shard_map(
        per_device,
        mesh=fine,
        in_specs=(
            P(narrow, None, wide),
            P(narrow, wide),
            P(narrow, wide),
            P(narrow, wide),
        ),
        out_specs=(P(narrow, None, wide), P(narrow, None, wide)),
        check_vma=False,
    )
```

```python
import functools

import jax
import jax.numpy as jnp
from jax import lax
from jax.experimental import pallas as pl
from jax.experimental.pallas import tpu as pltpu
from jax.sharding import Mesh, PartitionSpec as P

BF = jnp.bfloat16
F32 = jnp.float32
VM = pltpu.VMEM


def first_axis_steps(k):
    pairs = []
    for z in range(4):
        for x in range(4):
            pairs.append(((z * 4 + x) * 2, (z * 4 + (x + k) % 4) * 2))
            pairs.append(((z * 4 + x) * 2 + 1, (((z + k) % 4) * 4 + x) * 2 + 1))
    return pairs


def second_axis_steps(k):
    pairs = []
    for z in range(4):
        for x in range(4):
            pairs.append(((z * 4 + x) * 2, (((z + k) % 4) * 4 + x) * 2))
            pairs.append(((z * 4 + x) * 2 + 1, (z * 4 + (x + k) % 4) * 2 + 1))
    return pairs


def shift(value, pairs):
    return lax.ppermute(value, ("z", "x", "c"), pairs)


def swap(value, axis):
    return lax.ppermute(value, axis, [(0, 1), (1, 0)])


LIMIT = pltpu.CompilerParams(vmem_limit_bytes=12 << 20)
EARLY = int(2e9)
IN = pl.BlockSpec(memory_space=VM)
HBM = pl.BlockSpec(memory_space=pltpu.HBM)


def kept(*values):
    return [pltpu.with_memory_space_constraint(v, VM) for v in values]


def roles():
    c, x, z = lax.axis_index("c"), lax.axis_index("x"), lax.axis_index("z")
    return c, jnp.where(c == 0, x, z), jnp.where(c == 0, z, x)


def spread_scales(s_ref, wide_ref):
    row = lax.broadcasted_iota(jnp.int32, (16, 256), 0)
    col = lax.broadcasted_iota(jnp.int32, (16, 256), 1)
    spread = jnp.where(col // 16 == row, 1.0, 0.0).astype(BF)
    wide_ref[...] = lax.dot_general(
        s_ref[...], spread, (((0,), (0,)), ((), ())), preferred_element_type=F32
    )


def scale_into(outs, w_ref, s_ref, narrow_ref, wide_ref, sems):
    c, first, _ = roles()
    scales = pltpu.make_async_copy(s_ref, narrow_ref, sems.at[16])
    scales.start()
    copies = []
    for j, (k, buffers) in enumerate(outs):
        p = (first + k) & 3
        places = [r.at[pl.ds(i, 2)] for r in buffers for i in range(0, r.shape[0], 2)]
        for i, o_ref in enumerate(places):
            z, x = c * p + (1 - c) * i, c * i + (1 - c) * p
            copy = pltpu.make_async_copy(w_ref.at[z, :, x], o_ref, sems.at[j * 4 + i])
            copy.start()
            copies.append((copy, o_ref, z, x))
    scales.wait()
    spread_scales(narrow_ref, wide_ref)
    for copy, o_ref, z, x in copies:
        copy.wait()
        for yl in range(2):
            r = pl.multiple_of((z * 8 + yl * 4 + x) * 16, 16)
            s = wide_ref[pl.ds(r, 16), :]
            w = o_ref[yl].astype(F32).reshape(16, 16, 256)
            o_ref[yl] = (w * s[:, None, :]).reshape(256, 256).astype(BF)


def scale_body(w_ref, s_ref, o0, o1a, o1b, o2, o3, *scratch):
    outs = [(1, (o1a, o1b)), (3, (o3,)), (2, (o2,)), (0, (o0,))]
    scale_into(outs, w_ref, s_ref, *scratch)


def scaled_rows(w5, scales_t):
    return pl.pallas_call(
        scale_body,
        out_shape=[VM((n, 256, 256), BF) for n in (8, 6, 2, 8, 8)],
        in_specs=[HBM, HBM],
        out_specs=[IN] * 5,
        scratch_shapes=[VM((16, 512), BF), VM((512, 256), F32), pltpu.SemaphoreType.DMA((17,))],
        compiler_params=LIMIT,
        name="scale",
    )(w5, scales_t)


def packed_body(g_ref, h_ref, o_ref):
    o_ref[0] = g_ref[...]
    h = h_ref[...].reshape(128, 1024)
    for n in range(4):
        o_ref[1 + n] = h[:, n * 256 : (n + 1) * 256]


def packed(grad_out, hidden):
    return pl.pallas_call(
        packed_body,
        out_shape=VM((5, 128, 256), BF),
        in_specs=[IN] * 2,
        out_specs=IN,
        compiler_params=LIMIT,
        name="packed",
    )(grad_out, hidden)


def tokens_body(rows_ref, p0, p1, p2, p3, g_ref, h_ref, o_ref):
    n = lax.axis_index("yh") * 2 + lax.axis_index("c")
    for r, p in enumerate((p0, p1, p2, p3)):
        t = n ^ r
        g_ref[t >> 1, pl.ds(pl.multiple_of((t & 1) * 128, 128), 128), :] = p[0]
        rows = pl.ds(pl.multiple_of(t * 128, 128), 128)
        for m in range(4):
            h_ref[rows, m * 256 : (m + 1) * 256] = p[1 + m]
    o_ref[0:2] = rows_ref[...]
    o_ref[2:4] = g_ref[...]


def all_tokens(own, rows):
    far = swap(own, "yh")
    pieces = [own, swap(own, "c"), far, swap(far, "c")]
    return pl.pallas_call(
        tokens_body,
        out_shape=[VM((2, 256, 256), BF), VM((512, 1024), BF), VM((4, 256, 256), BF)],
        in_specs=[IN] * 5,
        out_specs=[IN] * 3,
        compiler_params=LIMIT,
        cost_estimate=pl.CostEstimate(flops=1000, bytes_accessed=1000, transcendentals=0),
        name="tokens",
    )(*kept(rows, *pieces))


def block_product(g, w, q):
    return lax.dot_general(
        g[...].reshape(512, 256),
        w[pl.ds(q, 2)].reshape(512, 256),
        (((1,), (1,)), ((), ())),
        preferred_element_type=F32,
    )


def early_body(r0, r3, g0, g3, acc):
    for q in range(4):
        acc[q] = block_product(g0, r0, 2 * q) + block_product(g3, r3, 2 * q)


def early_sums(*operands):
    return pl.pallas_call(
        early_body,
        out_shape=VM((4, 512, 512), F32),
        in_specs=[IN] * 4,
        out_specs=IN,
        compiler_params=LIMIT,
        cost_estimate=pl.CostEstimate(flops=EARLY, bytes_accessed=6 << 20, transcendentals=0),
        name="early",
    )(*kept(*operands))


def plane_body(g0, r1b, g2, g3, keep, give):
    z, yh = lax.axis_index("z"), lax.axis_index("yh")
    g = (g0, r1b.at[2:4], g2, g3)
    for k in range(4):

        @pl.when(((z - 2 * yh) & 3) == k)
        def _():
            give[...] = g[k][...]

        @pl.when(((z - 2 * yh - 1) & 3) == k)
        def _():
            keep[...] = g[k][...]


def plane_blocks(*grads):
    return pl.pallas_call(
        plane_body,
        out_shape=[VM((2, 256, 256), BF)] * 2,
        in_specs=[IN] * 4,
        out_specs=[IN] * 2,
        compiler_params=LIMIT,
        name="plane",
    )(*kept(*grads))


def partial_body(acc, r1a, r1b, r2, g2, *outs):
    outs, r1 = outs[:4], outs[4]
    r1[0:6] = r1a[...]
    r1[6:8] = r1b[0:2]
    g1 = r1b.at[2:4]
    _, _, second = roles()
    for k in (2, 1, 3, 0):
        q = (second + k) & 3
        total = acc[q] + block_product(g1, r1, 2 * q) + block_product(g2, r2, 2 * q)
        outs[k][...] = total.astype(outs[k].dtype)


def partial_sums(*operands):
    return pl.pallas_call(
        partial_body,
        out_shape=[VM((512, 512), F32)]
        + [VM((512, 512), BF)] * 3,
        in_specs=[IN] * 5,
        out_specs=[IN] * 4,
        scratch_shapes=[VM((8, 256, 256), BF)],
        compiler_params=LIMIT,
        name="partial",
    )(*kept(*operands))


def gather_body(a, b, c, d, o_ref):
    total = a[...] + b[...].astype(F32) + c[...].astype(F32) + d[...].astype(F32)
    total = total.astype(BF)
    for yl in range(2):
        for n in range(4):
            t = n * 128
            o_ref[yl * 4 + n] = total[t : t + 128, yl * 256 : (yl + 1) * 256]


def summed_blocks(parts):
    return pl.pallas_call(
        gather_body,
        out_shape=VM((8, 128, 256), BF),
        in_specs=[IN] * 4,
        out_specs=IN,
        compiler_params=LIMIT,
        name="summed",
    )(parts[0], *kept(*parts[1:]))


def finish_body(r_ref, o_ref):
    r = [(r_ref[n].astype(F32) + r_ref[4 + n].astype(F32)).astype(BF) for n in range(4)]
    o_ref[...] = jnp.concatenate(r, axis=1).reshape(128, 4, 256)


def finished(blocks):
    return pl.pallas_call(
        finish_body,
        out_shape=jax.ShapeDtypeStruct((128, 4, 256), BF),
        in_specs=[IN],
        out_specs=IN,
        compiler_params=LIMIT,
        name="finish",
    )(*kept(blocks))


def picked_body(a_ref, b_ref, o_ref):
    @pl.when(lax.axis_index("c") == 0)
    def _():
        o_ref[...] = a_ref[...]

    @pl.when(lax.axis_index("c") == 1)
    def _():
        o_ref[...] = b_ref[...]


def picked(for_core_0, for_core_1):
    return pl.pallas_call(
        picked_body,
        out_shape=VM((2, 256, 256), BF),
        in_specs=[IN] * 2,
        out_specs=IN,
        compiler_params=LIMIT,
        name="picked",
    )(for_core_0, for_core_1)


def paired_body(a_ref, b_ref, o_ref, one_ref):
    o_ref[0:2] = a_ref[...]
    o_ref[2:4] = b_ref[...]
    odd = lax.axis_index("z") & 1
    one_ref[...] = o_ref[pl.ds(2 * odd, 2)]


def paired(a, b):
    return pl.pallas_call(
        paired_body,
        out_shape=[VM((4, 256, 256), BF), VM((2, 256, 256), BF)],
        in_specs=[IN] * 2,
        out_specs=[IN] * 2,
        compiler_params=LIMIT,
        name="paired",
    )(*kept(a, b))


def z_pairs(value):
    pairs = []
    for z in range(4):
        pairs.append((z * 2, (z ^ 1) * 2))
        pairs.append((z * 2 + 1, (z + 1 if z & 1 else z + 3) % 4 * 2 + 1))
    return lax.ppermute(value, ("z", "c"), pairs)


def outer_into(blocks, h_ref, o_ref, buf, sems):
    x = lax.axis_index("x")
    copies = []
    for i, (yl, k, g) in enumerate(blocks):
        r = pl.multiple_of((yl * 4 + ((x - k) & 3)) * 256, 256)
        p = lax.dot_general(
            g[...].reshape(512, 256),
            h_ref[...],
            (((0,), (0,)), ((), ())),
            preferred_element_type=F32,
        )
        buf[i] = p.astype(BF).reshape(256, 4, 256)
        copy = pltpu.make_async_copy(buf.at[i], o_ref.at[pl.ds(r, 256)], sems.at[i])
        copy.start()
        copies.append(copy)
    for copy in copies:
        copy.wait()


def first_part_body(h_ref, seed, other, *refs):
    yl = lax.axis_index("yl")
    outer_into([(yl, 0, seed), (1 - yl, 0, other)], h_ref, *refs)


def second_part_body(o_in, h_ref, far, far_pair, *refs):
    here = lax.axis_index("yl") ^ (lax.axis_index("z") & 1)
    outer_into([(here, 2, far), (1 - here, 2, far_pair)], h_ref, *refs)


def third_part_body(o_in, h_ref, up, down, *refs):
    yl = lax.axis_index("yl")
    blocks = []
    for k, ref in ((1, up), (3, down)):
        blocks += [(yl, k, ref.at[0:2]), (1 - yl, k, ref.at[2:4])]
    outer_into(blocks, h_ref, *refs)


def outer_part(body, name, operands, so_far=None):
    aliased = so_far is not None
    return pl.pallas_call(
        body,
        out_shape=jax.ShapeDtypeStruct((2048, 4, 256), BF),
        in_specs=[HBM] * aliased + [IN] * len(operands),
        out_specs=HBM,
        scratch_shapes=[VM((4, 256, 4, 256), BF), pltpu.SemaphoreType.DMA((4,))],
        input_output_aliases={0: 0} if aliased else {},
        compiler_params=LIMIT,
        cost_estimate=pl.CostEstimate(flops=int(1e6), bytes_accessed=1 << 10, transcendentals=0),
        name=name,
    )(*([so_far] if aliased else []), *kept(*operands))


def per_device(hidden, grad_out, weight_base, block_scale):
    w5 = pltpu.with_memory_space_constraint(weight_base.reshape(4, 2, 4, 256, 256), pltpu.HBM)
    scales_t = pltpu.with_memory_space_constraint(block_scale.T, pltpu.HBM)

    r0, sent1a, sent1b, sent2, sent3 = scaled_rows(w5, scales_t)
    r1a = shift(sent1a, first_axis_steps(1))
    r2, r3 = shift(sent2, first_axis_steps(2)), shift(sent3, first_axis_steps(3))
    grad_out, hidden, _ = lax.optimization_barrier((grad_out, hidden, r0))
    g0, h, sent1b = all_tokens(packed(grad_out, hidden), sent1b)
    sent1b, g0, r1a = lax.optimization_barrier((sent1b, g0, r1a))
    r1b = shift(sent1b, first_axis_steps(1))
    g2, g3 = [shift(g0, first_axis_steps(k)) for k in (2, 3)]

    acc = early_sums(r0, r3, g0, g3)
    plane, acc = lax.optimization_barrier(((g0, r1b, g2, g3), acc))
    keep, give = plane_blocks(*plane)
    acc, keep, give = lax.optimization_barrier((acc, keep, give))
    sums = partial_sums(acc, r1a, r1b, r2, g2)
    seed = picked(lax.ppermute(give, "c", [(1, 0)]), keep)
    other = swap(seed, "yl")
    parts = [sums[0]] + [None] * 3
    for k in (1, 3, 2):
        parts[k] = shift(sums[k], second_axis_steps(k))
    both, one = paired(seed, other)
    along_x = lambda value, k: lax.ppermute(value, "x", [(i, (i + k) % 4) for i in range(4)])
    far = along_x(one, 2)
    up, down = along_x(both, 1), along_x(both, 3)
    far_pair = z_pairs(far)

    blocks = summed_blocks(parts)
    blocks = lax.all_to_all(blocks, ("yl", "yh", "c"), 0, 0, tiled=True)
    part = outer_part(first_part_body, "first_part", (h, seed, other))
    part = outer_part(second_part_body, "second_part", (h, far, far_pair), part)
    blocks, part = lax.optimization_barrier((blocks, part))
    grad_weight = outer_part(third_part_body, "third_part", (h, up, down), part)
    return finished(blocks), grad_weight


def solution(mesh):
    fine = Mesh(mesh.devices.reshape(4, 2, 4, 2, 2), ("z", "yl", "x", "yh", "c"))
    narrow, wide = ("yh", "c"), ("z", "yl", "x")
    return jax.shard_map(
        per_device,
        mesh=fine,
        in_specs=(
            P(narrow, None, wide),
            P(narrow, wide),
            P(narrow, wide),
            P(narrow, wide),
        ),
        out_specs=(P(narrow, None, wide), P(narrow, None, wide)),
        check_vma=False,
    )
```

```python
import functools

import jax
import jax.numpy as jnp
from jax import lax
from jax.experimental import pallas as pl
from jax.experimental.pallas import tpu as pltpu
from jax.sharding import Mesh, PartitionSpec as P

BF = jnp.bfloat16
F32 = jnp.float32
VM = pltpu.VMEM


def first_axis_steps(k):
    pairs = []
    for z in range(4):
        for x in range(4):
            pairs.append(((z * 4 + x) * 2, (z * 4 + (x + k) % 4) * 2))
            pairs.append(((z * 4 + x) * 2 + 1, (((z + k) % 4) * 4 + x) * 2 + 1))
    return pairs


def second_axis_steps(k):
    pairs = []
    for z in range(4):
        for x in range(4):
            pairs.append(((z * 4 + x) * 2, (((z + k) % 4) * 4 + x) * 2))
            pairs.append(((z * 4 + x) * 2 + 1, (z * 4 + (x + k) % 4) * 2 + 1))
    return pairs


def shift(value, pairs):
    return lax.ppermute(value, ("z", "x", "c"), pairs)


def swap(value, axis):
    return lax.ppermute(value, axis, [(0, 1), (1, 0)])


LIMIT = pltpu.CompilerParams(vmem_limit_bytes=12 << 20)
EARLY = int(2e9)
IN = pl.BlockSpec(memory_space=VM)
HBM = pl.BlockSpec(memory_space=pltpu.HBM)


def kept(*values):
    return [pltpu.with_memory_space_constraint(v, VM) for v in values]


def roles():
    c, x, z = lax.axis_index("c"), lax.axis_index("x"), lax.axis_index("z")
    return c, jnp.where(c == 0, x, z), jnp.where(c == 0, z, x)


def spread_scales(s_ref, wide_ref):
    row = lax.broadcasted_iota(jnp.int32, (16, 256), 0)
    col = lax.broadcasted_iota(jnp.int32, (16, 256), 1)
    spread = jnp.where(col // 16 == row, 1.0, 0.0).astype(BF)
    wide_ref[...] = lax.dot_general(
        s_ref[...], spread, (((0,), (0,)), ((), ())), preferred_element_type=F32
    )


def scale_into(outs, w_ref, s_ref, narrow_ref, wide_ref, sems):
    c, first, _ = roles()
    scales = pltpu.make_async_copy(s_ref, narrow_ref, sems.at[16])
    scales.start()
    copies = []
    for j, (k, buffers) in enumerate(outs):
        p = (first + k) & 3
        places = [r.at[pl.ds(i, 2)] for r in buffers for i in range(0, r.shape[0], 2)]
        for i, o_ref in enumerate(places):
            z, x = c * p + (1 - c) * i, c * i + (1 - c) * p
            copy = pltpu.make_async_copy(w_ref.at[z, :, x], o_ref, sems.at[j * 4 + i])
            copy.start()
            copies.append((copy, o_ref, z, x))
    scales.wait()
    spread_scales(narrow_ref, wide_ref)
    for copy, o_ref, z, x in copies:
        copy.wait()
        for yl in range(2):
            r = pl.multiple_of((z * 8 + yl * 4 + x) * 16, 16)
            s = wide_ref[pl.ds(r, 16), :]
            w = o_ref[yl].astype(F32).reshape(16, 16, 256)
            o_ref[yl] = (w * s[:, None, :]).reshape(256, 256).astype(BF)


def scale_body(w_ref, s_ref, o0, o1a, o1b, o2, o3, *scratch):
    outs = [(1, (o1a, o1b)), (3, (o3,)), (2, (o2,)), (0, (o0,))]
    scale_into(outs, w_ref, s_ref, *scratch)


def scaled_rows(w5, scales_t):
    return pl.pallas_call(
        scale_body,
        out_shape=[VM((n, 256, 256), BF) for n in (8, 6, 2, 8, 8)],
        in_specs=[HBM, HBM],
        out_specs=[IN] * 5,
        scratch_shapes=[VM((16, 512), BF), VM((512, 256), F32), pltpu.SemaphoreType.DMA((17,))],
        compiler_params=LIMIT,
        name="scale",
    )(w5, scales_t)


def packed_body(g_ref, h_ref, o_ref):
    o_ref[0] = g_ref[...]
    h = h_ref[...].reshape(128, 1024)
    for n in range(4):
        o_ref[1 + n] = h[:, n * 256 : (n + 1) * 256]


def packed(grad_out, hidden):
    return pl.pallas_call(
        packed_body,
        out_shape=VM((5, 128, 256), BF),
        in_specs=[IN] * 2,
        out_specs=IN,
        compiler_params=LIMIT,
        name="packed",
    )(grad_out, hidden)


def tokens_body(rows_ref, p0, p1, p2, p3, g_ref, h_ref, o_ref):
    n = lax.axis_index("yh") * 2 + lax.axis_index("c")
    for r, p in enumerate((p0, p1, p2, p3)):
        t = n ^ r
        g_ref[t >> 1, pl.ds(pl.multiple_of((t & 1) * 128, 128), 128), :] = p[0]
        rows = pl.ds(pl.multiple_of(t * 128, 128), 128)
        for m in range(4):
            h_ref[rows, m * 256 : (m + 1) * 256] = p[1 + m]
    o_ref[0:2] = rows_ref[...]
    o_ref[2:4] = g_ref[...]


def all_tokens(own, rows):
    far = swap(own, "yh")
    pieces = [own, swap(own, "c"), far, swap(far, "c")]
    return pl.pallas_call(
        tokens_body,
        out_shape=[VM((2, 256, 256), BF), VM((512, 1024), BF), VM((4, 256, 256), BF)],
        in_specs=[IN] * 5,
        out_specs=[IN] * 3,
        compiler_params=LIMIT,
        cost_estimate=pl.CostEstimate(flops=1000, bytes_accessed=1000, transcendentals=0),
        name="tokens",
    )(*kept(rows, *pieces))


def block_product(g, w, q):
    return lax.dot_general(
        g[...].reshape(512, 256),
        w[pl.ds(q, 2)].reshape(512, 256),
        (((1,), (1,)), ((), ())),
        preferred_element_type=F32,
    )


def early_body(r0, r3, g0, g3, acc):
    for q in range(4):
        acc[q] = block_product(g0, r0, 2 * q) + block_product(g3, r3, 2 * q)


def early_sums(*operands):
    return pl.pallas_call(
        early_body,
        out_shape=VM((4, 512, 512), F32),
        in_specs=[IN] * 4,
        out_specs=IN,
        compiler_params=LIMIT,
        cost_estimate=pl.CostEstimate(flops=EARLY, bytes_accessed=6 << 20, transcendentals=0),
        name="early",
    )(*kept(*operands))


def plane_body(g0, r1b, g2, g3, keep, give):
    z, yh = lax.axis_index("z"), lax.axis_index("yh")
    g = (g0, r1b.at[2:4], g2, g3)
    for k in range(4):

        @pl.when(((z - 2 * yh) & 3) == k)
        def _():
            give[...] = g[k][...]

        @pl.when(((z - 2 * yh - 1) & 3) == k)
        def _():
            keep[...] = g[k][...]


def plane_blocks(*grads):
    return pl.pallas_call(
        plane_body,
        out_shape=[VM((2, 256, 256), BF)] * 2,
        in_specs=[IN] * 4,
        out_specs=[IN] * 2,
        compiler_params=LIMIT,
        name="plane",
    )(*kept(*grads))


def partial_body(acc, r1a, r1b, r2, g2, *outs):
    outs, r1 = outs[:4], outs[4]
    r1[0:6] = r1a[...]
    r1[6:8] = r1b[0:2]
    g1 = r1b.at[2:4]
    _, _, second = roles()
    for k in (2, 1, 3, 0):
        q = (second + k) & 3
        total = acc[q] + block_product(g1, r1, 2 * q) + block_product(g2, r2, 2 * q)
        outs[k][...] = total.astype(outs[k].dtype)


def partial_sums(*operands):
    return pl.pallas_call(
        partial_body,
        out_shape=[VM((512, 512), F32)]
        + [VM((512, 512), BF)] * 3,
        in_specs=[IN] * 5,
        out_specs=[IN] * 4,
        scratch_shapes=[VM((8, 256, 256), BF)],
        compiler_params=LIMIT,
        name="partial",
    )(*kept(*operands))


def gather_body(a, b, c, d, o_ref):
    total = a[...] + b[...].astype(F32) + c[...].astype(F32) + d[...].astype(F32)
    total = total.astype(BF)
    for yl in range(2):
        for n in range(4):
            t = n * 128
            o_ref[yl * 4 + n] = total[t : t + 128, yl * 256 : (yl + 1) * 256]


def summed_blocks(parts):
    return pl.pallas_call(
        gather_body,
        out_shape=VM((8, 128, 256), BF),
        in_specs=[IN] * 4,
        out_specs=IN,
        compiler_params=LIMIT,
        name="summed",
    )(parts[0], *kept(*parts[1:]))


def picked_body(a_ref, b_ref, o_ref):
    @pl.when(lax.axis_index("c") == 0)
    def _():
        o_ref[...] = a_ref[...]

    @pl.when(lax.axis_index("c") == 1)
    def _():
        o_ref[...] = b_ref[...]


def picked(for_core_0, for_core_1):
    return pl.pallas_call(
        picked_body,
        out_shape=VM((2, 256, 256), BF),
        in_specs=[IN] * 2,
        out_specs=IN,
        compiler_params=LIMIT,
        name="picked",
    )(for_core_0, for_core_1)


def paired_body(a_ref, b_ref, o_ref, one_ref):
    o_ref[0:2] = a_ref[...]
    o_ref[2:4] = b_ref[...]
    odd = lax.axis_index("z") & 1
    one_ref[...] = o_ref[pl.ds(2 * odd, 2)]


def paired(a, b):
    return pl.pallas_call(
        paired_body,
        out_shape=[VM((4, 256, 256), BF), VM((2, 256, 256), BF)],
        in_specs=[IN] * 2,
        out_specs=[IN] * 2,
        compiler_params=LIMIT,
        name="paired",
    )(*kept(a, b))


def z_pairs(value):
    pairs = []
    for z in range(4):
        pairs.append((z * 2, (z ^ 1) * 2))
        pairs.append((z * 2 + 1, (z + 1 if z & 1 else z + 3) % 4 * 2 + 1))
    return lax.ppermute(value, ("z", "c"), pairs)


def outer_into(blocks, h_ref, o_ref, buf, sems):
    x = lax.axis_index("x")
    copies = []
    for i, (yl, k, g) in enumerate(blocks):
        r = pl.multiple_of((yl * 4 + ((x - k) & 3)) * 256, 256)
        p = lax.dot_general(
            g[...].reshape(512, 256),
            h_ref[...],
            (((0,), (0,)), ((), ())),
            preferred_element_type=F32,
        )
        buf[i] = p.astype(BF).reshape(256, 4, 256)
        copy = pltpu.make_async_copy(buf.at[i], o_ref.at[pl.ds(r, 256)], sems.at[i])
        copy.start()
        copies.append(copy)
    for copy in copies:
        copy.wait()


def first_part_body(h_ref, seed, other, *refs):
    yl = lax.axis_index("yl")
    outer_into([(yl, 0, seed), (1 - yl, 0, other)], h_ref, *refs)


def second_part_body(o_in, h_ref, far, far_pair, *refs):
    here = lax.axis_index("yl") ^ (lax.axis_index("z") & 1)
    outer_into([(here, 2, far), (1 - here, 2, far_pair)], h_ref, *refs)


def last_part_body(o_in, h_ref, up, down, r_ref, o_ref, d_ref, buf, sems, d_buf, d_sem):
    r = [(r_ref[n].astype(F32) + r_ref[4 + n].astype(F32)).astype(BF) for n in range(4)]
    d_buf[...] = jnp.concatenate(r, axis=1).reshape(128, 4, 256)
    copy = pltpu.make_async_copy(d_buf, d_ref, d_sem.at[0])
    copy.start()
    yl = lax.axis_index("yl")
    blocks = []
    for k, ref in ((1, up), (3, down)):
        blocks += [(yl, k, ref.at[0:2]), (1 - yl, k, ref.at[2:4])]
    outer_into(blocks, h_ref, o_ref, buf, sems)
    copy.wait()


def last_part(operands, so_far):
    return pl.pallas_call(
        last_part_body,
        out_shape=[
            jax.ShapeDtypeStruct((2048, 4, 256), BF),
            jax.ShapeDtypeStruct((128, 4, 256), BF),
        ],
        in_specs=[HBM] + [IN] * len(operands),
        out_specs=[HBM, HBM],
        scratch_shapes=[
            VM((4, 256, 4, 256), BF),
            pltpu.SemaphoreType.DMA((4,)),
            VM((128, 4, 256), BF),
            pltpu.SemaphoreType.DMA((1,)),
        ],
        input_output_aliases={0: 0},
        compiler_params=LIMIT,
        name="last_part",
    )(so_far, *kept(*operands))


def outer_part(body, name, operands, so_far=None):
    aliased = so_far is not None
    return pl.pallas_call(
        body,
        out_shape=jax.ShapeDtypeStruct((2048, 4, 256), BF),
        in_specs=[HBM] * aliased + [IN] * len(operands),
        out_specs=HBM,
        scratch_shapes=[VM((4, 256, 4, 256), BF), pltpu.SemaphoreType.DMA((4,))],
        input_output_aliases={0: 0} if aliased else {},
        compiler_params=LIMIT,
        cost_estimate=pl.CostEstimate(flops=int(1e6), bytes_accessed=1 << 10, transcendentals=0),
        name=name,
    )(*([so_far] if aliased else []), *kept(*operands))


def per_device(hidden, grad_out, weight_base, block_scale):
    w5 = pltpu.with_memory_space_constraint(weight_base.reshape(4, 2, 4, 256, 256), pltpu.HBM)
    scales_t = pltpu.with_memory_space_constraint(block_scale.T, pltpu.HBM)

    r0, sent1a, sent1b, sent2, sent3 = scaled_rows(w5, scales_t)
    r1a = shift(sent1a, first_axis_steps(1))
    r2, r3 = shift(sent2, first_axis_steps(2)), shift(sent3, first_axis_steps(3))
    grad_out, hidden, _ = lax.optimization_barrier((grad_out, hidden, r0))
    g0, h, sent1b = all_tokens(packed(grad_out, hidden), sent1b)
    sent1b, g0, r1a = lax.optimization_barrier((sent1b, g0, r1a))
    r1b = shift(sent1b, first_axis_steps(1))
    g2, g3 = [shift(g0, first_axis_steps(k)) for k in (2, 3)]

    acc = early_sums(r0, r3, g0, g3)
    plane, acc = lax.optimization_barrier(((g0, r1b, g2, g3), acc))
    keep, give = plane_blocks(*plane)
    acc, keep, give = lax.optimization_barrier((acc, keep, give))
    sums = partial_sums(acc, r1a, r1b, r2, g2)
    seed = picked(lax.ppermute(give, "c", [(1, 0)]), keep)
    other = swap(seed, "yl")
    parts = [sums[0]] + [None] * 3
    for k in (1, 3, 2):
        parts[k] = shift(sums[k], second_axis_steps(k))
    both, one = paired(seed, other)
    along_x = lambda value, k: lax.ppermute(value, "x", [(i, (i + k) % 4) for i in range(4)])
    far = along_x(one, 2)
    up, down = along_x(both, 1), along_x(both, 3)
    far_pair = z_pairs(far)

    blocks = summed_blocks(parts)
    blocks = lax.all_to_all(blocks, ("yl", "yh", "c"), 0, 0, tiled=True)
    part = outer_part(first_part_body, "first_part", (h, seed, other))
    part = outer_part(second_part_body, "second_part", (h, far, far_pair), part)
    grad_weight, grad_hidden = last_part((h, up, down, blocks), part)
    return grad_hidden, grad_weight


def solution(mesh):
    fine = Mesh(mesh.devices.reshape(4, 2, 4, 2, 2), ("z", "yl", "x", "yh", "c"))
    narrow, wide = ("yh", "c"), ("z", "yl", "x")
    return jax.shard_map(
        per_device,
        mesh=fine,
        in_specs=(
            P(narrow, None, wide),
            P(narrow, wide),
            P(narrow, wide),
            P(narrow, wide),
        ),
        out_specs=(P(narrow, None, wide), P(narrow, None, wide)),
        check_vma=False,
    )
```

```python
import functools

import jax
import jax.numpy as jnp
from jax import lax
from jax.experimental import pallas as pl
from jax.experimental.pallas import tpu as pltpu
from jax.sharding import Mesh, PartitionSpec as P

BF = jnp.bfloat16
F32 = jnp.float32
VM = pltpu.VMEM


def first_axis_steps(k):
    pairs = []
    for z in range(4):
        for x in range(4):
            pairs.append(((z * 4 + x) * 2, (z * 4 + (x + k) % 4) * 2))
            pairs.append(((z * 4 + x) * 2 + 1, (((z + k) % 4) * 4 + x) * 2 + 1))
    return pairs


def second_axis_steps(k):
    pairs = []
    for z in range(4):
        for x in range(4):
            pairs.append(((z * 4 + x) * 2, (((z + k) % 4) * 4 + x) * 2))
            pairs.append(((z * 4 + x) * 2 + 1, (z * 4 + (x + k) % 4) * 2 + 1))
    return pairs


def shift(value, pairs):
    return lax.ppermute(value, ("z", "x", "c"), pairs)


def swap(value, axis):
    return lax.ppermute(value, axis, [(0, 1), (1, 0)])


LIMIT = pltpu.CompilerParams(vmem_limit_bytes=12 << 20)
EARLY = int(2e9)
IN = pl.BlockSpec(memory_space=VM)
HBM = pl.BlockSpec(memory_space=pltpu.HBM)


def kept(*values):
    return [pltpu.with_memory_space_constraint(v, VM) for v in values]


def roles():
    c, x, z = lax.axis_index("c"), lax.axis_index("x"), lax.axis_index("z")
    return c, jnp.where(c == 0, x, z), jnp.where(c == 0, z, x)


def spread_scales(s_ref, wide_ref):
    row = lax.broadcasted_iota(jnp.int32, (16, 256), 0)
    col = lax.broadcasted_iota(jnp.int32, (16, 256), 1)
    spread = jnp.where(col // 16 == row, 1.0, 0.0).astype(BF)
    wide_ref[...] = lax.dot_general(
        s_ref[...], spread, (((0,), (0,)), ((), ())), preferred_element_type=F32
    )


def scale_into(outs, w_ref, s_ref, narrow_ref, wide_ref, sems):
    c, first, _ = roles()
    scales = pltpu.make_async_copy(s_ref, narrow_ref, sems.at[16])
    scales.start()
    copies = []
    for j, (k, buffers) in enumerate(outs):
        p = (first + k) & 3
        places = [r.at[pl.ds(i, 2)] for r in buffers for i in range(0, r.shape[0], 2)]
        for i, o_ref in enumerate(places):
            z, x = c * p + (1 - c) * i, c * i + (1 - c) * p
            copy = pltpu.make_async_copy(w_ref.at[z, :, x], o_ref, sems.at[j * 4 + i])
            copy.start()
            copies.append((copy, o_ref, z, x))
    scales.wait()
    spread_scales(narrow_ref, wide_ref)
    for copy, o_ref, z, x in copies:
        copy.wait()
        for yl in range(2):
            r = pl.multiple_of((z * 8 + yl * 4 + x) * 16, 16)
            s = wide_ref[pl.ds(r, 16), :]
            w = o_ref[yl].astype(F32).reshape(16, 16, 256)
            o_ref[yl] = (w * s[:, None, :]).reshape(256, 256).astype(BF)


def scale_body(w_ref, s_ref, o0, o1a, o1b, o2, o3, *scratch):
    outs = [(1, (o1a, o1b)), (3, (o3,)), (2, (o2,)), (0, (o0,))]
    scale_into(outs, w_ref, s_ref, *scratch)


def scaled_rows(w5, scales_t):
    return pl.pallas_call(
        scale_body,
        out_shape=[VM((n, 256, 256), BF) for n in (8, 6, 2, 8, 8)],
        in_specs=[HBM, HBM],
        out_specs=[IN] * 5,
        scratch_shapes=[VM((16, 512), BF), VM((512, 256), F32), pltpu.SemaphoreType.DMA((17,))],
        compiler_params=LIMIT,
        name="scale",
    )(w5, scales_t)


def packed_body(g_ref, h_ref, o_ref):
    o_ref[0] = g_ref[...]
    h = h_ref[...].reshape(128, 1024)
    for n in range(4):
        o_ref[1 + n] = h[:, n * 256 : (n + 1) * 256]


def packed(grad_out, hidden):
    return pl.pallas_call(
        packed_body,
        out_shape=VM((5, 128, 256), BF),
        in_specs=[IN] * 2,
        out_specs=IN,
        compiler_params=LIMIT,
        name="packed",
    )(grad_out, hidden)


def tokens_body(rows_ref, p0, p1, p2, p3, g_ref, h_ref, o_ref):
    n = lax.axis_index("yh") * 2 + lax.axis_index("c")
    for r, p in enumerate((p0, p1, p2, p3)):
        t = n ^ r
        g_ref[t >> 1, pl.ds(pl.multiple_of((t & 1) * 128, 128), 128), :] = p[0]
        rows = pl.ds(pl.multiple_of(t * 128, 128), 128)
        for m in range(4):
            h_ref[rows, m * 256 : (m + 1) * 256] = p[1 + m]
    o_ref[0:2] = rows_ref[...]
    o_ref[2:4] = g_ref[...]


def all_tokens(own, rows):
    far = swap(own, "yh")
    pieces = [own, swap(own, "c"), far, swap(far, "c")]
    return pl.pallas_call(
        tokens_body,
        out_shape=[VM((2, 256, 256), BF), VM((512, 1024), BF), VM((4, 256, 256), BF)],
        in_specs=[IN] * 5,
        out_specs=[IN] * 3,
        compiler_params=LIMIT,
        cost_estimate=pl.CostEstimate(flops=1000, bytes_accessed=1000, transcendentals=0),
        name="tokens",
    )(*kept(rows, *pieces))


def block_product(g, w, q):
    return lax.dot_general(
        g[...].reshape(512, 256),
        w[pl.ds(q, 2)].reshape(512, 256),
        (((1,), (1,)), ((), ())),
        preferred_element_type=F32,
    )


def early_body(r0, r3, g0, g3, acc):
    for q in range(4):
        acc[q] = block_product(g0, r0, 2 * q) + block_product(g3, r3, 2 * q)


def early_sums(*operands):
    return pl.pallas_call(
        early_body,
        out_shape=VM((4, 512, 512), F32),
        in_specs=[IN] * 4,
        out_specs=IN,
        compiler_params=LIMIT,
        cost_estimate=pl.CostEstimate(flops=EARLY, bytes_accessed=6 << 20, transcendentals=0),
        name="early",
    )(*kept(*operands))


def plane_body(g0, r1b, g2, g3, keep, give):
    z, yh = lax.axis_index("z"), lax.axis_index("yh")
    g = (g0, r1b.at[2:4], g2, g3)
    for k in range(4):

        @pl.when(((z - 2 * yh) & 3) == k)
        def _():
            give[...] = g[k][...]

        @pl.when(((z - 2 * yh - 1) & 3) == k)
        def _():
            keep[...] = g[k][...]


def plane_blocks(*grads):
    return pl.pallas_call(
        plane_body,
        out_shape=[VM((2, 256, 256), BF)] * 2,
        in_specs=[IN] * 4,
        out_specs=[IN] * 2,
        compiler_params=LIMIT,
        name="plane",
    )(*kept(*grads))


def partial_body(acc, r1a, r1b, r2, g2, *outs):
    outs, r1 = outs[:4], outs[4]
    r1[0:6] = r1a[...]
    r1[6:8] = r1b[0:2]
    g1 = r1b.at[2:4]
    _, _, second = roles()
    for k in (2, 1, 3, 0):
        q = (second + k) & 3
        total = acc[q] + block_product(g1, r1, 2 * q) + block_product(g2, r2, 2 * q)
        outs[k][...] = total.astype(outs[k].dtype)


def partial_sums(*operands):
    return pl.pallas_call(
        partial_body,
        out_shape=[VM((512, 512), F32)]
        + [VM((512, 512), BF)] * 3,
        in_specs=[IN] * 5,
        out_specs=[IN] * 4,
        scratch_shapes=[VM((8, 256, 256), BF)],
        compiler_params=LIMIT,
        name="partial",
    )(*kept(*operands))


def gather_body(a, b, c, d, o_ref):
    total = a[...] + b[...].astype(F32) + c[...].astype(F32) + d[...].astype(F32)
    total = total.astype(BF)
    for yl in range(2):
        for n in range(4):
            t = n * 128
            o_ref[yl * 4 + n] = total[t : t + 128, yl * 256 : (yl + 1) * 256]


def summed_blocks(parts):
    return pl.pallas_call(
        gather_body,
        out_shape=VM((8, 128, 256), BF),
        in_specs=[IN] * 4,
        out_specs=IN,
        compiler_params=LIMIT,
        name="summed",
    )(parts[0], *kept(*parts[1:]))


def picked_body(a_ref, b_ref, o_ref):
    @pl.when(lax.axis_index("c") == 0)
    def _():
        o_ref[...] = a_ref[...]

    @pl.when(lax.axis_index("c") == 1)
    def _():
        o_ref[...] = b_ref[...]


def picked(for_core_0, for_core_1):
    return pl.pallas_call(
        picked_body,
        out_shape=VM((2, 256, 256), BF),
        in_specs=[IN] * 2,
        out_specs=IN,
        compiler_params=LIMIT,
        name="picked",
    )(for_core_0, for_core_1)


def paired_body(a_ref, b_ref, o_ref, one_ref):
    o_ref[0:2] = a_ref[...]
    o_ref[2:4] = b_ref[...]
    odd = lax.axis_index("z") & 1
    one_ref[...] = o_ref[pl.ds(2 * odd, 2)]


def paired(a, b):
    return pl.pallas_call(
        paired_body,
        out_shape=[VM((4, 256, 256), BF), VM((2, 256, 256), BF)],
        in_specs=[IN] * 2,
        out_specs=[IN] * 2,
        compiler_params=LIMIT,
        name="paired",
    )(*kept(a, b))


def z_pairs(value):
    pairs = []
    for z in range(4):
        pairs.append((z * 2, (z ^ 1) * 2))
        pairs.append((z * 2 + 1, (z + 1 if z & 1 else z + 3) % 4 * 2 + 1))
    return lax.ppermute(value, ("z", "c"), pairs)


def outer_into(blocks, h_ref, o_ref, buf, sems):
    x = lax.axis_index("x")
    copies = []
    for i, (yl, k, g) in enumerate(blocks):
        r = pl.multiple_of((yl * 4 + ((x - k) & 3)) * 256, 256)
        p = lax.dot_general(
            g[...].reshape(512, 256),
            h_ref[...],
            (((0,), (0,)), ((), ())),
            preferred_element_type=F32,
        )
        buf[i] = p.astype(BF).reshape(256, 4, 256)
        copy = pltpu.make_async_copy(buf.at[i], o_ref.at[pl.ds(r, 256)], sems.at[i])
        copy.start()
        copies.append(copy)
    for copy in copies:
        copy.wait()


def own_part_body(h_ref, seed, *refs):
    outer_into([(lax.axis_index("yl"), 0, seed)], h_ref, *refs)


def first_part_body(o_in, h_ref, other, far, *refs):
    yl = lax.axis_index("yl")
    outer_into([(1 - yl, 0, other), (yl ^ (lax.axis_index("z") & 1), 2, far)], h_ref, *refs)


def second_part_body(o_in, h_ref, far_pair, *refs):
    here = lax.axis_index("yl") ^ (lax.axis_index("z") & 1)
    outer_into([(1 - here, 2, far_pair)], h_ref, *refs)


def last_part_body(o_in, h_ref, up, down, r_ref, o_ref, d_ref, buf, sems, d_buf, d_sem):
    r = [(r_ref[n].astype(F32) + r_ref[4 + n].astype(F32)).astype(BF) for n in range(4)]
    d_buf[...] = jnp.concatenate(r, axis=1).reshape(128, 4, 256)
    copy = pltpu.make_async_copy(d_buf, d_ref, d_sem.at[0])
    copy.start()
    yl = lax.axis_index("yl")
    blocks = []
    for k, ref in ((1, up), (3, down)):
        blocks += [(yl, k, ref.at[0:2]), (1 - yl, k, ref.at[2:4])]
    outer_into(blocks, h_ref, o_ref, buf, sems)
    copy.wait()


def last_part(operands, so_far):
    return pl.pallas_call(
        last_part_body,
        out_shape=[
            jax.ShapeDtypeStruct((2048, 4, 256), BF),
            jax.ShapeDtypeStruct((128, 4, 256), BF),
        ],
        in_specs=[HBM] + [IN] * len(operands),
        out_specs=[HBM, HBM],
        scratch_shapes=[
            VM((4, 256, 4, 256), BF),
            pltpu.SemaphoreType.DMA((4,)),
            VM((128, 4, 256), BF),
            pltpu.SemaphoreType.DMA((1,)),
        ],
        input_output_aliases={0: 0},
        compiler_params=LIMIT,
        name="last_part",
    )(so_far, *kept(*operands))


def outer_part(body, name, operands, so_far=None):
    aliased = so_far is not None
    return pl.pallas_call(
        body,
        out_shape=jax.ShapeDtypeStruct((2048, 4, 256), BF),
        in_specs=[HBM] * aliased + [IN] * len(operands),
        out_specs=HBM,
        scratch_shapes=[VM((4, 256, 4, 256), BF), pltpu.SemaphoreType.DMA((4,))],
        input_output_aliases={0: 0} if aliased else {},
        compiler_params=LIMIT,
        cost_estimate=pl.CostEstimate(flops=int(1e6), bytes_accessed=1 << 10, transcendentals=0),
        name=name,
    )(*([so_far] if aliased else []), *kept(*operands))


def per_device(hidden, grad_out, weight_base, block_scale):
    w5 = pltpu.with_memory_space_constraint(weight_base.reshape(4, 2, 4, 256, 256), pltpu.HBM)
    scales_t = pltpu.with_memory_space_constraint(block_scale.T, pltpu.HBM)

    r0, sent1a, sent1b, sent2, sent3 = scaled_rows(w5, scales_t)
    r1a = shift(sent1a, first_axis_steps(1))
    r2, r3 = shift(sent2, first_axis_steps(2)), shift(sent3, first_axis_steps(3))
    grad_out, hidden, _ = lax.optimization_barrier((grad_out, hidden, r0))
    g0, h, sent1b = all_tokens(packed(grad_out, hidden), sent1b)
    sent1b, g0, r1a = lax.optimization_barrier((sent1b, g0, r1a))
    r1b = shift(sent1b, first_axis_steps(1))
    g2, g3 = [shift(g0, first_axis_steps(k)) for k in (2, 3)]

    acc = early_sums(r0, r3, g0, g3)
    plane, acc = lax.optimization_barrier(((g0, r1b, g2, g3), acc))
    keep, give = plane_blocks(*plane)
    acc, keep, give = lax.optimization_barrier((acc, keep, give))
    sums = partial_sums(acc, r1a, r1b, r2, g2)
    seed = picked(lax.ppermute(give, "c", [(1, 0)]), keep)
    other = swap(seed, "yl")
    parts = [sums[0]] + [None] * 3
    for k in (1, 3, 2):
        parts[k] = shift(sums[k], second_axis_steps(k))
    part = outer_part(own_part_body, "own_part", (h, seed))
    other, part = lax.optimization_barrier((other, part))
    both, one = paired(seed, other)
    along_x = lambda value, k: lax.ppermute(value, "x", [(i, (i + k) % 4) for i in range(4)])
    far = along_x(one, 2)
    up, down = along_x(both, 1), along_x(both, 3)
    far_pair = z_pairs(far)

    blocks = summed_blocks(parts)
    blocks = lax.all_to_all(blocks, ("yl", "yh", "c"), 0, 0, tiled=True)
    part = outer_part(first_part_body, "first_part", (h, other, far), part)
    part = outer_part(second_part_body, "second_part", (h, far_pair), part)
    grad_weight, grad_hidden = last_part((h, up, down, blocks), part)
    return grad_hidden, grad_weight


def solution(mesh):
    fine = Mesh(mesh.devices.reshape(4, 2, 4, 2, 2), ("z", "yl", "x", "yh", "c"))
    narrow, wide = ("yh", "c"), ("z", "yl", "x")
    return jax.shard_map(
        per_device,
        mesh=fine,
        in_specs=(
            P(narrow, None, wide),
            P(narrow, wide),
            P(narrow, wide),
            P(narrow, wide),
        ),
        out_specs=(P(narrow, None, wide), P(narrow, None, wide)),
        check_vma=False,
    )
```
